32 devices in a mesh: rep: 4 (over x, core), shard: 8 (over z, y).
Axes of the slice: x: 2, y: 2, z: 4, core: 2. Of those that a mesh axis runs over, the one named last changes fastest.
Arguments:
- inputs: bfloat16 [32, 1024, 512], P(('rep', 'shard')), may hold values from -6 to 6
- segments: int32 [32, 1024], P(('rep', 'shard')), may hold values from 0 to 7, never falling along the last dimension, each value on 1 to 512 neighbouring positions
- valid_mask: int32 [32, 1024], P(('rep', 'shard')), may hold values from 0 to 1, as said below
- teacher: bfloat16 [32, 1024, 512], P(('rep', 'shard')), may hold values from -6 to 6
- query_weight: bfloat16 [512, 512], P('shard'), may hold values from -0.5 to 0.5
- key_weight: bfloat16 [512, 512], P('shard'), may hold values from -0.25 to 0.25
- value_weight: bfloat16 [512, 512], P('shard'), may hold values from -0.25 to 0.25
- control_weight: bfloat16 [512, 512], P('shard'), may hold values from -0.75 to 0.75
- output_weight: bfloat16 [512, 512], P('shard'), may hold values from -0.75 to 0.75
- gain_first: bfloat16 [512], P('shard'), may hold values from 0.5 to 1.5
- shift_first: bfloat16 [512], P('shard'), may hold values from -4 to 4
- expand_weight: bfloat16 [512, 2048], P('shard'), may hold values from -0.25 to 0.25
- expand_bias: bfloat16 [2048], P('shard'), may hold values from -4 to 4
- contract_weight: bfloat16 [2048, 512], P('shard'), may hold values from -0.1875 to 0.1875
- contract_bias: bfloat16 [512], P('shard'), may hold values from -4 to 4
- gain_second: bfloat16 [512], P('shard'), may hold values from 0.5 to 1.5
- shift_second: bfloat16 [512], P('shard'), may hold values from -4 to 4
Outputs:
- layer_out: bfloat16 [32, 1024, 512], P(('rep', 'shard'))
- grad_inputs: float32 [32, 1024, 512], P(('rep', 'shard'))
- loss_value: float32 [], replicated
- grad_query_weight: float32 [512, 512], P('shard')
- grad_key_weight: float32 [512, 512], P('shard')
- grad_value_weight: float32 [512, 512], P('shard')
- grad_control_weight: float32 [512, 512], P('shard')
- grad_output_weight: float32 [512, 512], P('shard')
- grad_gain_first: float32 [512], P('shard')
- grad_shift_first: float32 [512], P('shard')
- grad_expand_weight: float32 [512, 2048], P('shard')
- grad_expand_bias: float32 [2048], P('shard')
- grad_contract_weight: float32 [2048, 512], P('shard')
- grad_contract_bias: float32 [512], P('shard')
- grad_gain_second: float32 [512], P('shard')
- grad_shift_second: float32 [512], P('shard')
The draws below stay inside these ranges and needn't reach their ends.
Inputs may be any that keep to these rules, and one draw needn't show every extreme that they name: `valid_mask`: 1 marks a token that counts toward the loss; the first token of every sequence always counts. `segments`: within each sequence ids start at 0 and never fall; each document has 1 to 512 tokens, and one has exactly 512.
All inputs are finite; a program needn't handle non-finite values.
Results may differ from the reference program's by a relative error of at most 0.017.
Values may be sent and summed in bfloat16 or wider, within the bound.
No kernel may reach another device: no remote copies, remote signals or barrier semaphores. Data moves between devices by JAX's collectives and lax.ppermute only.
A program may use at most 128 MiB of HBM per device.

```python
import math
from functools import partial
import jax
import jax.numpy as jnp
import numpy as np
from jax import lax

D = 512
HEADS = 8
SLOTS = 64
FF = 2048
LEN = 1024
SEQS = 32


def draw_valid_mask(key, part):
    places = jnp.arange(SEQS * LEN, dtype=jnp.int32).reshape(SEQS, LEN)
    sequence_index = places // LEN
    threshold = 250 + 500 * sequence_index // SEQS
    rolls = jax.random.randint(key, (SEQS, LEN), 0, 1000, dtype=jnp.int32)
    keeper = (rolls < threshold) | (places % LEN == 0)
    return jnp.where(keeper, 1, 0).astype(jnp.int32)


def level_of(key, shape, shards, smallest, largest):
    level = 1.0
    for axis_at, blocks in shards:
        draws = jax.random.uniform(jax.random.fold_in(jax.random.fold_in(key, 6), axis_at), (blocks,), jnp.float32, smallest / len(shards), largest / len(shards))
        level = level * jnp.repeat(jnp.exp(draws), shape[axis_at] // blocks).reshape((-1,) + (1,) * (len(shape) - 1 - axis_at))
    return level


def length_profile(count, total, bound, lean):
    loads = [(1 << 20) // math.isqrt(rank ** lean) + 1 for rank in range(2, count + 1)]
    surplus, given = total - bound - (count - 1), [1] * (count - 1)
    while surplus > 0:
        movable = [i for i in range(count - 1) if given[i] < bound]
        mass, remaining = sum([loads[i] for i in movable]), surplus
        for i in movable:
            extra = min(bound - given[i], max(1, remaining * loads[i] // mass), surplus)
            given[i] = given[i] + extra
            surplus = surplus - extra
    return np.array([bound] + given)


def uneven(key, count, total, limit, lean):
    if count == 2:
        one = jax.random.randint(key, (), max(1, total - limit), min(limit, total - 1) + 1)
        return jnp.stack([one, total - one])
    tallies = jnp.asarray(length_profile(count, total, limit, lean), jnp.int32)
    pairs = (count - 1) // 2
    donor, sink = tallies[1:1 + 2 * pairs:2], tallies[2:2 + 2 * pairs:2]
    room = jnp.minimum(donor - 1, limit - sink)
    passed = jax.random.randint(jax.random.fold_in(key, 1), (pairs,), 0, 1 << 20) % (room + 1)
    tallies = tallies.at[1:1 + 2 * pairs:2].set(donor - passed).at[2:2 + 2 * pairs:2].set(sink + passed)
    return tallies[jax.random.permutation(jax.random.fold_in(key, 2), count)]


def normal_values(own_key, extent, spread, limit, shards=(), kind=jnp.bfloat16):
    level = level_of(own_key, extent, shards, -0.22, 0.18) if shards else 1.0
    drawn = jax.random.normal(own_key, extent, jnp.float32) * spread * level
    return jnp.minimum(jnp.maximum(drawn, -limit), limit).astype(kind)


def setup_inputs(seed: int = 0) -> dict:
    seeds = jax.random.split(jax.random.key(seed), 18)
    return {
        "inputs": normal_values(seeds[0], (SEQS, LEN, D), 1.0, 6.0, ((0, 32),)),
        "segments": jax.vmap(lambda own: jnp.searchsorted(jnp.cumsum(uneven(own, max(LEN // 128, 4), LEN, LEN // 2, 3)), jnp.arange(LEN), side="right"))(jax.random.split(seeds[1], SEQS)).reshape((SEQS, LEN)).astype(jnp.int32),
        "valid_mask": draw_valid_mask(jax.random.fold_in(seeds[17], 71), 0),
        "teacher": normal_values(seeds[3], (SEQS, LEN, D), 1.0, 6.0, ((0, 32),)),
        "query_weight": normal_values(seeds[4], (D, D), (D // 4) ** -0.5, 0.5, ((0, 8),)),
        "key_weight": normal_values(seeds[5], (D, D), D ** -0.5, 0.25, ((0, 8),)),
        "value_weight": normal_values(seeds[6], (D, D), D ** -0.5, 0.25, ((0, 8),)),
        "control_weight": normal_values(seeds[7], (D, HEADS * SLOTS), (D // 9) ** -0.5, 0.75, ((0, 8),)),
        "output_weight": normal_values(seeds[8], (D, D), (D // 8) ** -0.5, 0.75, ((0, 8),)),
        "gain_first": jnp.clip(1.0 + 0.1 * jax.random.normal(seeds[9], (D,), jnp.float32), 0.5, 1.5).astype(jnp.bfloat16),
        "shift_first": normal_values(seeds[10], (D,), 0.3, 4.0, ((0, 8),)),
        "expand_weight": normal_values(seeds[11], (D, FF), D ** -0.5, 0.25, ((0, 8),)),
        "expand_bias": normal_values(seeds[12], (FF,), 0.3, 4.0, ((0, 8),)),
        "contract_weight": normal_values(seeds[13], (FF, D), (FF // 2) ** -0.5, 0.1875, ((0, 8),)),
        "contract_bias": normal_values(seeds[14], (D,), 0.3, 4.0, ((0, 8),)),
        "gain_second": jnp.clip(1.0 + 0.1 * jax.random.normal(seeds[15], (D,), jnp.float32), 0.5, 1.5).astype(jnp.bfloat16),
        "shift_second": normal_values(seeds[16], (D,), 0.3, 4.0, ((0, 8),)),
    }


EPSILON = 1e-05
HIGHEST = lax.Precision.HIGHEST

@jax.custom_vjp
def low(v):
    return lax.optimization_barrier(v.astype(jnp.bfloat16)).astype(jnp.float32)

@jax.custom_vjp
def low_back(v):
    return v

def low_keep(v):
    return (low(v), None)

def low_pass(kept, grad):
    return (grad,)

def back_keep(v):
    return (v, None)

def back_low(kept, grad):
    return (low(grad),)
low.defvjp(low_keep, low_pass)
low_back.defvjp(back_keep, back_low)

def layer_norm(activations, gain, shift):
    row_mean = lax.optimization_barrier(jnp.mean(activations, axis=-1, keepdims=True))
    centred = activations - row_mean
    variance = lax.optimization_barrier(jnp.mean(centred * centred, axis=-1, keepdims=True))
    return centred * lax.rsqrt(variance + EPSILON) * gain + shift

def doc_mask(segment_row):
    places = jnp.arange(segment_row.shape[0], dtype=jnp.int32)
    earlier = places[None, :] <= places[:, None]
    same_document = segment_row[:, None] == segment_row[None, :]
    return jnp.where(earlier & same_document, 1.0, 0.0).astype(jnp.float32)

def slot_core(causal, queries, key_rows, value_rows, control):
    weights = jnp.exp(control)
    totals = jnp.dot(causal, weights, precision=HIGHEST)
    scores = jnp.dot(queries, key_rows.T, precision=HIGHEST) * queries.shape[-1] ** (-0.5)
    slot_scores = jnp.dot(scores * causal, weights, precision=HIGHEST) / totals
    slot_shares = jax.nn.softmax(slot_scores, axis=-1)
    mixing = jnp.dot(slot_shares / totals, weights.T, precision=HIGHEST) * causal
    return jnp.dot(mixing, value_rows, precision=HIGHEST)

def head_apply(causal, head_bundle):
    return slot_core(causal, *head_bundle)

def split_heads(matrix, length):
    return matrix.reshape(length, HEADS, -1).transpose(1, 0, 2)

def forward(weight_set, layer_in, segment_row):
    query_weight, key_weight, value_weight, control_weight, output_weight, gain_first, shift_first, expand_weight, expand_bias, contract_weight, contract_bias, gain_second, shift_second = weight_set
    length = layer_in.shape[0]
    normed_one = low(layer_norm(layer_in, gain_first, shift_first))
    queries = low_back(low(jnp.dot(normed_one, query_weight, precision=HIGHEST)))
    key_rows = low_back(low(jnp.dot(normed_one, key_weight, precision=HIGHEST)))
    value_rows = low_back(low(jnp.dot(normed_one, value_weight, precision=HIGHEST)))
    control = low_back(jnp.dot(normed_one, control_weight, precision=HIGHEST))
    causal = doc_mask(segment_row)
    mixed = lax.map(jax.checkpoint(partial(head_apply, causal)), (split_heads(queries, length), split_heads(key_rows, length), split_heads(value_rows, length), split_heads(control, length)))
    mixed = low(mixed.transpose(1, 0, 2).reshape(length, -1))
    mixer_out = low_back(jnp.dot(mixed, output_weight, precision=HIGHEST))
    hidden_one = layer_in + mixer_out
    normed_two = low(layer_norm(hidden_one, gain_second, shift_second))
    before_relu = low_back(jnp.dot(normed_two, expand_weight, precision=HIGHEST) + expand_bias)
    after_relu = low(jax.nn.relu(before_relu))
    branch_out = low_back(jnp.dot(after_relu, contract_weight, precision=HIGHEST) + contract_bias)
    return hidden_one + branch_out

def reference(inputs, segments, valid_mask, teacher, query_weight, key_weight, value_weight, control_weight, output_weight, gain_first, shift_first, expand_weight, expand_bias, contract_weight, contract_bias, gain_second, shift_second):
    weight_set = tuple((weight_in.astype(jnp.float32) for weight_in in (query_weight, key_weight, value_weight, control_weight, output_weight, gain_first, shift_first, expand_weight, expand_bias, contract_weight, contract_bias, gain_second, shift_second)))
    valid_all = valid_mask.astype(jnp.float32)
    count_all = jnp.sum(valid_all)
    loss_scale = SEQS * LEN / count_all
    zero_grads = jax.tree.map(jnp.zeros_like, weight_set)

    def per_sequence(running, bundle):
        grad_total, error_total = running
        sequence_in, segment_row, valid_row, teacher_row = bundle

        def objective(weights_now, layer_in):
            result = forward(weights_now, layer_in, segment_row)
            error = result - teacher_row.astype(jnp.float32)
            error_sum = jnp.sum(valid_row[:, None] * error * error)
            return (loss_scale * 0.5 * error_sum, (result, error_sum))
        objective_value, pullback, extras = jax.vjp(objective, weight_set, sequence_in.astype(jnp.float32), has_aux=True)
        result, error_sum = extras
        grad_set, grad_layer_in = pullback(jnp.ones((), jnp.float32))
        grad_total = jax.tree.map(jnp.add, grad_total, grad_set)
        return ((grad_total, error_total + error_sum), (result.astype(jnp.bfloat16), grad_layer_in))
    (grad_total, error_total), (layer_out, grad_inputs) = lax.scan(per_sequence, (zero_grads, jnp.zeros((), jnp.float32)), (inputs, segments, valid_all, teacher))
    loss_value = error_total / (2.0 * count_all)
    return (layer_out, grad_inputs, loss_value, grad_total[0], grad_total[1], grad_total[2], grad_total[3], grad_total[4], grad_total[5], grad_total[6], grad_total[7], grad_total[8], grad_total[9], grad_total[10], grad_total[11], grad_total[12])
```

```python
import functools

import jax
import jax.numpy as jnp
from jax import lax
from jax.experimental import pallas as pl
from jax.experimental.pallas import tpu as pltpu
from jax.sharding import PartitionSpec as P

HEADS = 8
EPSILON = 1e-05
CHUNK = 256
QUAD = 256
F32 = jnp.float32
BF16 = jnp.bfloat16
VMEM_LIMIT = 60 << 20


def nn(left, right):
    return jnp.dot(left, right, preferred_element_type=F32)


def nt(left, right):
    return lax.dot_general(left, right, (((1,), (1,)), ((), ())), preferred_element_type=F32)


def tn(left, right):
    return lax.dot_general(left, right, (((0,), (0,)), ((), ())), preferred_element_type=F32)


def head_lanes():
    lane = lax.broadcasted_iota(jnp.int32, (1, QUAD), 1) // 64
    return [jnp.where(lane == h, 1.0, 0.0).astype(BF16) for h in range(4)]


def block_diagonal():
    rows = lax.broadcasted_iota(jnp.int32, (QUAD, QUAD), 0) // 64
    columns = lax.broadcasted_iota(jnp.int32, (QUAD, QUAD), 1) // 64
    return jnp.where(rows == columns, 1.0, 0.0)


def as_column(row):
    return jnp.broadcast_to(row, (CHUNK, CHUNK)).T


def causal_mask(column, row):
    at = lax.broadcasted_iota(jnp.int32, (CHUNK, CHUNK), 0)
    source = lax.broadcasted_iota(jnp.int32, (CHUNK, CHUNK), 1)
    return jnp.where((column == row) & (source <= at), 1.0, 0.0)


def causal_mask_transposed(column, row):
    source = lax.broadcasted_iota(jnp.int32, (CHUNK, CHUNK), 0)
    at = lax.broadcasted_iota(jnp.int32, (CHUNK, CHUNK), 1)
    return jnp.where((column == row) & (source <= at), 1.0, 0.0)


def per_head(values, reduce, fill):
    lane = lax.broadcasted_iota(jnp.int32, (1, 128), 1)
    first = lane < 64
    tiles = []
    for tile in range(values.shape[1] // 128):
        part = values[:, tile * 128 : (tile + 1) * 128]
        one = reduce(jnp.where(first, part, fill), axis=-1, keepdims=True)
        two = reduce(jnp.where(first, fill, part), axis=-1, keepdims=True)
        tiles.append(jnp.where(first, one, two))
    return jnp.concatenate(tiles, axis=1)


def standardise(values):
    mean = jnp.mean(values, axis=-1, keepdims=True)
    centred = values - mean
    variance = jnp.mean(centred * centred, axis=-1, keepdims=True)
    scale = lax.rsqrt(variance + EPSILON)
    return centred * scale, scale


def norm_backward(gradient, gain, normal, scale):
    upstream = gradient * gain
    one = jnp.mean(upstream, axis=-1, keepdims=True)
    two = jnp.mean(upstream * normal, axis=-1, keepdims=True)
    return (upstream - one - normal * two) * scale


def spread(rows, shards):
    width = 512 // shards
    lane = lax.broadcasted_iota(jnp.int32, (8, 128), 1)
    tiles = [None] * 4
    for s in range(shards):
        tile, offset = divmod(s * width, 128)
        moved = pltpu.roll(rows[s], offset, 1) if offset else rows[s]
        inside = (lane >= offset) & (lane < offset + width)
        tiles[tile] = jnp.where(inside, moved, 0.0 if tiles[tile] is None else tiles[tile])
    return jnp.concatenate(tiles, axis=1)


def piece_of(vectors, s, width):
    tile, offset = divmod(s * width, 128)
    part = vectors[:, tile * 128 : (tile + 1) * 128]
    return pltpu.roll(part, 128 - offset, 1) if offset else part


def attention_forward(
    shards,
    seg_s,
    pos_s,
    x_ref,
    seg_ref,
    mine_ref,
    theirs_ref,
    q_ref,
    k_ref,
    v_ref,
    e_ref,
    p_ref,
    s_ref,
    rz_ref,
    mix_ref,
    one_ref,
    two_ref,
    w_ref,
    vec_ref,
    eb_ref,
    count_ref,
    held,
    first_state,
    second_state,
    total_state,
    sems,
):
    step = pl.program_id(0)
    nb = 512 // shards // 16
    mine, core = pos_s[0], pos_s[1]

    @pl.when(step == 0)
    def _():
        for half, source in enumerate((mine_ref, theirs_ref)):
            column = pl.multiple_of(((core + half) % 2) * 256, 256)
            for j in range(shards):
                owner = mine ^ j
                for m in range(4):
                    pltpu.make_async_copy(
                        source.at[j, pl.ds(m * nb, nb)],
                        w_ref.at[m, pl.ds(owner * nb, nb), :, pl.ds(column, 256)],
                        sems.at[0],
                    ).start()
                pltpu.make_async_copy(
                    source.at[j, 4 * nb], held.at[half, owner], sems.at[1]
                ).start()
        first_state[...] = jnp.zeros_like(first_state)
        second_state[...] = jnp.zeros_like(second_state)
        total_state[...] = jnp.zeros_like(total_state)
        pltpu.make_async_copy(held, held, sems.at[1]).wait()
        own = [held[0, s].astype(F32) for s in range(shards)]
        other = [held[1, s].astype(F32) for s in range(shards)]
        vec_ref[...] = spread([part[:8, :128] for part in own], shards)
        width = 2048 // shards
        lane = lax.broadcasted_iota(jnp.int32, (8, 128), 1)
        if width >= 128:
            for s in range(shards):
                eb_ref[:, s * width : (s + 1) * width] = own[s][8:16, :width]
        else:
            for tile in range(16):
                built = jnp.zeros((8, 128), F32)
                for k in range(128 // width):
                    part = own[tile * (128 // width) + k][8:16, :128]
                    moved = pltpu.roll(part, k * width, 1) if k else part
                    built = jnp.where((lane >= k * width) & (lane < (k + 1) * width), moved, built)
                eb_ref[:, tile * 128 : (tile + 1) * 128] = built
        count_ref[...] = sum(part[:8, :128] for part in own + other)
        pltpu.make_async_copy(w_ref, w_ref, sems.at[0]).wait()

    start = step * CHUNK
    segment_last = seg_s[start + CHUNK - 1]
    segment_before = jnp.where(step == 0, -1, seg_s[jnp.maximum(start - 1, 0)])
    keep = jnp.where(segment_last == segment_before, 1.0, 0.0)
    row = seg_ref[...]
    column = as_column(row)
    causal = causal_mask(column, row).astype(BF16)
    enters = jnp.where(column == segment_before.astype(F32), 1.0, 0.0)
    leaves = jnp.where(column == segment_last.astype(F32), 1.0, 0.0).astype(BF16)
    lanes = head_lanes()
    diagonal = block_diagonal()

    normal, _ = standardise(x_ref[...].astype(F32))
    normed = (normal * vec_ref[0:1, :] + vec_ref[1:2, :]).astype(BF16)
    for g in range(2):
        at = slice(g * QUAD, (g + 1) * QUAD)
        weight = lambda m: w_ref[m, :, :, at].reshape(512, QUAD)
        queries = nn(normed, weight(0)).astype(BF16)
        keys = nn(normed, weight(1)).astype(BF16)
        values = nn(normed, weight(2)).astype(BF16)
        slots = jnp.exp(nn(normed, weight(3))).astype(BF16)
        q_ref[:, at] = queries
        k_ref[:, at] = keys
        v_ref[:, at] = values
        e_ref[:, at] = slots
        totals = nn(causal, slots) + enters * total_state[0:1, at]
        total_state[0:1, at] = totals[CHUNK - 1 : CHUNK, :]
        inverse = 1.0 / totals
        rz_ref[:, at] = inverse
        one = first_state[g].astype(BF16)
        two = second_state[g].astype(BF16)
        one_ref[0, g] = one
        two_ref[0, g] = two
        scores = jnp.concatenate(
            [nt(queries * lanes[h], keys).astype(BF16) * causal for h in range(4)], axis=1
        )
        gathered = nn(scores, jnp.concatenate([slots * lanes[h] for h in range(4)], axis=0))
        gathered += enters * nn(queries, one)
        slot_scores = gathered * (inverse * 0.125)
        raised = jnp.exp(slot_scores - per_head(slot_scores, jnp.max, -jnp.inf))
        shares = raised / per_head(raised, jnp.sum, 0.0)
        s_ref[:, at] = slot_scores.astype(BF16)
        p_ref[:, at] = shares.astype(BF16)
        scaled = (shares * inverse).astype(BF16)
        mixing = jnp.concatenate(
            [nt(scaled * lanes[h], slots).astype(BF16) * causal for h in range(4)], axis=1
        )
        mixed = nn(mixing, jnp.concatenate([values * lanes[h] for h in range(4)], axis=0))
        mixed += enters * nn(scaled, two)
        mix_ref[:, at] = mixed.astype(BF16)
        first_state[g] = keep * first_state[g] + diagonal * tn(keys * leaves, slots)
        second_state[g] = keep * second_state[g] + diagonal * tn(slots * leaves, values)


def feed_forward(
    shards,
    tokens,
    pos_s,
    x_ref,
    mix_ref,
    teacher_ref,
    valid_ref,
    vec_ref,
    eb_ref,
    count_ref,
    mine_ref,
    theirs_ref,
    out_ref,
    hidden_ref,
    grad_mix_ref,
    keep_ref,
    send_ref,
    loss_ref,
    wo,
    we,
    wc,
    act,
    d_wo,
    d_we,
    d_wc,
    d_vec,
    d_eb,
    sems,
):
    step = pl.program_id(0)
    r = 512 // shards
    nb = r // 16
    mine, core = pos_s[0], pos_s[1]

    @pl.when(step == 0)
    def _():
        for half, source in enumerate((mine_ref, theirs_ref)):
            column = pl.multiple_of(((core + half) % 2) * 256, 256)
            for j in range(shards):
                owner = mine ^ j
                pltpu.make_async_copy(
                    source.at[j, 0],
                    wo.at[pl.ds(owner * nb, nb), :, pl.ds(column, 256)],
                    sems.at[0],
                ).start()
                pltpu.make_async_copy(
                    source.at[j, 1:5],
                    we.at[:, pl.ds(owner * nb, nb), :, pl.ds(column, 256)],
                    sems.at[1],
                ).start()
                pltpu.make_async_copy(
                    source.at[j, 5:9],
                    wc.at[pl.ds(owner * 4, 4), :, :, pl.ds(column, 256)],
                    sems.at[2],
                ).start()
        for ref in (d_wo, d_we, d_wc, d_vec, d_eb, loss_ref):
            ref[...] = jnp.zeros_like(ref)
        pltpu.make_async_copy(wo, wo, sems.at[0]).wait()
        pltpu.make_async_copy(we, we, sems.at[1]).wait()
        pltpu.make_async_copy(wc, wc, sems.at[2]).wait()

    gain, shift, bias = vec_ref[2:3, :], vec_ref[3:4, :], vec_ref[4:5, :]
    weight_out = wo[...].reshape(512, 512)
    expand = lambda b: we[b].reshape(512, 512)
    contract = wc.reshape(2048, 512)
    mixed = mix_ref[...]
    hidden = x_ref[...].astype(F32) + nn(mixed, weight_out)
    normal, scale = standardise(hidden)
    normed = (normal * gain + shift).astype(BF16)
    for b in range(4):
        at = slice(b * 512, (b + 1) * 512)
        before = nn(normed, expand(b)) + eb_ref[0:1, at]
        act[:, at] = jnp.maximum(before, 0.0).astype(BF16)
    result = hidden + (nn(act[...], contract[...]) + bias)
    out_ref[...] = result.astype(BF16)
    valid = as_column(valid_ref[...])
    valid = jnp.concatenate([valid, valid], axis=1)
    error = result - teacher_ref[...].astype(F32)
    masked = valid * error
    loss_ref[...] += jnp.sum(masked * error)
    count = 256.0 * count_ref[6:7, 0:1] + count_ref[6:7, 1:2]
    grad_result = masked * (tokens / count)
    low = grad_result.astype(BF16)
    d_normed = None
    for b in range(4):
        at = slice(b * 512, (b + 1) * 512)
        active = act[:, at]
        d_wc[at, :] += tn(active, low)
        grad = jnp.where(active > 0, nt(low, contract[at, :]), 0.0)
        grad = grad.astype(BF16)
        d_we[b] += tn(normed, grad)
        d_eb[0:1, at] += jnp.sum(grad.astype(F32), axis=0, keepdims=True)
        part = nt(grad, expand(b))
        d_normed = part if d_normed is None else d_normed + part
    d_vec[0:1, :] += jnp.sum(d_normed * normal, axis=0, keepdims=True)
    d_vec[1:2, :] += jnp.sum(d_normed, axis=0, keepdims=True)
    d_vec[2:3, :] += jnp.sum(low.astype(F32), axis=0, keepdims=True)
    grad_hidden = grad_result + norm_backward(d_normed, gain, normal, scale)
    hidden_ref[...] = grad_hidden
    grad_low = grad_hidden.astype(BF16)
    d_wo[...] += tn(mixed, grad_low)
    grad_mix_ref[...] = nt(grad_low, weight_out).astype(BF16)

    @pl.when(step == pl.num_programs(0) - 1)
    def _():
        def write(ref, at):
            ref[:, 0:r, :] = d_wo[:, at].reshape(shards, r, 256).astype(BF16)
            for b in range(4):
                ref[:, (1 + b) * r : (2 + b) * r, :] = (
                    d_we[b, :, at].reshape(shards, r, 256).astype(BF16)
                )
            ref[:, 5 * r : 9 * r, :] = d_wc[:, at].reshape(shards, 4 * r, 256).astype(BF16)
            width = 2048 // shards
            for s in range(shards):
                top = piece_of(d_vec[...], s, r)
                top = jnp.concatenate([top, jnp.zeros_like(top)], axis=1)
                if width >= 128:
                    low_rows = d_eb[:, s * width : (s + 1) * width]
                else:
                    low_rows = piece_of(d_eb[...], s, width)
                if low_rows.shape[1] < 256:
                    pad = jnp.zeros((8, 256 - low_rows.shape[1]), F32)
                    low_rows = jnp.concatenate([low_rows, pad], axis=1)
                both = jnp.concatenate([top, low_rows], axis=0)
                ref[s, 9 * r : 9 * r + 16, :] = both.astype(BF16)

        left, right = slice(0, 256), slice(256, 512)

        @pl.when(core == 0)
        def _():
            write(keep_ref, left)
            write(send_ref, right)

        @pl.when(core == 1)
        def _():
            write(keep_ref, right)
            write(send_ref, left)


def attention_backward(last, shards, seg_s, pos_s, *refs):
    x_ref, seg_ref, q_ref, k_ref, v_ref, e_ref, p_ref, s_ref, rz_ref, g_ref = refs[:10]
    one_ref, two_ref, w_ref, vec_ref = refs[10:14]
    refs = refs[14:]
    if last:
        part_ref, hidden_ref = refs[:2]
        refs = refs[2:]
    out_ref, keep_ref, send_ref = refs[:3]
    first_state, second_state, total_state, d_w, d_vec = refs[3:]
    step = pl.program_id(0)
    chunks = pl.num_programs(0)
    chunk = chunks - 1 - step
    r = 512 // shards
    core = pos_s[1]

    @pl.when(step == 0)
    def _():
        for ref in (first_state, second_state, total_state, d_w, d_vec):
            ref[...] = jnp.zeros_like(ref)

    start = chunk * CHUNK
    length = chunks * CHUNK
    segment_first = seg_s[start]
    segment_before = jnp.where(chunk == 0, -1, seg_s[jnp.maximum(start - 1, 0)])
    segment_after = jnp.where(step == 0, -1, seg_s[jnp.minimum(start + CHUNK, length - 1)])
    keep = jnp.where(segment_first == segment_after, 1.0, 0.0)
    row = seg_ref[...]
    column = as_column(row)
    causal = causal_mask(column, row).astype(BF16)
    turned = causal_mask_transposed(column, row).astype(BF16)
    enters = jnp.where(column == segment_before.astype(F32), 1.0, 0.0)
    goes_on = jnp.where(column == segment_after.astype(F32), 1.0, 0.0)
    opens = jnp.where(column == segment_first.astype(F32), 1.0, 0.0).astype(BF16)
    lanes = head_lanes()
    diagonal = block_diagonal()

    def heads(values):
        return [values * lanes[h] for h in range(4)]

    def beside(parts):
        return jnp.concatenate(parts, axis=1)

    def stacked(parts):
        return jnp.concatenate(parts, axis=0)

    queries, keys, values, slots = q_ref[...], k_ref[...], v_ref[...], e_ref[...]
    shares, slot_scores = p_ref[...].astype(F32), s_ref[...].astype(F32)
    inverse, grad = rz_ref[...], g_ref[...]
    scaled = shares * inverse
    scaled_low = scaled.astype(BF16)
    one, two = one_ref[0, 0], two_ref[0, 0]
    one_back, two_back = first_state[...].astype(BF16), second_state[...].astype(BF16)
    grad_heads, slot_heads, value_heads = heads(grad), heads(slots), heads(values)
    slot_stack = stacked(slot_heads)

    d_mixing = beside([nt(part, values).astype(BF16) * causal for part in grad_heads])
    d_scaled = nn(d_mixing, slot_stack) + enters * nt(grad, two)
    d_shares = d_scaled * inverse
    product = shares * d_shares
    d_scores = product - shares * per_head(product, jnp.sum, 0.0)
    d_gathered = d_scores * inverse
    d_totals = -(d_scaled * scaled + d_scores * slot_scores) * inverse
    d_low = (d_gathered * 0.125).astype(BF16)
    d_low_heads = heads(d_low)

    d_raw = beside([nt(part, slots).astype(BF16) * causal for part in d_low_heads])
    d_queries = nn(d_raw, stacked(heads(keys))) + enters * nt(d_low, one)
    d_raw_t = beside([nt(part, d_low).astype(BF16) * turned for part in slot_heads])
    d_keys = nn(d_raw_t, stacked(heads(queries))) + goes_on * nt(slots, one_back)
    mixing_t = beside([nt(part, scaled_low).astype(BF16) * turned for part in slot_heads])
    d_values = nn(mixing_t, stacked(grad_heads)) + goes_on * nn(slots, two_back)
    scores_t = beside([nt(part, queries).astype(BF16) * turned for part in heads(keys)])
    d_slots = nn(scores_t, stacked(d_low_heads))
    d_mixing_t = beside([nt(part, grad).astype(BF16) * turned for part in value_heads])
    d_slots += nn(d_mixing_t, stacked(heads(scaled_low)))
    d_totals_low = d_totals.astype(BF16)
    rest = (d_totals - d_totals_low.astype(F32)).astype(BF16)
    sums = nn(turned, d_totals_low) + nn(turned, rest) + goes_on * total_state[0:1, :]
    d_slots += goes_on * (nn(keys, one_back) + nt(values, two_back)) + sums
    d_control = d_slots * slots.astype(F32)

    total_state[0:1, :] = sums[0:1, :]
    first_state[...] = keep * first_state[...] + diagonal * tn(queries * opens, d_low)
    second_state[...] = keep * second_state[...] + diagonal * tn(scaled_low * opens, grad)

    normal, scale = standardise(x_ref[...].astype(F32))
    gain = vec_ref[0:1, :]
    normed = (normal * gain + vec_ref[1:2, :]).astype(BF16)
    grads = [part.astype(BF16) for part in (d_queries, d_keys, d_values, d_control)]
    d_w[...] += tn(normed, beside(grads))
    d_normed = sum(nt(grads[m], w_ref[m].reshape(512, QUAD)) for m in range(4))
    if last:
        d_normed += part_ref[...]
        d_vec[0:1, :] += jnp.sum(d_normed * normal, axis=0, keepdims=True)
        d_vec[1:2, :] += jnp.sum(d_normed, axis=0, keepdims=True)
        out_ref[...] = hidden_ref[...] + norm_backward(d_normed, gain, normal, scale)
    else:
        out_ref[...] = d_normed

    @pl.when(step == chunks - 1)
    def _():
        def write(ref, half):
            for m in range(4):
                at = slice(m * QUAD + half * 128, m * QUAD + half * 128 + 128)
                ref[:, m * r : (m + 1) * r, :] = d_w[:, at].reshape(shards, r, 128).astype(BF16)
            if last:
                for s in range(shards):
                    top = piece_of(d_vec[...], s, r)
                    both = jnp.concatenate([top, jnp.zeros_like(top)], axis=0)
                    ref[s, 4 * r : 4 * r + 16, :] = both.astype(BF16)

        @pl.when(core == 0)
        def _():
            write(keep_ref, 0)
            write(send_ref, 1)

        @pl.when(core == 1)
        def _():
            write(keep_ref, 1)
            write(send_ref, 0)


def whole(shape):
    return pl.BlockSpec(shape, lambda *_: (0,) * len(shape))


def anywhere():
    return pl.BlockSpec(memory_space=pl.ANY)


def shaped(shape, dtype):
    return jax.ShapeDtypeStruct(shape, dtype)


def params():
    return pltpu.CompilerParams(
        dimension_semantics=("arbitrary",), vmem_limit_bytes=VMEM_LIMIT
    )


def call_forward(shards, seg_row, segments, position, x, mine, theirs):
    length = x.shape[0]
    chunks = length // CHUNK
    tile = lambda width: pl.BlockSpec((CHUNK, width), lambda c, *_: (c, 0))
    state = pl.BlockSpec((1, 2, QUAD, QUAD), lambda c, *_: (c, 0, 0, 0))
    low = shaped((length, 512), BF16)
    states = shaped((chunks, 2, QUAD, QUAD), BF16)
    grid_spec = pltpu.PrefetchScalarGridSpec(
        num_scalar_prefetch=2,
        grid=(chunks,),
        in_specs=[
            tile(512),
            pl.BlockSpec((1, CHUNK), lambda c, *_: (0, c)),
            anywhere(),
            anywhere(),
        ],
        out_specs=[tile(512)] * 8
        + [state] * 2
        + [whole((4, 32, 16, 512)), whole((8, 512)), whole((8, 2048)), whole((8, 128))],
        scratch_shapes=[
            pltpu.VMEM((2, shards, 16, 256), BF16),
            pltpu.VMEM((2, QUAD, QUAD), F32),
            pltpu.VMEM((2, QUAD, QUAD), F32),
            pltpu.VMEM((8, 512), F32),
            pltpu.SemaphoreType.DMA((2,)),
        ],
    )
    return pl.pallas_call(
        functools.partial(attention_forward, shards),
        grid_spec=grid_spec,
        out_shape=[low] * 6
        + [shaped((length, 512), F32), low, states, states]
        + [
            shaped((4, 32, 16, 512), BF16),
            shaped((8, 512), F32),
            shaped((8, 2048), F32),
            shaped((8, 128), F32),
        ],
        compiler_params=params(),
        cost_estimate=pl.CostEstimate(
            flops=12_000_000_000, bytes_accessed=18_000_000, transcendentals=1_000_000
        ),
        name="attention_forward",
    )(segments, position, x, seg_row, mine, theirs)


def call_feed_forward(
    shards, tokens, position, x, mixed, teacher, valid_row, vectors, bias, count, mine, theirs
):
    length = x.shape[0]
    chunks = length // CHUNK
    r = 512 // shards
    tile = lambda width: pl.BlockSpec((CHUNK, width), lambda c, *_: (c, 0))
    payload = (shards, 9 * r + 16, 256)
    grid_spec = pltpu.PrefetchScalarGridSpec(
        num_scalar_prefetch=1,
        grid=(chunks,),
        in_specs=[
            tile(512),
            tile(512),
            tile(512),
            pl.BlockSpec((1, CHUNK), lambda c, *_: (0, c)),
            whole((8, 512)),
            whole((8, 2048)),
            whole((8, 128)),
            anywhere(),
            anywhere(),
        ],
        out_specs=[tile(512)] * 3 + [whole(payload), whole(payload), whole((8, 128))],
        scratch_shapes=[
            pltpu.VMEM((32, 16, 512), BF16),
            pltpu.VMEM((4, 32, 16, 512), BF16),
            pltpu.VMEM((shards * 4, r // 16, 16, 512), BF16),
            pltpu.VMEM((CHUNK, 2048), BF16),
            pltpu.VMEM((512, 512), F32),
            pltpu.VMEM((4, 512, 512), F32),
            pltpu.VMEM((2048, 512), F32),
            pltpu.VMEM((8, 512), F32),
            pltpu.VMEM((8, 2048), F32),
            pltpu.SemaphoreType.DMA((3,)),
        ],
    )
    return pl.pallas_call(
        functools.partial(feed_forward, shards, tokens),
        grid_spec=grid_spec,
        out_shape=[
            shaped((length, 512), BF16),
            shaped((length, 512), F32),
            shaped((length, 512), BF16),
            shaped(payload, BF16),
            shaped(payload, BF16),
            shaped((8, 128), F32),
        ],
        compiler_params=params(),
        cost_estimate=pl.CostEstimate(
            flops=15_000_000_000, bytes_accessed=18_000_000, transcendentals=0
        ),
        name="feed_forward",
    )(position, x, mixed, teacher, valid_row, vectors, bias, count, mine, theirs)


def call_backward(
    quad, shards, seg_row, segments, position, x, saved, grad_mix, weights, vectors, extra
):
    length = x.shape[0]
    chunks = length // CHUNK
    r = 512 // shards
    last = quad == 1
    back = lambda c: chunks - 1 - c
    wide = pl.BlockSpec((CHUNK, 512), lambda c, *_: (back(c), 0))
    tile = pl.BlockSpec((CHUNK, QUAD), lambda c, *_: (back(c), quad))
    state = pl.BlockSpec((1, 1, QUAD, QUAD), lambda c, *_: (back(c), quad, 0, 0))
    rows = 4 * r + 16 if last else 4 * r
    payload = (shards, rows, 128)
    grid_spec = pltpu.PrefetchScalarGridSpec(
        num_scalar_prefetch=2,
        grid=(chunks,),
        in_specs=[
            wide,
            pl.BlockSpec((1, CHUNK), lambda c, *_: (0, back(c))),
        ]
        + [tile] * 8
        + [state] * 2
        + [
            pl.BlockSpec((4, 32, 16, QUAD), lambda c, *_: (0, 0, 0, quad)),
            whole((8, 512)),
        ]
        + [wide] * len(extra),
        out_specs=[wide, whole(payload), whole(payload)],
        scratch_shapes=[
            pltpu.VMEM((QUAD, QUAD), F32),
            pltpu.VMEM((QUAD, QUAD), F32),
            pltpu.VMEM((8, QUAD), F32),
            pltpu.VMEM((512, 4 * QUAD), F32),
            pltpu.VMEM((8, 512), F32),
        ],
    )
    return pl.pallas_call(
        functools.partial(attention_backward, last, shards),
        grid_spec=grid_spec,
        out_shape=[shaped((length, 512), F32), shaped(payload, BF16), shaped(payload, BF16)],
        compiler_params=params(),
        cost_estimate=pl.CostEstimate(
            flops=15_000_000_000, bytes_accessed=12_000_000, transcendentals=0
        ),
        name=f"attention_backward_{quad}",
    )(segments, position, x, seg_row, *saved, grad_mix[0], *grad_mix[1:], weights, vectors, *extra)


def swap(value, axis, bit):
    n = lax.axis_size(axis)
    return lax.ppermute(value, axis, [(i, i ^ bit) for i in range(n)])


def swap_both(value, rep_bit, shard_bit):
    n, m = lax.axis_size("rep"), lax.axis_size("shard")
    pairs = [
        (a * m + b, (a ^ rep_bit) * m + (b ^ shard_bit)) for a in range(n) for b in range(m)
    ]
    return lax.ppermute(value, ("rep", "shard"), pairs)


def bit_groups(shards):
    bits = shards.bit_length() - 1
    return [(low, min(2, bits - low)) for low in range(1, bits, 2)]


def gather(payload):
    shards = lax.axis_size("shard")
    held = payload[None]
    for low, width in [(0, 1)] + bit_groups(shards):
        arrived = [swap(held, "shard", a << low) for a in range(1, 1 << width)]
        held = jnp.concatenate([held] + arrived, axis=0)
    return held, swap(held, "rep", 1)


def add_low(*parts):
    return sum(part.astype(F32) for part in parts).astype(BF16)


def reduce_shares(keep, send):
    shards = lax.axis_size("shard")
    me = lax.axis_index("shard")
    rows, columns = keep.shape[1:]
    current = (keep, swap(send, "rep", 1))
    for low, width in reversed(bit_groups(shards)):
        ways = 1 << width
        mine = (me >> low) & (ways - 1)
        views = [part.reshape(ways, -1, rows, columns) for part in current]
        pieces = [
            add_low(*(lax.dynamic_index_in_dim(v, mine ^ a, 0, keepdims=False) for v in views))
            for a in range(ways)
        ]
        arrived = [swap(pieces[a], "shard", a << low) for a in range(1, ways)]
        current = (pieces[0], *arrived)
    both = add_low(*current)
    own = lax.dynamic_index_in_dim(both, me & 1, 0, keepdims=False)
    other = lax.dynamic_index_in_dim(both, (me & 1) ^ 1, 0, keepdims=False)
    from_y = swap(other, "shard", 1)
    from_x = swap(own, "rep", 2)
    from_xy = swap_both(other, 2, 1)
    here = own.astype(F32) + from_y.astype(F32)
    there = from_x.astype(F32) + from_xy.astype(F32)
    total = (here + there).astype(BF16)
    bit = 4
    while bit < lax.axis_size("rep"):
        total = add_low(total, swap(total, "rep", bit))
        bit *= 2
    sibling = swap(total, "rep", 1)
    first = lax.axis_index("rep") % 2 == 0
    left = jnp.where(first, total, sibling).astype(F32)
    right = jnp.where(first, sibling, total).astype(F32)
    return left, right


def local(
    inputs,
    segments,
    valid_mask,
    teacher,
    query_weight,
    key_weight,
    value_weight,
    control_weight,
    output_weight,
    gain_first,
    shift_first,
    expand_weight,
    expand_bias,
    contract_weight,
    contract_bias,
    gain_second,
    shift_second,
):
    _, length, width = inputs.shape
    shards, reps = lax.axis_size("shard"), lax.axis_size("rep")
    r = width // shards
    core = lax.axis_index("rep") % 2
    position = jnp.stack([lax.axis_index("shard"), core]).astype(jnp.int32)

    count = jnp.sum(valid_mask)
    count_pair = jnp.stack([count // 256, count % 256]).astype(BF16)

    def padded(vector):
        return jnp.pad(vector, (0, 256 - vector.shape[0]))

    blank = jnp.zeros((256,), BF16)
    rows = [gain_first, shift_first, gain_second, shift_second, contract_bias, blank, count_pair]
    rows += [blank, expand_bias] + [blank] * 7
    vec_block = jnp.stack([padded(v) for v in rows])[None]

    def my_half(matrix):
        halves = matrix.reshape(matrix.shape[0], -1, 2, 256)
        return lax.dynamic_index_in_dim(halves, core, 2, keepdims=False)

    mixer = jnp.stack([query_weight, key_weight, value_weight, control_weight])
    mixer = my_half(mixer.reshape(4 * r, width)).reshape(4 * r // 16, 16, 256)
    mine_a, theirs_a = gather(jnp.concatenate([mixer, vec_block], axis=0))
    branch = jnp.concatenate(
        [
            my_half(output_weight).reshape(1, r // 16, 16, 256),
            my_half(expand_weight).transpose(1, 0, 2).reshape(4, r // 16, 16, 256),
            my_half(contract_weight).reshape(4, r // 16, 16, 256),
        ],
        axis=0,
    )
    branch, mine_a = lax.optimization_barrier((branch, mine_a))
    mine_b, theirs_b = gather(branch)

    x = inputs.reshape(length, width)
    seg_row = segments.astype(F32)
    seg_flat = segments.reshape(length)
    forward = call_forward(shards, seg_row, seg_flat, position, x, mine_a, theirs_a)
    saved, mixed, one, two = forward[:7], forward[7], forward[8], forward[9]
    weights, vectors, bias, count_part = forward[10:]
    bit = 2
    while bit < reps:
        count_part = count_part + swap(count_part, "rep", bit)
        bit *= 2

    layer_out, grad_hidden, grad_mix, keep_f, send_f, loss = call_feed_forward(
        shards,
        float(length * shards * reps),
        position,
        x,
        mixed,
        teacher.reshape(length, width),
        valid_mask.astype(F32),
        vectors,
        bias,
        count_part,
        mine_b,
        theirs_b,
    )
    back = functools.partial(
        call_backward,
        shards=shards,
        seg_row=seg_row,
        segments=seg_flat,
        position=position,
        x=x,
        saved=saved,
        grad_mix=(grad_mix, one, two),
        weights=weights,
        vectors=vectors,
    )
    part, keep_0, send_0 = back(0, extra=())
    grad_inputs, keep_1, send_1 = back(1, extra=(part, grad_hidden))

    left_f, right_f = reduce_shares(keep_f, send_f)
    left_0, right_0 = reduce_shares(keep_0, send_0)
    left_1, right_1 = reduce_shares(keep_1, send_1)

    for axis, size in (("rep", reps), ("shard", shards)):
        bit = 1
        while bit < size:
            loss = loss + swap(loss, axis, bit)
            bit *= 2
    count_all = 256.0 * count_part[6, 0] + count_part[6, 1]
    loss_value = loss[0, 0] / (2.0 * count_all)

    mats = []
    for m in range(4):
        at = slice(m * r, (m + 1) * r)
        mats.append(
            jnp.concatenate([left_0[at], right_0[at], left_1[at], right_1[at]], axis=1)
        )
    grad_output = jnp.concatenate([left_f[:r], right_f[:r]], axis=1)
    expand_parts = []
    for b in range(4):
        at = slice((1 + b) * r, (2 + b) * r)
        expand_parts += [left_f[at], right_f[at]]
    grad_expand = jnp.concatenate(expand_parts, axis=1)
    grad_contract = jnp.concatenate([left_f[5 * r : 9 * r], right_f[5 * r : 9 * r]], axis=1)
    vec_f, vec_1 = left_f[9 * r :], left_1[4 * r :]
    return (
        layer_out.reshape(inputs.shape),
        grad_inputs.reshape(inputs.shape),
        loss_value,
        *mats,
        grad_output,
        vec_1[0, :r],
        vec_1[1, :r],
        grad_expand,
        vec_f[8, : 4 * r],
        grad_contract,
        vec_f[2, :r],
        vec_f[0, :r],
        vec_f[1, :r],
    )


def solution(mesh):
    every = P(("rep", "shard"), None, None)
    every_row = P(("rep", "shard"), None)
    matrix, vector = P("shard", None), P("shard")
    in_specs = (
        every,
        every_row,
        every_row,
        every,
        *[matrix] * 5,
        *[vector] * 2,
        matrix,
        vector,
        matrix,
        *[vector] * 3,
    )
    out_specs = (
        every,
        every,
        P(),
        *[matrix] * 5,
        *[vector] * 2,
        matrix,
        vector,
        matrix,
        *[vector] * 3,
    )
    return jax.shard_map(local, mesh=mesh, in_specs=in_specs, out_specs=out_specs, check_vma=False)
```

```python
import functools

import jax
import jax.numpy as jnp
from jax import lax
from jax.experimental import pallas as pl
from jax.experimental.pallas import tpu as pltpu
from jax.sharding import PartitionSpec as P

HEADS = 8
EPSILON = 1e-05
CHUNK = 256
QUAD = 256
F32 = jnp.float32
BF16 = jnp.bfloat16
VMEM_LIMIT = 60 << 20
LOSS_DIGITS = 30
LOSS_ZERO = 10
COST = pl.CostEstimate(flops=1000, bytes_accessed=1000, transcendentals=0)


def place():
    rep = lax.axis_index("rep")
    return lax.axis_index("shard"), rep % 2, (rep // 2) % 2


def slots_of(shards):
    ways = shards // 2
    low, high = range(ways // 2), range(ways // 2, ways)
    first = [(z, y, x) for x in (0, 1) for y in (0, 1) for z in low]
    second = [(z, y, x) for y in (0, 1) for x in (0, 1) for z in high]
    return first + second


def nn(left, right):
    return jnp.dot(left, right, preferred_element_type=F32)


def nt(left, right):
    return lax.dot_general(left, right, (((1,), (1,)), ((), ())), preferred_element_type=F32)


def tn(left, right):
    return lax.dot_general(left, right, (((0,), (0,)), ((), ())), preferred_element_type=F32)


def head_lanes():
    lane = lax.broadcasted_iota(jnp.int32, (1, QUAD), 1) // 64
    return [jnp.where(lane == h, 1.0, 0.0).astype(BF16) for h in range(4)]


def block_diagonal():
    rows = lax.broadcasted_iota(jnp.int32, (QUAD, QUAD), 0) // 64
    columns = lax.broadcasted_iota(jnp.int32, (QUAD, QUAD), 1) // 64
    return jnp.where(rows == columns, 1.0, 0.0)


def as_column(row):
    return jnp.broadcast_to(row, (CHUNK, CHUNK)).T


def causal_mask(column, row):
    at = lax.broadcasted_iota(jnp.int32, (CHUNK, CHUNK), 0)
    source = lax.broadcasted_iota(jnp.int32, (CHUNK, CHUNK), 1)
    return jnp.where((column == row) & (source <= at), 1.0, 0.0)


def causal_mask_transposed(column, row):
    source = lax.broadcasted_iota(jnp.int32, (CHUNK, CHUNK), 0)
    at = lax.broadcasted_iota(jnp.int32, (CHUNK, CHUNK), 1)
    return jnp.where((column == row) & (source <= at), 1.0, 0.0)


def per_head(values, reduce, fill):
    lane = lax.broadcasted_iota(jnp.int32, (1, 128), 1)
    first = lane < 64
    tiles = []
    for tile in range(values.shape[1] // 128):
        part = values[:, tile * 128 : (tile + 1) * 128]
        one = reduce(jnp.where(first, part, fill), axis=-1, keepdims=True)
        two = reduce(jnp.where(first, fill, part), axis=-1, keepdims=True)
        tiles.append(jnp.where(first, one, two))
    return jnp.concatenate(tiles, axis=1)


def standardise(values):
    mean = jnp.mean(values, axis=-1, keepdims=True)
    centred = values - mean
    variance = jnp.mean(centred * centred, axis=-1, keepdims=True)
    scale = lax.rsqrt(variance + EPSILON)
    return centred * scale, scale


def norm_backward(gradient, gain, normal, scale):
    upstream = gradient * gain
    one = jnp.mean(upstream, axis=-1, keepdims=True)
    two = jnp.mean(upstream * normal, axis=-1, keepdims=True)
    return (upstream - one - normal * two) * scale


def spread(rows, shards):
    width = 512 // shards
    lane = lax.broadcasted_iota(jnp.int32, (8, 128), 1)
    tiles = [None] * 4
    for s in range(shards):
        tile, offset = divmod(s * width, 128)
        moved = pltpu.roll(rows[s], offset, 1) if offset else rows[s]
        inside = (lane >= offset) & (lane < offset + width)
        tiles[tile] = jnp.where(inside, moved, 0.0 if tiles[tile] is None else tiles[tile])
    return jnp.concatenate(tiles, axis=1)


def digits_of(value):
    lane = lax.broadcasted_iota(jnp.int32, (8, 128), 1)
    scale = jnp.zeros((8, 128), F32)
    for k in range(LOSS_DIGITS):
        scale = jnp.where(lane == k, 8.0 ** (LOSS_ZERO - k), scale)
    shifted = value * scale
    return jnp.floor(shifted) - 8.0 * jnp.floor(shifted * 0.125)


def piece_of(vectors, s, width):
    tile, offset = divmod(s * width, 128)
    part = vectors[:, tile * 128 : (tile + 1) * 128]
    return pltpu.roll(part, 128 - offset, 1) if offset else part


def pack(shards, *refs):
    query, key, value, control, output, expand, contract = refs[:7]
    gain_1, shift_1, gain_2, shift_2, bias_2, bias_1, valid = refs[7:14]
    mixer_ref, branch_ref = refs[14:]
    r = 512 // shards
    _, core, cross = place()

    def write(half, third):
        at = slice(half * 256, half * 256 + 256)
        for m, ref in enumerate(((query, key), (value, control))[third]):
            mixer_ref[m * r : (m + 1) * r] = ref[:, at]
        if third == 0:
            for b in range(4):
                part = expand[:, b * 512 + half * 256 : b * 512 + half * 256 + 256]
                branch_ref[b * r : (b + 1) * r] = part
        else:
            branch_ref[0 : 4 * r] = contract[:, at]
        branch_ref[4 * r : 4 * r + r // 2] = output[third * (r // 2) : (third + 1) * (r // 2), at]

    for half in range(2):
        for third in range(2):
            pl.when((core == half) & (cross == third))(functools.partial(write, half, third))

    row = lax.broadcasted_iota(jnp.int32, (16, 256), 0)
    lane = lax.broadcasted_iota(jnp.int32, (16, 256), 1)
    block = jnp.zeros((16, 256), F32)
    for k, ref in ((0, gain_1), (1, shift_1), (2, gain_2), (3, shift_2), (4, bias_2), (8, bias_1)):
        part = ref[...].astype(F32)
        width = part.shape[1]
        if width < 256:
            part = jnp.concatenate([part, jnp.zeros((1, 256 - width), F32)], axis=1)
        block = jnp.where(row == k, part, block)
    count = jnp.sum(valid[...].astype(F32))
    high = jnp.floor(count / 256.0)
    block = jnp.where((row == 6) & (lane == 0), high, block)
    block = jnp.where((row == 6) & (lane == 1), count - 256.0 * high, block)
    mixer_ref[2 * r : 2 * r + 16] = block.astype(BF16)


def attention_forward(quad, shards, seg_s, x_ref, seg_ref, *refs):
    step = pl.program_id(0)
    r = 512 // shards
    at = slice(quad * QUAD, (quad + 1) * QUAD)
    if quad == 0:
        mine_ref, theirs_ref = refs[:2]
        q_ref, k_ref, v_ref, e_ref, p_ref, s_ref, rz_ref, mix_ref, one_ref, two_ref = refs[2:12]
        w_ref, vec_ref, eb_ref = refs[12:15]
        held, first_state, second_state, total_state, sems = refs[15:]
        weight = lambda m: w_ref[m, :, at]
    else:
        w_ref, vec_ref = refs[:2]
        q_ref, k_ref, v_ref, e_ref, p_ref, s_ref, rz_ref, mix_ref, one_ref, two_ref = refs[2:12]
        first_state, second_state, total_state = refs[12:]
        weight = lambda m: w_ref[m]

    @pl.when(step == 0)
    def _():
        first_state[...] = jnp.zeros_like(first_state)
        second_state[...] = jnp.zeros_like(second_state)
        total_state[...] = jnp.zeros_like(total_state)

    def assemble():
        me, core, cross = place()
        for half, source in enumerate((mine_ref, theirs_ref)):
            column = pl.multiple_of(((core + half) % 2) * 256, 256)
            for slot, (z, y, x) in enumerate(slots_of(shards)):
                owner = me ^ (2 * z + y)
                third = cross ^ x
                for m in range(2):
                    pltpu.make_async_copy(
                        source.at[slot, pl.ds(m * r, r)],
                        w_ref.at[
                            2 * third + m,
                            pl.ds(pl.multiple_of(owner * r, r), r),
                            pl.ds(column, 256),
                        ],
                        sems.at[0],
                    ).start()
                if half == 0 and x == 0:
                    pltpu.make_async_copy(
                        source.at[slot, pl.ds(2 * r, 16)], held.at[owner], sems.at[1]
                    ).start()
        pltpu.make_async_copy(held, held, sems.at[1]).wait()
        own = [held[s].astype(F32) for s in range(shards)]
        vec_ref[...] = spread([part[:8, :128] for part in own], shards)
        width = 2048 // shards
        lane = lax.broadcasted_iota(jnp.int32, (8, 128), 1)
        if width >= 128:
            for s in range(shards):
                eb_ref[:, s * width : (s + 1) * width] = own[s][8:16, :width]
        else:
            for tile in range(16):
                built = jnp.zeros((8, 128), F32)
                for k in range(128 // width):
                    part = own[tile * (128 // width) + k][8:16, :128]
                    moved = pltpu.roll(part, k * width, 1) if k else part
                    built = jnp.where((lane >= k * width) & (lane < (k + 1) * width), moved, built)
                eb_ref[:, tile * 128 : (tile + 1) * 128] = built
        pltpu.make_async_copy(w_ref, w_ref, sems.at[0]).wait()

    if quad == 0:
        pl.when(step == 0)(assemble)

    start = step * CHUNK
    segment_last = seg_s[0, start + CHUNK - 1]
    segment_before = jnp.where(step == 0, -1, seg_s[0, jnp.maximum(start - 1, 0)])
    keep = jnp.where(segment_last == segment_before, 1.0, 0.0)
    row = seg_ref[...].astype(F32)
    column = as_column(row)
    causal = causal_mask(column, row).astype(BF16)
    enters = jnp.where(column == segment_before.astype(F32), 1.0, 0.0)
    leaves = jnp.where(column == segment_last.astype(F32), 1.0, 0.0).astype(BF16)
    lanes = head_lanes()
    diagonal = block_diagonal()

    normal, _ = standardise(x_ref[...].astype(F32))
    normed = (normal * vec_ref[0:1, :] + vec_ref[1:2, :]).astype(BF16)
    queries = nn(normed, weight(0)).astype(BF16)
    keys = nn(normed, weight(1)).astype(BF16)
    values = nn(normed, weight(2)).astype(BF16)
    slots = jnp.exp(nn(normed, weight(3))).astype(BF16)
    q_ref[...] = queries
    k_ref[...] = keys
    v_ref[...] = values
    e_ref[...] = slots
    totals = nn(causal, slots) + enters * total_state[0:1, :]
    total_state[0:1, :] = totals[CHUNK - 1 : CHUNK, :]
    inverse = 1.0 / totals
    rz_ref[...] = inverse
    one = first_state[...].astype(BF16)
    two = second_state[...].astype(BF16)
    one_ref[0] = one
    two_ref[0] = two
    scores = jnp.concatenate(
        [nt(queries * lanes[h], keys).astype(BF16) * causal for h in range(4)], axis=1
    )
    gathered = nn(scores, jnp.concatenate([slots * lanes[h] for h in range(4)], axis=0))
    gathered += enters * nn(queries, one)
    slot_scores = gathered * (inverse * 0.125)
    raised = jnp.exp(slot_scores - per_head(slot_scores, jnp.max, -jnp.inf))
    shares = raised / per_head(raised, jnp.sum, 0.0)
    s_ref[...] = slot_scores.astype(BF16)
    p_ref[...] = shares.astype(BF16)
    scaled = (shares * inverse).astype(BF16)
    mixing = jnp.concatenate(
        [nt(scaled * lanes[h], slots).astype(BF16) * causal for h in range(4)], axis=1
    )
    mixed = nn(mixing, jnp.concatenate([values * lanes[h] for h in range(4)], axis=0))
    mixed += enters * nn(scaled, two)
    mix_ref[...] = mixed.astype(BF16)
    first_state[...] = keep * first_state[...] + diagonal * tn(keys * leaves, slots)
    second_state[...] = keep * second_state[...] + diagonal * tn(slots * leaves, values)


def feed_forward(
    shards,
    tokens,
    x_ref,
    mix_0_ref,
    mix_1_ref,
    teacher_ref,
    valid_ref,
    vec_ref,
    eb_ref,
    count_ref,
    mine_ref,
    theirs_ref,
    out_ref,
    hidden_ref,
    grad_mix_ref,
    keep_1_ref,
    send_1_ref,
    keep_2_ref,
    send_2_ref,
    wo,
    we,
    wc,
    act,
    d_wo,
    d_we,
    d_wc,
    d_vec,
    d_eb,
    loss_ref,
    sems,
):
    step = pl.program_id(0)
    r = 512 // shards
    me, core, cross = place()

    @pl.when(step == 0)
    def _():
        loss_ref[...] = jnp.zeros_like(loss_ref)
        for half, source in enumerate((mine_ref, theirs_ref)):
            column = pl.multiple_of(((core + half) % 2) * 256, 256)
            for slot, (z, y, x) in enumerate(slots_of(shards)):
                owner = me ^ (2 * z + y)
                third = cross ^ x
                pltpu.make_async_copy(
                    source.at[slot, pl.ds(4 * r, r // 2)],
                    wo.at[2 * owner + third, :, pl.ds(column, 256)],
                    sems.at[0],
                ).start()

                def expansion():
                    for b in range(4):
                        pltpu.make_async_copy(
                            source.at[slot, pl.ds(b * r, r)],
                            we.at[
                                b, pl.ds(pl.multiple_of(owner * r, r), r), pl.ds(column, 256)
                            ],
                            sems.at[1],
                        ).start()

                def contraction():
                    pltpu.make_async_copy(
                        source.at[slot, pl.ds(0, 4 * r)],
                        wc.at[
                            pl.ds(pl.multiple_of(owner * 4 * r, 4 * r), 4 * r), pl.ds(column, 256)
                        ],
                        sems.at[2],
                    ).start()

                pl.when(third == 0)(expansion)
                pl.when(third == 1)(contraction)
        for ref in (d_wo, d_we, d_wc, d_vec, d_eb):
            ref[...] = jnp.zeros_like(ref)
        pltpu.make_async_copy(wo, wo, sems.at[0]).wait()
        pltpu.make_async_copy(we, we, sems.at[1]).wait()
        pltpu.make_async_copy(wc, wc, sems.at[2]).wait()

    gain, shift, bias = vec_ref[2:3, :], vec_ref[3:4, :], vec_ref[4:5, :]
    weight_out = wo[...].reshape(512, 512)
    mixed = jnp.concatenate([mix_0_ref[...], mix_1_ref[...]], axis=1)
    hidden = x_ref[...].astype(F32) + nn(mixed, weight_out)
    normal, scale = standardise(hidden)
    normed = (normal * gain + shift).astype(BF16)
    for b in range(4):
        at = slice(b * 512, (b + 1) * 512)
        before = nn(normed, we[b]) + eb_ref[0:1, at]
        act[:, at] = jnp.maximum(before, 0.0).astype(BF16)
    result = hidden + (nn(act[...], wc[...]) + bias)
    out_ref[...] = result.astype(BF16)
    valid = as_column(valid_ref[...].astype(F32))
    valid = jnp.concatenate([valid, valid], axis=1)
    error = result - teacher_ref[...].astype(F32)
    masked = valid * error
    loss_ref[...] += jnp.sum(masked * error)
    count = 256.0 * count_ref[0:1, 0:1] + count_ref[0:1, 1:2]
    grad_result = masked * (tokens / count)
    low = grad_result.astype(BF16)
    d_normed = None
    for b in range(4):
        at = slice(b * 512, (b + 1) * 512)
        active = act[:, at]
        d_wc[at, :] += tn(active, low)
        grad = jnp.where(active > 0, nt(low, wc[at, :]), 0.0)
        grad = grad.astype(BF16)
        d_we[b] += tn(normed, grad)
        d_eb[0:1, at] += jnp.sum(grad.astype(F32), axis=0, keepdims=True)
        part = nt(grad, we[b])
        d_normed = part if d_normed is None else d_normed + part
    d_vec[0:1, :] += jnp.sum(d_normed * normal, axis=0, keepdims=True)
    d_vec[1:2, :] += jnp.sum(d_normed, axis=0, keepdims=True)
    d_vec[2:3, :] += jnp.sum(low.astype(F32), axis=0, keepdims=True)
    grad_hidden = grad_result + norm_backward(d_normed, gain, normal, scale)
    hidden_ref[...] = grad_hidden
    grad_low = grad_hidden.astype(BF16)
    d_wo[...] += tn(mixed, grad_low)
    grad_mix_ref[...] = nt(grad_low, weight_out).astype(BF16)

    @pl.when(step == pl.num_programs(0) - 1)
    def _():
        width = 2048 // shards
        digits = digits_of(loss_ref[...])

        def write(first_ref, second_ref, at):
            for s in range(shards):
                y, z = (me ^ s) & 1, (me ^ s) >> 1
                rows = slice(s * r, (s + 1) * r)
                top = jnp.concatenate([piece_of(d_vec[...], s, r), digits], axis=1)
                if width >= 128:
                    low_rows = d_eb[:, s * width : (s + 1) * width]
                else:
                    low_rows = piece_of(d_eb[...], s, width)
                if low_rows.shape[1] < 256:
                    pad = jnp.zeros((8, 256 - low_rows.shape[1]), F32)
                    low_rows = jnp.concatenate([low_rows, pad], axis=1)
                both = jnp.concatenate([top, low_rows], axis=0).astype(BF16)
                for half in range(2):
                    x = cross ^ half
                    start = s * 4 * r + half * 2 * r
                    first_ref[y, x, z] = d_wc[start : start + 2 * r, at].astype(BF16)
                    for b in range(2):
                        part = d_we[2 * half + b, rows, at]
                        second_ref[x, y, z, b * r : (b + 1) * r, :] = part.astype(BF16)
                    second_ref[x, y, z, 2 * r : 2 * r + 16, :] = both
                    start = s * r + half * (r // 2)
                    part = d_wo[start : start + r // 2, at]
                    second_ref[x, y, z, 2 * r + 16 :, :] = part.astype(BF16)

        left, right = slice(0, 256), slice(256, 512)

        @pl.when(core == 0)
        def _():
            write(keep_1_ref, keep_2_ref, left)
            write(send_1_ref, send_2_ref, right)

        @pl.when(core == 1)
        def _():
            write(keep_1_ref, keep_2_ref, right)
            write(send_1_ref, send_2_ref, left)


def attention_backward(last, shards, seg_s, *refs):
    x_ref, seg_ref, q_ref, k_ref, v_ref, e_ref, p_ref, s_ref, rz_ref, g_ref = refs[:10]
    one_ref, two_ref, w_ref, vec_ref = refs[10:14]
    refs = refs[14:]
    if last:
        part_ref, hidden_ref = refs[:2]
        refs = refs[2:]
    out_ref, keep_ref, send_ref = refs[:3]
    first_state, second_state, total_state, d_w, d_vec = refs[3:]
    step = pl.program_id(0)
    chunks = pl.num_programs(0)
    chunk = chunks - 1 - step
    r = 512 // shards
    me, core, cross = place()

    @pl.when(step == 0)
    def _():
        for ref in (first_state, second_state, total_state, d_w, d_vec):
            ref[...] = jnp.zeros_like(ref)

    start = chunk * CHUNK
    length = chunks * CHUNK
    segment_first = seg_s[0, start]
    segment_before = jnp.where(chunk == 0, -1, seg_s[0, jnp.maximum(start - 1, 0)])
    segment_after = jnp.where(step == 0, -1, seg_s[0, jnp.minimum(start + CHUNK, length - 1)])
    keep = jnp.where(segment_first == segment_after, 1.0, 0.0)
    row = seg_ref[...].astype(F32)
    column = as_column(row)
    causal = causal_mask(column, row).astype(BF16)
    turned = causal_mask_transposed(column, row).astype(BF16)
    enters = jnp.where(column == segment_before.astype(F32), 1.0, 0.0)
    goes_on = jnp.where(column == segment_after.astype(F32), 1.0, 0.0)
    opens = jnp.where(column == segment_first.astype(F32), 1.0, 0.0).astype(BF16)
    lanes = head_lanes()
    diagonal = block_diagonal()

    def heads(values):
        return [values * lanes[h] for h in range(4)]

    def beside(parts):
        return jnp.concatenate(parts, axis=1)

    def stacked(parts):
        return jnp.concatenate(parts, axis=0)

    queries, keys, values, slots = q_ref[...], k_ref[...], v_ref[...], e_ref[...]
    shares, slot_scores = p_ref[...].astype(F32), s_ref[...].astype(F32)
    inverse, grad = rz_ref[...], g_ref[...]
    scaled = shares * inverse
    scaled_low = scaled.astype(BF16)
    one, two = one_ref[0], two_ref[0]
    one_back, two_back = first_state[...].astype(BF16), second_state[...].astype(BF16)
    grad_heads, slot_heads, value_heads = heads(grad), heads(slots), heads(values)
    slot_stack = stacked(slot_heads)

    d_mixing = beside([nt(part, values).astype(BF16) * causal for part in grad_heads])
    d_scaled = nn(d_mixing, slot_stack) + enters * nt(grad, two)
    d_shares = d_scaled * inverse
    product = shares * d_shares
    d_scores = product - shares * per_head(product, jnp.sum, 0.0)
    d_gathered = d_scores * inverse
    d_totals = -(d_scaled * scaled + d_scores * slot_scores) * inverse
    d_low = (d_gathered * 0.125).astype(BF16)
    d_low_heads = heads(d_low)

    d_raw = beside([nt(part, slots).astype(BF16) * causal for part in d_low_heads])
    d_queries = nn(d_raw, stacked(heads(keys))) + enters * nt(d_low, one)
    d_raw_t = beside([nt(part, d_low).astype(BF16) * turned for part in slot_heads])
    d_keys = nn(d_raw_t, stacked(heads(queries))) + goes_on * nt(slots, one_back)
    mixing_t = beside([nt(part, scaled_low).astype(BF16) * turned for part in slot_heads])
    d_values = nn(mixing_t, stacked(grad_heads)) + goes_on * nn(slots, two_back)
    scores_t = beside([nt(part, queries).astype(BF16) * turned for part in heads(keys)])
    d_slots = nn(scores_t, stacked(d_low_heads))
    d_mixing_t = beside([nt(part, grad).astype(BF16) * turned for part in value_heads])
    d_slots += nn(d_mixing_t, stacked(heads(scaled_low)))
    d_totals_low = d_totals.astype(BF16)
    rest = (d_totals - d_totals_low.astype(F32)).astype(BF16)
    sums = nn(turned, d_totals_low) + nn(turned, rest) + goes_on * total_state[0:1, :]
    d_slots += goes_on * (nn(keys, one_back) + nt(values, two_back)) + sums
    d_control = d_slots * slots.astype(F32)

    total_state[0:1, :] = sums[0:1, :]
    first_state[...] = keep * first_state[...] + diagonal * tn(queries * opens, d_low)
    second_state[...] = keep * second_state[...] + diagonal * tn(scaled_low * opens, grad)

    normal, scale = standardise(x_ref[...].astype(F32))
    gain = vec_ref[0:1, :]
    normed = (normal * gain + vec_ref[1:2, :]).astype(BF16)
    grads = [part.astype(BF16) for part in (d_queries, d_keys, d_values, d_control)]
    d_w[...] += tn(normed, beside(grads))
    d_normed = sum(nt(grads[m], w_ref[m]) for m in range(4))
    if last:
        d_normed += part_ref[...]
        d_vec[0:1, :] += jnp.sum(d_normed * normal, axis=0, keepdims=True)
        d_vec[1:2, :] += jnp.sum(d_normed, axis=0, keepdims=True)
        out_ref[...] = hidden_ref[...] + norm_backward(d_normed, gain, normal, scale)
    else:
        out_ref[...] = d_normed

    @pl.when(step == chunks - 1)
    def _():
        def write(ref, half):
            for s in range(shards):
                y, z = (me ^ s) & 1, (me ^ s) >> 1
                for m in range(4):
                    x = cross ^ (m // 2)
                    lead = (x, y, z) if last else (y, x, z)
                    at = slice(m * QUAD + half * 128, m * QUAD + half * 128 + 128)
                    part = d_w[s * r : (s + 1) * r, at].astype(BF16)
                    ref[(*lead, slice((m % 2) * r, (m % 2 + 1) * r), slice(None))] = part
                for x in range(2):
                    lead = (x, y, z) if last else (y, x, z)
                    top = piece_of(d_vec[...], s, r)
                    both = jnp.concatenate([top, jnp.zeros_like(top)], axis=0)
                    ref[(*lead, slice(2 * r, 2 * r + 16), slice(None))] = both.astype(BF16)

        @pl.when(core == 0)
        def _():
            write(keep_ref, 0)
            write(send_ref, 1)

        @pl.when(core == 1)
        def _():
            write(keep_ref, 1)
            write(send_ref, 0)


def whole(shape):
    return pl.BlockSpec(shape, lambda *_: (0,) * len(shape))


def anywhere():
    return pl.BlockSpec(memory_space=pl.ANY)


def shaped(shape, dtype):
    return jax.ShapeDtypeStruct(shape, dtype)


def params():
    return pltpu.CompilerParams(
        dimension_semantics=("arbitrary",), vmem_limit_bytes=VMEM_LIMIT
    )


def call_pack(shards, matrices, vectors, valid):
    r = 512 // shards
    operands = [*matrices, *[v[None] for v in vectors], valid]
    mixer, branch = (2 * r + 16, 256), (4 * r + r // 2, 256)
    return pl.pallas_call(
        functools.partial(pack, shards),
        grid=(1,),
        in_specs=[whole(v.shape) for v in operands],
        out_specs=[whole(mixer), whole(branch)],
        out_shape=[shaped(mixer, BF16), shaped(branch, BF16)],
        compiler_params=params(),
        cost_estimate=COST,
        name="pack",
    )(*operands)


def call_forward(quad, shards, segments, x, operands):
    length = x.shape[0]
    chunks = length // CHUNK
    wide = pl.BlockSpec((CHUNK, 512), lambda c, *_: (c, 0))
    tile = pl.BlockSpec((CHUNK, QUAD), lambda c, *_: (c, 0))
    state = pl.BlockSpec((1, QUAD, QUAD), lambda c, *_: (c, 0, 0))
    low = shaped((length, QUAD), BF16)
    states = shaped((chunks, QUAD, QUAD), BF16)
    if quad == 0:
        in_specs = [anywhere(), anywhere()]
        out_specs = [whole((4, 512, 512)), whole((8, 512)), whole((8, 2048))]
        out_shape = [shaped((4, 512, 512), BF16), shaped((8, 512), F32), shaped((8, 2048), F32)]
        first = [pltpu.VMEM((shards, 16, 256), BF16)]
        last = [pltpu.SemaphoreType.DMA((2,))]
    else:
        in_specs = [pl.BlockSpec((4, 512, QUAD), lambda c, *_: (0, 0, 1)), whole((8, 512))]
        out_specs, out_shape, first, last = [], [], [], []
    grid_spec = pltpu.PrefetchScalarGridSpec(
        num_scalar_prefetch=1,
        grid=(chunks,),
        in_specs=[wide, pl.BlockSpec((1, CHUNK), lambda c, *_: (0, c)), *in_specs],
        out_specs=[tile] * 8 + [state] * 2 + out_specs,
        scratch_shapes=first
        + [
            pltpu.VMEM((QUAD, QUAD), F32),
            pltpu.VMEM((QUAD, QUAD), F32),
            pltpu.VMEM((8, QUAD), F32),
        ]
        + last,
    )
    return pl.pallas_call(
        functools.partial(attention_forward, quad, shards),
        grid_spec=grid_spec,
        out_shape=[low] * 6 + [shaped((length, QUAD), F32), low, states, states] + out_shape,
        compiler_params=params(),
        cost_estimate=COST,
        name=f"attention_forward_{quad}",
    )(segments, x, segments, *operands)


def call_feed_forward(shards, tokens, *operands):
    length = operands[0].shape[0]
    chunks = length // CHUNK
    r = 512 // shards
    tile = lambda width: pl.BlockSpec((CHUNK, width), lambda c: (c, 0))
    first = (2, 2, shards // 2, 2 * r, 256)
    second = (2, 2, shards // 2, 2 * r + 16 + r // 2, 256)
    return pl.pallas_call(
        functools.partial(feed_forward, shards, tokens),
        grid=(chunks,),
        in_specs=[
            tile(512),
            tile(QUAD),
            tile(QUAD),
            tile(512),
            pl.BlockSpec((1, CHUNK), lambda c: (0, c)),
            whole((8, 512)),
            whole((8, 2048)),
            whole((1, 2)),
            anywhere(),
            anywhere(),
        ],
        out_specs=[tile(512)] * 3 + [whole(first)] * 2 + [whole(second)] * 2,
        out_shape=[
            shaped((length, 512), BF16),
            shaped((length, 512), F32),
            shaped((length, 512), BF16),
            *[shaped(first, BF16)] * 2,
            *[shaped(second, BF16)] * 2,
        ],
        scratch_shapes=[
            pltpu.VMEM((2 * shards, r // 2, 512), BF16),
            pltpu.VMEM((4, 512, 512), BF16),
            pltpu.VMEM((2048, 512), BF16),
            pltpu.VMEM((CHUNK, 2048), BF16),
            pltpu.VMEM((512, 512), F32),
            pltpu.VMEM((4, 512, 512), F32),
            pltpu.VMEM((2048, 512), F32),
            pltpu.VMEM((8, 512), F32),
            pltpu.VMEM((8, 2048), F32),
            pltpu.VMEM((8, 128), F32),
            pltpu.SemaphoreType.DMA((3,)),
        ],
        compiler_params=params(),
        cost_estimate=COST,
        name="feed_forward",
    )(*operands)


def call_backward(quad, shards, segments, x, saved, grad_mix, states, weights, vectors, extra):
    length = x.shape[0]
    chunks = length // CHUNK
    r = 512 // shards
    last = quad == 1
    back = lambda c: chunks - 1 - c
    wide = pl.BlockSpec((CHUNK, 512), lambda c, *_: (back(c), 0))
    own = pl.BlockSpec((CHUNK, QUAD), lambda c, *_: (back(c), 0))
    tile = pl.BlockSpec((CHUNK, QUAD), lambda c, *_: (back(c), quad))
    state = pl.BlockSpec((1, QUAD, QUAD), lambda c, *_: (back(c), 0, 0))
    payload = (2, 2, shards // 2, 2 * r + 16, 128)
    grid_spec = pltpu.PrefetchScalarGridSpec(
        num_scalar_prefetch=1,
        grid=(chunks,),
        in_specs=[
            wide,
            pl.BlockSpec((1, CHUNK), lambda c, *_: (0, back(c))),
            *[own] * 7,
            tile,
            *[state] * 2,
            pl.BlockSpec((4, 512, QUAD), lambda c, *_: (0, 0, quad)),
            whole((8, 512)),
            *[wide] * len(extra),
        ],
        out_specs=[wide, whole(payload), whole(payload)],
        scratch_shapes=[
            pltpu.VMEM((QUAD, QUAD), F32),
            pltpu.VMEM((QUAD, QUAD), F32),
            pltpu.VMEM((8, QUAD), F32),
            pltpu.VMEM((512, 4 * QUAD), F32),
            pltpu.VMEM((8, 512), F32),
        ],
    )
    return pl.pallas_call(
        functools.partial(attention_backward, last, shards),
        grid_spec=grid_spec,
        out_shape=[shaped((length, 512), F32), shaped(payload, BF16), shaped(payload, BF16)],
        compiler_params=params(),
        cost_estimate=COST,
        name=f"attention_backward_{quad}",
    )(segments, x, segments, *saved, grad_mix, *states, weights, vectors, *extra)


def swap(value, axis, bit):
    n = lax.axis_size(axis)
    return lax.ppermute(value, axis, [(i, i ^ bit) for i in range(n)])


def bit_groups(shards):
    bits = shards.bit_length() - 1
    return [(low, min(2, bits - low)) for low in range(1, bits, 2)]


def after(value, *others):
    return lax.optimization_barrier((value, *others))[0]


def add_low(*parts):
    return sum(part.astype(F32) for part in parts).astype(BF16)


def local(
    inputs,
    segments,
    valid_mask,
    teacher,
    query_weight,
    key_weight,
    value_weight,
    control_weight,
    output_weight,
    gain_first,
    shift_first,
    expand_weight,
    expand_bias,
    contract_weight,
    contract_bias,
    gain_second,
    shift_second,
):
    _, length, width = inputs.shape
    shards, reps = lax.axis_size("shard"), lax.axis_size("rep")
    r = width // shards
    core = lax.axis_index("rep") % 2
    cross = (lax.axis_index("rep") // 2) % 2
    groups = bit_groups(shards)

    matrices = (query_weight, key_weight, value_weight, control_weight, output_weight)
    matrices += (expand_weight, contract_weight)
    biases = (gain_first, shift_first, gain_second, shift_second, contract_bias, expand_bias)
    mixer, branch = call_pack(shards, matrices, biases, valid_mask)

    def along_z(payload):
        held = [payload[None]]
        for low, bits in groups:
            if len(held) > 1:
                held = [jnp.concatenate(held, axis=0)]
            held += [swap(held[0], "shard", a << low) for a in range(1, 1 << bits)]
        return held

    def halves(held):
        half = shards // 4
        if len(held) == 4:
            groups_of = [[], held[:2], held[2:]]
            return jnp.concatenate(held[:2], axis=0), jnp.concatenate(held[2:], axis=0)
        joined = jnp.concatenate(held, axis=0)
        return joined[:half], joined[half:]

    def step_one(first, second):
        return swap(first, "shard", 1), swap(second, "rep", 2)

    def join(first, second, arrived):
        return jnp.concatenate([first, arrived[0]]), jnp.concatenate([second, arrived[1]])

    def step_two(first, second):
        return swap(first, "rep", 2), swap(second, "shard", 1)

    held_a = along_z(mixer)
    branch = after(branch, held_a[1:])
    held_b = along_z(branch)
    first, second = halves(held_a)
    arrived = step_one(first, second)
    first, second = join(first, second, arrived)
    arrived = step_two(first, second)
    mine_a = jnp.concatenate([first, arrived[0], second, arrived[1]])
    theirs_a = swap(mine_a, "rep", 1)

    first, second = halves(after(held_b, arrived))
    pending = step_one(first, second)

    own_slots = [n for n, slot in enumerate(slots_of(shards)) if slot[2] == 0]
    count = sum(
        part[n : n + 1, 2 * r + 6, :2].astype(F32) for part in (mine_a, theirs_a) for n in own_slots
    )
    bit = 2
    while bit < reps:
        count = count + swap(count, "rep", bit)
        bit *= 2

    x = inputs.reshape(length, width)
    forward_0 = call_forward(0, shards, segments, after(x, first, second), (mine_a, theirs_a))
    weights, vectors, bias = forward_0[10:]
    first, second = join(first, second, after(pending, forward_0[7]))
    pending = step_two(first, second)
    vectors = after(vectors, first, second)
    forward_1 = call_forward(1, shards, segments, x, (weights, vectors))
    mixed = (forward_0[7], forward_1[7])
    pending = after(pending, forward_1[7])
    mine_b = jnp.concatenate([first, pending[0], second, pending[1]])
    theirs_b = swap(mine_b, "rep", 1)

    layer_out, grad_hidden, grad_mix, keep_c, send_c, keep_e, send_e = call_feed_forward(
        shards,
        float(length * shards * reps),
        x,
        *mixed,
        teacher.reshape(length, width),
        valid_mask,
        vectors,
        bias,
        count,
        mine_b,
        theirs_b,
    )

    def core_swap(keep, send):
        return keep, swap(send, "rep", 1)

    def split(parts):
        return add_low(*(part[0] for part in parts)), add_low(*(part[1] for part in parts))

    def cross_first(parts):
        keep, send = split(parts)
        return keep, swap(send, "rep", 2)

    def row_first(parts):
        keep, send = split(parts)
        return keep, swap(send, "shard", 1)

    def z_stage(parts_list):
        current = parts_list
        for low, bits in reversed(groups):
            span = 1 << (low - 1)
            pieces = [
                jnp.concatenate(
                    [
                        add_low(*(part[a * span : (a + 1) * span] for part in parts))
                        for parts in current
                    ],
                    axis=1,
                )
                for a in range(1 << bits)
            ]
            arrived = [swap(pieces[a], "shard", a << low) for a in range(1, 1 << bits)]
            current = [(pieces[0], *arrived)]
        return current[0]

    def finish(parts):
        total = add_low(*(part[0] for part in parts))
        bit = 4
        while bit < reps:
            total = add_low(total, swap(total, "rep", bit))
            bit *= 2
        over = swap(total, "rep", 2)
        near = jnp.where(cross == 0, total, over)
        far = jnp.where(cross == 0, over, total)
        both = jnp.stack([near, far])
        sibling = swap(both, "rep", 1)
        left = jnp.where(core == 0, both, sibling)
        right = jnp.where(core == 0, sibling, both)
        return jnp.concatenate([left, right], axis=2).astype(F32)

    def back(quad, saved, grad_mix, extra):
        return call_backward(
            quad, shards, segments, x, saved[:7], grad_mix, saved[8:10], weights, vectors, extra
        )

    c_parts = row_first(core_swap(keep_c, send_c))
    e_parts = cross_first(core_swap(keep_e, send_e))
    grad_mix = after(grad_mix, c_parts[0], e_parts[0])
    part, keep_0, send_0 = back(0, forward_0, grad_mix, ())
    c_parts = (c_parts[0], after(c_parts[1], part))
    e_parts = (e_parts[0], after(e_parts[1], part))
    c_parts, e_parts = cross_first(c_parts), row_first(e_parts)
    parts_0 = core_swap(keep_0, send_0)
    part = after(part, c_parts[0], e_parts[0])
    grad_inputs, keep_1, send_1 = back(1, forward_1, grad_mix, (part, grad_hidden))

    parts_0 = (parts_0[0], after(parts_0[1], grad_inputs))
    c_parts = (c_parts[0], after(c_parts[1], grad_inputs))
    e_parts = (e_parts[0], after(e_parts[1], grad_inputs))
    parts_1 = core_swap(keep_1, send_1)
    f_parts = z_stage([c_parts, e_parts])
    parts_0, parts_1 = row_first(parts_0), cross_first(parts_1)
    parts_0, parts_1 = cross_first(parts_0), row_first(parts_1)
    q_parts = z_stage([parts_0, parts_1])
    final_f = finish(f_parts)
    final_q = finish(q_parts)

    grad_contract = final_f[:, : 2 * r].reshape(4 * r, width)
    rest = final_f[:, 2 * r :]
    grad_expand = jnp.concatenate(
        [rest[h, b * r : (b + 1) * r] for h in range(2) for b in range(2)], axis=1
    )
    vec_f = rest[0, 2 * r : 2 * r + 16, :256]
    grad_output = rest[:, 2 * r + 16 :].reshape(r, width)
    mats = []
    for m in range(4):
        parts = [
            final_q[m // 2, q * (2 * r + 16) + (m % 2) * r : q * (2 * r + 16) + (m % 2 + 1) * r]
            for q in range(2)
        ]
        mats.append(jnp.concatenate(parts, axis=1))
    vec_1 = final_q[0, 4 * r + 32 - 16 : 4 * r + 32, :128]
    powers = jnp.array([8.0 ** (k - LOSS_ZERO) for k in range(LOSS_DIGITS)], F32)
    loss_sum = jnp.sum(vec_f[0, 128 : 128 + LOSS_DIGITS] * powers)
    loss_value = loss_sum / (2.0 * (256.0 * count[0, 0] + count[0, 1]))
    return (
        layer_out.reshape(inputs.shape),
        grad_inputs.reshape(inputs.shape),
        loss_value,
        *mats,
        grad_output,
        vec_1[0, :r],
        vec_1[1, :r],
        grad_expand,
        vec_f[8, : 4 * r],
        grad_contract,
        vec_f[2, :r],
        vec_f[0, :r],
        vec_f[1, :r],
    )


def solution(mesh):
    every = P(("rep", "shard"), None, None)
    every_row = P(("rep", "shard"), None)
    matrix, vector = P("shard", None), P("shard")
    in_specs = (
        every,
        every_row,
        every_row,
        every,
        *[matrix] * 5,
        *[vector] * 2,
        matrix,
        vector,
        matrix,
        *[vector] * 3,
    )
    out_specs = (
        every,
        every,
        P(),
        *[matrix] * 5,
        *[vector] * 2,
        matrix,
        vector,
        matrix,
        *[vector] * 3,
    )
    return jax.shard_map(local, mesh=mesh, in_specs=in_specs, out_specs=out_specs, check_vma=False)
```

```python
import functools

import jax
import jax.numpy as jnp
from jax import lax
from jax.experimental import pallas as pl
from jax.experimental.pallas import tpu as pltpu
from jax.sharding import PartitionSpec as P

HEADS = 8
EPSILON = 1e-05
CHUNK = 256
ROWS = 512
QUAD = 256
F32 = jnp.float32
BF16 = jnp.bfloat16
VMEM_LIMIT = 60 << 20
LOSS_DIGITS = 30
LOSS_ZERO = 10
COST = pl.CostEstimate(flops=1000, bytes_accessed=1000, transcendentals=0)


def ordered(kernel, at, count, *refs):
    kernel(*refs[:at], *refs[at + count :])


def place():
    rep = lax.axis_index("rep")
    return lax.axis_index("shard"), rep % 2, (rep // 2) % 2


def slots_of(shards):
    ways = shards // 2
    low, high = range(ways // 2), range(ways // 2, ways)
    first = [(z, y, x) for x in (0, 1) for y in (0, 1) for z in low]
    second = [(z, y, x) for y in (0, 1) for x in (0, 1) for z in high]
    return first + second


def nn(left, right):
    return jnp.dot(left, right, preferred_element_type=F32)


def nt(left, right):
    return lax.dot_general(left, right, (((1,), (1,)), ((), ())), preferred_element_type=F32)


def tn(left, right):
    return lax.dot_general(left, right, (((0,), (0,)), ((), ())), preferred_element_type=F32)


def head_lanes():
    lane = lax.broadcasted_iota(jnp.int32, (1, QUAD), 1) // 64
    return [jnp.where(lane == h, 1.0, 0.0).astype(BF16) for h in range(4)]


def block_diagonal():
    rows = lax.broadcasted_iota(jnp.int32, (QUAD, QUAD), 0) // 64
    columns = lax.broadcasted_iota(jnp.int32, (QUAD, QUAD), 1) // 64
    return jnp.where(rows == columns, 1.0, 0.0)


def as_column(row, width):
    tile = jnp.broadcast_to(row, (128, row.shape[1])).T
    return jnp.concatenate([tile] * (width // 128), axis=1)


def causal_mask(column, row):
    at = lax.broadcasted_iota(jnp.int32, (CHUNK, CHUNK), 0)
    source = lax.broadcasted_iota(jnp.int32, (CHUNK, CHUNK), 1)
    return jnp.where((column == row) & (source <= at), 1.0, 0.0)


def causal_mask_transposed(column, row):
    source = lax.broadcasted_iota(jnp.int32, (CHUNK, CHUNK), 0)
    at = lax.broadcasted_iota(jnp.int32, (CHUNK, CHUNK), 1)
    return jnp.where((column == row) & (source <= at), 1.0, 0.0)


def per_head(values, reduce, fill):
    lane = lax.broadcasted_iota(jnp.int32, (1, 128), 1)
    first = lane < 64
    tiles = []
    for tile in range(values.shape[1] // 128):
        part = values[:, tile * 128 : (tile + 1) * 128]
        one = reduce(jnp.where(first, part, fill), axis=-1, keepdims=True)
        two = reduce(jnp.where(first, fill, part), axis=-1, keepdims=True)
        tiles.append(jnp.where(first, one, two))
    return jnp.concatenate(tiles, axis=1)


def standardise(values):
    mean = jnp.mean(values, axis=-1, keepdims=True)
    centred = values - mean
    variance = jnp.mean(centred * centred, axis=-1, keepdims=True)
    scale = lax.rsqrt(variance + EPSILON)
    return centred * scale, scale


def norm_backward(gradient, gain, normal, scale):
    upstream = gradient * gain
    one = jnp.mean(upstream, axis=-1, keepdims=True)
    two = jnp.mean(upstream * normal, axis=-1, keepdims=True)
    return (upstream - one - normal * two) * scale


def spread(rows, shards):
    width = 512 // shards
    lane = lax.broadcasted_iota(jnp.int32, (8, 128), 1)
    tiles = [None] * 4
    for s in range(shards):
        tile, offset = divmod(s * width, 128)
        moved = pltpu.roll(rows[s], offset, 1) if offset else rows[s]
        inside = (lane >= offset) & (lane < offset + width)
        tiles[tile] = jnp.where(inside, moved, 0.0 if tiles[tile] is None else tiles[tile])
    return jnp.concatenate(tiles, axis=1)


def digits_of(value):
    lane = lax.broadcasted_iota(jnp.int32, (8, 128), 1)
    scale = jnp.zeros((8, 128), F32)
    for k in range(LOSS_DIGITS):
        scale = jnp.where(lane == k, 8.0 ** (LOSS_ZERO - k), scale)
    shifted = value * scale
    return jnp.floor(shifted) - 8.0 * jnp.floor(shifted * 0.125)


def piece_of(vectors, s, width):
    tile, offset = divmod(s * width, 128)
    part = vectors[:, tile * 128 : (tile + 1) * 128]
    return pltpu.roll(part, 128 - offset, 1) if offset else part


def pack(shards, *refs):
    query, key, value, control, output, expand, contract = refs[:7]
    gain_1, shift_1, gain_2, shift_2, bias_2, bias_1, valid = refs[7:14]
    mixer_ref, branch_ref = refs[14:]
    r = 512 // shards
    _, core, cross = place()

    def write(half, third):
        at = slice(half * 256, half * 256 + 256)
        for m, ref in enumerate(((query, key), (value, control))[third]):
            mixer_ref[m * r : (m + 1) * r] = ref[:, at]
        if third == 0:
            for b in range(4):
                part = expand[:, b * 512 + half * 256 : b * 512 + half * 256 + 256]
                branch_ref[b * r : (b + 1) * r] = part
        else:
            branch_ref[0 : 4 * r] = contract[:, at]
        branch_ref[4 * r : 4 * r + r // 2] = output[third * (r // 2) : (third + 1) * (r // 2), at]

    for half in range(2):
        for third in range(2):
            pl.when((core == half) & (cross == third))(functools.partial(write, half, third))

    row = lax.broadcasted_iota(jnp.int32, (16, 256), 0)
    lane = lax.broadcasted_iota(jnp.int32, (16, 256), 1)
    block = jnp.zeros((16, 256), F32)
    for k, ref in ((0, gain_1), (1, shift_1), (2, gain_2), (3, shift_2), (4, bias_2), (8, bias_1)):
        part = ref[...].astype(F32)
        width = part.shape[1]
        if width < 256:
            part = jnp.concatenate([part, jnp.zeros((1, 256 - width), F32)], axis=1)
        block = jnp.where(row == k, part, block)
    count = jnp.sum(valid[...].astype(F32))
    high = jnp.floor(count / 256.0)
    block = jnp.where((row == 6) & (lane == 0), high, block)
    block = jnp.where((row == 6) & (lane == 1), count - 256.0 * high, block)
    mixer_ref[2 * r : 2 * r + 16] = block.astype(BF16)


def attention_forward(quad, shards, seg_s, x_ref, seg_ref, *refs):
    step = pl.program_id(0)
    r = 512 // shards
    at = slice(quad * QUAD, (quad + 1) * QUAD)
    if quad == 0:
        mine_ref, theirs_ref = refs[:2]
        q_ref, k_ref, v_ref, e_ref, p_ref, s_ref, rz_ref, mix_ref, one_ref, two_ref = refs[2:12]
        w_ref, vec_ref, eb_ref, count_ref = refs[12:16]
        held, first_state, second_state, total_state, sems = refs[16:]
        weight = lambda m: w_ref[m, :, at]
    else:
        w_ref, vec_ref = refs[:2]
        q_ref, k_ref, v_ref, e_ref, p_ref, s_ref, rz_ref, mix_ref, one_ref, two_ref = refs[2:12]
        first_state, second_state, total_state = refs[12:]
        weight = lambda m: w_ref[m]

    @pl.when(step == 0)
    def _():
        first_state[...] = jnp.zeros_like(first_state)
        second_state[...] = jnp.zeros_like(second_state)
        total_state[...] = jnp.zeros_like(total_state)

    def assemble():
        me, core, cross = place()
        for half, source in enumerate((mine_ref, theirs_ref)):
            column = pl.multiple_of(((core + half) % 2) * 256, 256)
            for slot, (z, y, x) in enumerate(slots_of(shards)):
                owner = me ^ (2 * z + y)
                third = cross ^ x
                for m in range(2):
                    pltpu.make_async_copy(
                        source.at[slot, pl.ds(m * r, r)],
                        w_ref.at[
                            2 * third + m,
                            pl.ds(pl.multiple_of(owner * r, r), r),
                            pl.ds(column, 256),
                        ],
                        sems.at[0],
                    ).start()
                pltpu.make_async_copy(
                    source.at[slot, pl.ds(2 * r, 16)], held.at[2 * half + x, owner], sems.at[1]
                ).start()
        pltpu.make_async_copy(held, held, sems.at[1]).wait()
        own = [held[0, s].astype(F32) for s in range(shards)]
        count = sum(part[:8, :128] for part in own)
        for k in range(1, 4):
            count += jnp.sum(held[k, :, :8, :128].astype(F32), axis=0)
        count_ref[...] = count
        vec_ref[...] = spread([part[:8, :128] for part in own], shards)
        width = 2048 // shards
        lane = lax.broadcasted_iota(jnp.int32, (8, 128), 1)
        if width >= 128:
            for s in range(shards):
                eb_ref[:, s * width : (s + 1) * width] = own[s][8:16, :width]
        else:
            for tile in range(16):
                built = jnp.zeros((8, 128), F32)
                for k in range(128 // width):
                    part = own[tile * (128 // width) + k][8:16, :128]
                    moved = pltpu.roll(part, k * width, 1) if k else part
                    built = jnp.where((lane >= k * width) & (lane < (k + 1) * width), moved, built)
                eb_ref[:, tile * 128 : (tile + 1) * 128] = built
        pltpu.make_async_copy(w_ref, w_ref, sems.at[0]).wait()

    if quad == 0:
        pl.when(step == 0)(assemble)

    start = step * CHUNK
    segment_last = seg_s[0, start + CHUNK - 1]
    segment_before = jnp.where(step == 0, -1, seg_s[0, jnp.maximum(start - 1, 0)])
    keep = jnp.where(segment_last == segment_before, 1.0, 0.0)
    row = seg_ref[...].astype(F32)
    column = as_column(row, CHUNK)
    causal = causal_mask(column, row).astype(BF16)
    enters = jnp.where(column == segment_before.astype(F32), 1.0, 0.0)
    leaves = jnp.where(column == segment_last.astype(F32), 1.0, 0.0).astype(BF16)
    lanes = head_lanes()
    diagonal = block_diagonal()

    normal, _ = standardise(x_ref[...].astype(F32))
    normed = (normal * vec_ref[0:1, :] + vec_ref[1:2, :]).astype(BF16)
    queries = nn(normed, weight(0)).astype(BF16)
    keys = nn(normed, weight(1)).astype(BF16)
    values = nn(normed, weight(2)).astype(BF16)
    slots = jnp.exp(nn(normed, weight(3))).astype(BF16)
    q_ref[...] = queries
    k_ref[...] = keys
    v_ref[...] = values
    e_ref[...] = slots
    totals = nn(causal, slots) + enters * total_state[0:1, :]
    total_state[0:1, :] = totals[CHUNK - 1 : CHUNK, :]
    inverse = 1.0 / totals
    rz_ref[...] = inverse
    one = first_state[...].astype(BF16)
    two = second_state[...].astype(BF16)
    one_ref[0] = one
    two_ref[0] = two
    scores = jnp.concatenate(
        [nt(queries * lanes[h], keys).astype(BF16) * causal for h in range(4)], axis=1
    )
    gathered = nn(scores, jnp.concatenate([slots * lanes[h] for h in range(4)], axis=0))
    gathered += enters * nn(queries, one)
    slot_scores = gathered * (inverse * 0.125)
    raised = jnp.exp(slot_scores - per_head(slot_scores, jnp.max, -jnp.inf))
    shares = raised / per_head(raised, jnp.sum, 0.0)
    s_ref[...] = slot_scores.astype(BF16)
    p_ref[...] = shares.astype(BF16)
    scaled = (shares * inverse).astype(BF16)
    mixing = jnp.concatenate(
        [nt(scaled * lanes[h], slots).astype(BF16) * causal for h in range(4)], axis=1
    )
    mixed = nn(mixing, jnp.concatenate([values * lanes[h] for h in range(4)], axis=0))
    mixed += enters * nn(scaled, two)
    mix_ref[...] = mixed.astype(BF16)
    first_state[...] = keep * first_state[...] + diagonal * tn(keys * leaves, slots)
    second_state[...] = keep * second_state[...] + diagonal * tn(slots * leaves, values)


def feed_forward(
    shards,
    tokens,
    x_ref,
    mix_0_ref,
    mix_1_ref,
    teacher_ref,
    valid_ref,
    vec_ref,
    eb_ref,
    count_ref,
    mine_ref,
    theirs_ref,
    out_ref,
    hidden_ref,
    grad_mix_ref,
    keep_ref,
    send_ref,
    wo,
    we,
    wc,
    act,
    d_wo,
    d_we,
    d_wc,
    d_vec,
    d_eb,
    loss_ref,
    sems,
):
    step = pl.program_id(0)
    r = 512 // shards
    me, core, cross = place()

    @pl.when(step == 0)
    def _():
        loss_ref[...] = jnp.zeros_like(loss_ref)
        for half, source in enumerate((mine_ref, theirs_ref)):
            column = pl.multiple_of(((core + half) % 2) * 256, 256)
            for slot, (z, y, x) in enumerate(slots_of(shards)):
                owner = me ^ (2 * z + y)
                third = cross ^ x
                pltpu.make_async_copy(
                    source.at[slot, pl.ds(4 * r, r // 2)],
                    wo.at[2 * owner + third, :, pl.ds(column, 256)],
                    sems.at[0],
                ).start()

                def expansion():
                    for b in range(4):
                        pltpu.make_async_copy(
                            source.at[slot, pl.ds(b * r, r)],
                            we.at[
                                b, pl.ds(pl.multiple_of(owner * r, r), r), pl.ds(column, 256)
                            ],
                            sems.at[1],
                        ).start()

                def contraction():
                    pltpu.make_async_copy(
                        source.at[slot, pl.ds(0, 4 * r)],
                        wc.at[
                            pl.ds(pl.multiple_of(owner * 4 * r, 4 * r), 4 * r), pl.ds(column, 256)
                        ],
                        sems.at[2],
                    ).start()

                pl.when(third == 0)(expansion)
                pl.when(third == 1)(contraction)
        for ref in (d_wo, d_we, d_wc, d_vec, d_eb):
            ref[...] = jnp.zeros_like(ref)
        pltpu.make_async_copy(wo, wo, sems.at[0]).wait()

    gain, shift, bias = vec_ref[2:3, :], vec_ref[3:4, :], vec_ref[4:5, :]
    weight_out = wo[...].reshape(512, 512)
    mixed = jnp.concatenate([mix_0_ref[...], mix_1_ref[...]], axis=1)
    hidden = x_ref[...].astype(F32) + nn(mixed, weight_out)
    normal, scale = standardise(hidden)
    normed = (normal * gain + shift).astype(BF16)
    pl.when(step == 0)(lambda: pltpu.make_async_copy(we, we, sems.at[1]).wait())
    for b in range(4):
        at = slice(b * 512, (b + 1) * 512)
        before = nn(normed, we[b]) + eb_ref[0:1, at]
        act[:, at] = jnp.maximum(before, 0.0).astype(BF16)
    pl.when(step == 0)(lambda: pltpu.make_async_copy(wc, wc, sems.at[2]).wait())
    result = hidden + (nn(act[...], wc[...]) + bias)
    out_ref[...] = result.astype(BF16)
    valid = as_column(valid_ref[...].astype(F32), 512)
    error = result - teacher_ref[...].astype(F32)
    masked = valid * error
    loss_ref[...] += jnp.sum(masked * error)
    count = 256.0 * count_ref[6:7, 0:1] + count_ref[6:7, 1:2]
    grad_result = masked * (tokens / count)
    low = grad_result.astype(BF16)
    d_normed = None
    for b in range(4):
        at = slice(b * 512, (b + 1) * 512)
        active = act[:, at]
        d_wc[at, :] += tn(active, low)
        grad = jnp.where(active > 0, nt(low, wc[at, :]), 0.0)
        grad = grad.astype(BF16)
        d_we[b] += tn(normed, grad)
        d_eb[0:1, at] += jnp.sum(grad.astype(F32), axis=0, keepdims=True)
        part = nt(grad, we[b])
        d_normed = part if d_normed is None else d_normed + part
    d_vec[0:1, :] += jnp.sum(d_normed * normal, axis=0, keepdims=True)
    d_vec[1:2, :] += jnp.sum(d_normed, axis=0, keepdims=True)
    d_vec[2:3, :] += jnp.sum(low.astype(F32), axis=0, keepdims=True)
    grad_hidden = grad_result + norm_backward(d_normed, gain, normal, scale)
    hidden_ref[...] = grad_hidden
    grad_low = grad_hidden.astype(BF16)
    d_wo[...] += tn(mixed, grad_low)
    grad_mix_ref[...] = nt(grad_low, weight_out).astype(BF16)

    @pl.when(step == pl.num_programs(0) - 1)
    def _():
        width = 2048 // shards
        digits = digits_of(loss_ref[...])

        _, rows = branch_rows(shards, keep_ref.shape[0])

        def write(ref, at):
            for s in range(shards):
                top = jnp.concatenate([piece_of(d_vec[...], s, r), digits], axis=1)
                if width >= 128:
                    low_rows = d_eb[:, s * width : (s + 1) * width]
                else:
                    low_rows = piece_of(d_eb[...], s, width)
                if low_rows.shape[1] < 256:
                    pad = jnp.zeros((8, 256 - low_rows.shape[1]), F32)
                    low_rows = jnp.concatenate([low_rows, pad], axis=1)
                both = jnp.concatenate([top, low_rows], axis=0)
                for name, done, part, offset, size in rows:
                    if name == "contract":
                        value = d_wc[s * 4 * r + done : s * 4 * r + done + size, at]
                    elif name == "output":
                        value = d_wo[s * r + done : s * r + done + size, at]
                    elif name == "vectors":
                        value = both[done : done + size]
                    elif name == "none":
                        value = jnp.zeros((size, 256), F32)
                    else:
                        value = d_we[name, s * r + done : s * r + done + size, at]
                    ref[part, s, offset : offset + size, :] = value.astype(BF16)

        left, right = slice(0, 256), slice(256, 512)

        @pl.when(core == 0)
        def _():
            write(keep_ref, left)
            write(send_ref, right)

        @pl.when(core == 1)
        def _():
            write(keep_ref, right)
            write(send_ref, left)


def attention_backward(last, shards, seg_s, *refs):
    x_ref, seg_ref, q_ref, k_ref, v_ref, e_ref, p_ref, s_ref, rz_ref, g_ref = refs[:10]
    one_ref, two_ref, w_ref, vec_ref = refs[10:14]
    refs = refs[14:]
    if last:
        part_ref, hidden_ref = refs[:2]
        refs = refs[2:]
    out_ref, keep_ref, send_ref = refs[:3]
    first_state, second_state, total_state, d_w, d_vec = refs[3:]
    step = pl.program_id(0)
    chunks = pl.num_programs(0)
    chunk = chunks - 1 - step
    r = 512 // shards
    me, core, cross = place()

    @pl.when(step == 0)
    def _():
        for ref in (first_state, second_state, total_state, d_w, d_vec):
            ref[...] = jnp.zeros_like(ref)

    start = chunk * CHUNK
    length = chunks * CHUNK
    segment_first = seg_s[0, start]
    segment_before = jnp.where(chunk == 0, -1, seg_s[0, jnp.maximum(start - 1, 0)])
    segment_after = jnp.where(step == 0, -1, seg_s[0, jnp.minimum(start + CHUNK, length - 1)])
    keep = jnp.where(segment_first == segment_after, 1.0, 0.0)
    row = seg_ref[...].astype(F32)
    column = as_column(row, CHUNK)
    causal = causal_mask(column, row).astype(BF16)
    turned = causal_mask_transposed(column, row).astype(BF16)
    enters = jnp.where(column == segment_before.astype(F32), 1.0, 0.0)
    goes_on = jnp.where(column == segment_after.astype(F32), 1.0, 0.0)
    opens = jnp.where(column == segment_first.astype(F32), 1.0, 0.0).astype(BF16)
    lanes = head_lanes()
    diagonal = block_diagonal()

    def heads(values):
        return [values * lanes[h] for h in range(4)]

    def beside(parts):
        return jnp.concatenate(parts, axis=1)

    def stacked(parts):
        return jnp.concatenate(parts, axis=0)

    queries, keys, values, slots = q_ref[...], k_ref[...], v_ref[...], e_ref[...]
    shares, slot_scores = p_ref[...].astype(F32), s_ref[...].astype(F32)
    inverse, grad = rz_ref[...], g_ref[...]
    scaled = shares * inverse
    scaled_low = scaled.astype(BF16)
    one, two = one_ref[0], two_ref[0]
    one_back, two_back = first_state[...].astype(BF16), second_state[...].astype(BF16)
    grad_heads, slot_heads, value_heads = heads(grad), heads(slots), heads(values)
    slot_stack = stacked(slot_heads)

    d_mixing = beside([nt(part, values).astype(BF16) * causal for part in grad_heads])
    d_scaled = nn(d_mixing, slot_stack) + enters * nt(grad, two)
    d_shares = d_scaled * inverse
    product = shares * d_shares
    d_scores = product - shares * per_head(product, jnp.sum, 0.0)
    d_gathered = d_scores * inverse
    d_totals = -(d_scaled * scaled + d_scores * slot_scores) * inverse
    d_low = (d_gathered * 0.125).astype(BF16)
    d_low_heads = heads(d_low)

    d_raw = beside([nt(part, slots).astype(BF16) * causal for part in d_low_heads])
    d_queries = nn(d_raw, stacked(heads(keys))) + enters * nt(d_low, one)
    d_raw_t = beside([nt(part, d_low).astype(BF16) * turned for part in slot_heads])
    d_keys = nn(d_raw_t, stacked(heads(queries))) + goes_on * nt(slots, one_back)
    mixing_t = beside([nt(part, scaled_low).astype(BF16) * turned for part in slot_heads])
    d_values = nn(mixing_t, stacked(grad_heads)) + goes_on * nn(slots, two_back)
    scores_t = beside([nt(part, queries).astype(BF16) * turned for part in heads(keys)])
    d_slots = nn(scores_t, stacked(d_low_heads))
    d_mixing_t = beside([nt(part, grad).astype(BF16) * turned for part in value_heads])
    d_slots += nn(d_mixing_t, stacked(heads(scaled_low)))
    d_totals_low = d_totals.astype(BF16)
    rest = (d_totals - d_totals_low.astype(F32)).astype(BF16)
    sums = nn(turned, d_totals_low) + nn(turned, rest) + goes_on * total_state[0:1, :]
    d_slots += goes_on * (nn(keys, one_back) + nt(values, two_back)) + sums
    d_control = d_slots * slots.astype(F32)

    total_state[0:1, :] = sums[0:1, :]
    first_state[...] = keep * first_state[...] + diagonal * tn(queries * opens, d_low)
    second_state[...] = keep * second_state[...] + diagonal * tn(scaled_low * opens, grad)

    normal, scale = standardise(x_ref[...].astype(F32))
    gain = vec_ref[0:1, :]
    normed = (normal * gain + vec_ref[1:2, :]).astype(BF16)
    grads = [part.astype(BF16) for part in (d_queries, d_keys, d_values, d_control)]
    d_w[...] += tn(normed, beside(grads))
    d_normed = sum(nt(grads[m], w_ref[m]) for m in range(4))
    if last:
        d_normed += part_ref[...]
        d_vec[0:1, :] += jnp.sum(d_normed * normal, axis=0, keepdims=True)
        d_vec[1:2, :] += jnp.sum(d_normed, axis=0, keepdims=True)
        out_ref[...] = hidden_ref[...] + norm_backward(d_normed, gain, normal, scale)
    else:
        out_ref[...] = d_normed

    @pl.when(step == chunks - 1)
    def _():
        def write(ref, half):
            for s in range(shards):
                y, z = (me ^ s) & 1, (me ^ s) >> 1
                for m in range(4):
                    x = cross ^ (m // 2)
                    lead = (x, y, z) if last else (y, x, z)
                    at = slice(m * QUAD + half * 128, m * QUAD + half * 128 + 128)
                    part = d_w[s * r : (s + 1) * r, at].astype(BF16)
                    ref[(*lead, slice((m % 2) * r, (m % 2 + 1) * r), slice(None))] = part
                for x in range(2):
                    lead = (x, y, z) if last else (y, x, z)
                    top = piece_of(d_vec[...], s, r)
                    both = jnp.concatenate([top, jnp.zeros_like(top)], axis=0)
                    ref[(*lead, slice(2 * r, 2 * r + 16), slice(None))] = both.astype(BF16)

        @pl.when(core == 0)
        def _():
            write(keep_ref, 0)
            write(send_ref, 1)

        @pl.when(core == 1)
        def _():
            write(keep_ref, 1)
            write(send_ref, 0)


def whole(shape):
    return pl.BlockSpec(shape, lambda *_: (0,) * len(shape))


def anywhere():
    return pl.BlockSpec(memory_space=pl.ANY)


def shaped(shape, dtype):
    return jax.ShapeDtypeStruct(shape, dtype)


def params():
    return pltpu.CompilerParams(
        dimension_semantics=("arbitrary",), vmem_limit_bytes=VMEM_LIMIT
    )


def call_pack(shards, matrices, vectors, valid):
    r = 512 // shards
    operands = [*matrices, *[v[None] for v in vectors], valid]
    mixer, branch = (2 * r + 16, 256), (4 * r + r // 2, 256)
    return pl.pallas_call(
        functools.partial(pack, shards),
        grid=(1,),
        in_specs=[whole(v.shape) for v in operands],
        out_specs=[whole(mixer), whole(branch)],
        out_shape=[shaped(mixer, BF16), shaped(branch, BF16)],
        compiler_params=params(),
        cost_estimate=COST,
        name="pack",
    )(*operands)


def call_forward(quad, shards, segments, x, operands, earlier):
    length = x.shape[0]
    chunks = length // CHUNK
    wide = pl.BlockSpec((CHUNK, 512), lambda c, *_: (c, 0))
    tile = pl.BlockSpec((CHUNK, QUAD), lambda c, *_: (c, 0))
    state = pl.BlockSpec((1, QUAD, QUAD), lambda c, *_: (c, 0, 0))
    low = shaped((length, QUAD), BF16)
    states = shaped((chunks, QUAD, QUAD), BF16)
    if quad == 0:
        in_specs = [anywhere(), anywhere()]
        out_specs = [whole((4, 512, 512)), whole((8, 512)), whole((8, 2048)), whole((8, 128))]
        out_shape = [shaped((4, 512, 512), BF16), shaped((8, 512), F32)]
        out_shape += [shaped((8, 2048), F32), shaped((8, 128), F32)]
        first = [pltpu.VMEM((4, shards, 16, 256), BF16)]
        last = [pltpu.SemaphoreType.DMA((2,))]
    else:
        in_specs = [pl.BlockSpec((4, 512, QUAD), lambda c, *_: (0, 0, 1)), whole((8, 512))]
        out_specs, out_shape, first, last = [], [], [], []
    grid_spec = pltpu.PrefetchScalarGridSpec(
        num_scalar_prefetch=1,
        grid=(chunks,),
        in_specs=[wide, pl.BlockSpec((1, CHUNK), lambda c, *_: (0, c)), *in_specs]
        + [anywhere()] * len(earlier),
        out_specs=[tile] * 8 + [state] * 2 + out_specs,
        scratch_shapes=first
        + [
            pltpu.VMEM((QUAD, QUAD), F32),
            pltpu.VMEM((QUAD, QUAD), F32),
            pltpu.VMEM((8, QUAD), F32),
        ]
        + last,
    )
    return pl.pallas_call(
        functools.partial(
            ordered,
            functools.partial(attention_forward, quad, shards),
            3 + len(operands),
            len(earlier),
        ),
        grid_spec=grid_spec,
        out_shape=[low] * 6 + [shaped((length, QUAD), F32), low, states, states]
        + out_shape,
        compiler_params=params(),
        cost_estimate=COST,
        name=f"attention_forward_{quad}",
    )(segments, x, segments, *operands, *earlier)


def call_feed_forward(shards, reps, tokens, *operands):
    length = operands[0].shape[0]
    chunks = length // ROWS
    r = 512 // shards
    tile = lambda width: pl.BlockSpec((ROWS, width), lambda c: (c, 0))
    payload = (reps, shards, branch_rows(shards, reps)[0], 256)
    return pl.pallas_call(
        functools.partial(feed_forward, shards, tokens),
        grid=(chunks,),
        in_specs=[
            tile(512),
            tile(QUAD),
            tile(QUAD),
            tile(512),
            pl.BlockSpec((1, ROWS), lambda c: (0, c)),
            whole((8, 512)),
            whole((8, 2048)),
            whole((8, 128)),
            anywhere(),
            anywhere(),
        ],
        out_specs=[tile(512)] * 3 + [whole(payload)] * 2,
        out_shape=[
            shaped((length, 512), BF16),
            shaped((length, 512), F32),
            shaped((length, 512), BF16),
            *[shaped(payload, BF16)] * 2,
        ],
        scratch_shapes=[
            pltpu.VMEM((2 * shards, r // 2, 512), BF16),
            pltpu.VMEM((4, 512, 512), BF16),
            pltpu.VMEM((2048, 512), BF16),
            pltpu.VMEM((ROWS, 2048), BF16),
            pltpu.VMEM((512, 512), F32),
            pltpu.VMEM((4, 512, 512), F32),
            pltpu.VMEM((2048, 512), F32),
            pltpu.VMEM((8, 512), F32),
            pltpu.VMEM((8, 2048), F32),
            pltpu.VMEM((8, 128), F32),
            pltpu.SemaphoreType.DMA((3,)),
        ],
        compiler_params=params(),
        cost_estimate=COST,
        name="feed_forward",
    )(*operands)


def call_backward(quad, shards, segments, x, *operands, extra, earlier):
    length = x.shape[0]
    chunks = length // CHUNK
    r = 512 // shards
    last = quad == 1
    back = lambda c: chunks - 1 - c
    wide = pl.BlockSpec((CHUNK, 512), lambda c, *_: (back(c), 0))
    own = pl.BlockSpec((CHUNK, QUAD), lambda c, *_: (back(c), 0))
    tile = pl.BlockSpec((CHUNK, QUAD), lambda c, *_: (back(c), quad))
    state = pl.BlockSpec((1, QUAD, QUAD), lambda c, *_: (back(c), 0, 0))
    payload = (2, 2, shards // 2, 2 * r + 16, 128)
    grid_spec = pltpu.PrefetchScalarGridSpec(
        num_scalar_prefetch=1,
        grid=(chunks,),
        in_specs=[
            wide,
            pl.BlockSpec((1, CHUNK), lambda c, *_: (0, back(c))),
            *[own] * 7,
            tile,
            *[state] * 2,
            pl.BlockSpec((4, 512, QUAD), lambda c, *_: (0, 0, quad)),
            whole((8, 512)),
            *[wide] * len(extra),
            *[anywhere()] * len(earlier),
        ],
        out_specs=[wide, whole(payload), whole(payload)],
        scratch_shapes=[
            pltpu.VMEM((QUAD, QUAD), F32),
            pltpu.VMEM((QUAD, QUAD), F32),
            pltpu.VMEM((8, QUAD), F32),
            pltpu.VMEM((512, 4 * QUAD), F32),
            pltpu.VMEM((8, 512), F32),
        ],
    )
    return pl.pallas_call(
        functools.partial(
            ordered,
            functools.partial(attention_backward, last, shards),
            3 + len(operands) + len(extra),
            len(earlier),
        ),
        grid_spec=grid_spec,
        out_shape=[
            shaped((length, 512), F32),
            shaped(payload, BF16),
            shaped(payload, BF16),
        ],
        compiler_params=params(),
        cost_estimate=COST,
        name=f"attention_backward_{quad}",
    )(segments, x, segments, *operands, *extra, *earlier)


def swap(value, axis, bit):
    n = lax.axis_size(axis)
    return lax.ppermute(value, axis, [(i, i ^ bit) for i in range(n)])


def bit_groups(shards):
    bits = shards.bit_length() - 1
    return [(low, min(2, bits - low)) for low in range(1, bits, 2)]


def branch_rows(shards, reps):
    r = 512 // shards
    piece = -(-(9 * r + 16) // (16 * reps)) * 16
    names = [("contract", 4 * r)] + [(b, r) for b in range(4)] + [("output", r), ("vectors", 16)]
    rows, at = [], 0
    for name, height in names + [("none", piece * reps - 9 * r - 16)]:
        done = 0
        while done < height:
            part, offset = divmod(at, piece)
            size = min(height - done, piece - offset)
            rows.append((name, done, part, offset, size))
            done += size
            at += size
    return piece, rows


def add_arrived(shards, *refs):
    source, target = refs[0], refs[-1]
    for half in range(2):
        total = 0.0
        for rep in range(half, source.shape[0], 2):
            for s in range(shards):
                total = total + source[rep, s].astype(F32)
        target[half] = total.astype(BF16)


def call_add_arrived(shards, arrived, *others):
    reps, _, piece, width = arrived.shape
    return pl.pallas_call(
        functools.partial(add_arrived, shards),
        in_specs=[pl.BlockSpec(memory_space=pltpu.VMEM)] + [anywhere()] * len(others),
        out_specs=pl.BlockSpec(memory_space=pltpu.VMEM),
        out_shape=shaped((2, piece, width), BF16),
        compiler_params=pltpu.CompilerParams(vmem_limit_bytes=VMEM_LIMIT),
        cost_estimate=COST,
        name="add_arrived",
    )(arrived, *others)


def zero_of(arrays):
    return sum(array[(0,) * array.ndim] for array in arrays) * jnp.zeros((), BF16)


def after(value, *others):
    return lax.optimization_barrier((value, *others))[0]


def quarters(refs):
    _, core, cross = place()

    def quarter(rows, half, third):
        parts = [ref[rows, :] for ref in refs]
        near = jnp.where(core == half, parts[0], parts[1])
        far = jnp.where(core == half, parts[2], parts[3])
        return jnp.where(cross == third, near, far).astype(F32)

    def both(rows, third):
        return jnp.concatenate([quarter(rows, half, third) for half in range(2)], axis=1)

    return both


def assemble_branch(shards, count_ref, *refs):
    held = refs[-1]
    reps = held.shape[0]
    me = lax.axis_index("rep")
    for a in range(reps):
        held[me ^ a] = refs[a][...]
    contract_ref, expand_ref, output_ref, bias_1_ref, bias_2_ref, gain_ref, shift_ref, loss_ref = (
        refs[reps:-1]
    )
    r = 512 // shards
    _, rows = branch_rows(shards, reps)
    vectors = []
    for name, done, part, offset, size in rows:
        value = jnp.concatenate(
            [held[part, half, offset : offset + size, :] for half in range(2)], axis=1
        ).astype(F32)
        if name == "contract":
            contract_ref[done : done + size, :] = value
        elif name == "output":
            output_ref[done : done + size, :] = value
        elif name == "vectors":
            vectors.append(value[:, :256])
        elif name != "none":
            expand_ref[done : done + size, name * 512 : (name + 1) * 512] = value
    vectors = vectors[0] if len(vectors) == 1 else jnp.concatenate(vectors, axis=0)
    bias_1_ref[...] = vectors[8:9, : 4 * r]
    gain_ref[...] = vectors[0:1, :r]
    shift_ref[...] = vectors[1:2, :r]
    bias_2_ref[...] = vectors[2:3, :r]
    lane = lax.broadcasted_iota(jnp.int32, (1, 128), 1)
    power = jnp.zeros((1, 128), F32)
    for k in range(LOSS_DIGITS):
        power = jnp.where(lane == k, 8.0 ** (k - LOSS_ZERO), power)
    total = jnp.sum(vectors[0:1, 128:256] * power, axis=1, keepdims=True)
    count = 256.0 * count_ref[6:7, 0:1] + count_ref[6:7, 1:2]
    loss_ref[...] = total / (2.0 * count)


def assemble_mixer(shards, *refs):
    both = quarters(refs[:4])
    gain_ref, shift_ref = refs[8:]
    r = 512 // shards
    for m, ref in enumerate(refs[4:8]):
        for quad in range(2):
            at = quad * (2 * r + 16) + (m % 2) * r
            ref[:, quad * 256 : (quad + 1) * 256] = both(slice(at, at + r), m // 2)
    vectors = both(slice(4 * r + 16, 4 * r + 32), 0)
    gain_ref[...] = vectors[0:1, :r]
    shift_ref[...] = vectors[1:2, :r]


def assemble(body, shards, parts, shapes, scratch=()):
    return pl.pallas_call(
        functools.partial(body, shards),
        in_specs=[pl.BlockSpec(memory_space=pltpu.VMEM)] * len(parts),
        out_specs=[pl.BlockSpec(memory_space=pltpu.VMEM)] * len(shapes),
        out_shape=[shaped(shape, F32) for shape in shapes],
        scratch_shapes=list(scratch),
        cost_estimate=COST,
        name="assemble",
    )(*parts)


def add_low(*parts):
    return sum(part.astype(F32) for part in parts).astype(BF16)


def local(
    inputs,
    segments,
    valid_mask,
    teacher,
    query_weight,
    key_weight,
    value_weight,
    control_weight,
    output_weight,
    gain_first,
    shift_first,
    expand_weight,
    expand_bias,
    contract_weight,
    contract_bias,
    gain_second,
    shift_second,
):
    _, length, width = inputs.shape
    shards, reps = lax.axis_size("shard"), lax.axis_size("rep")
    r = width // shards
    core = lax.axis_index("rep") % 2
    cross = (lax.axis_index("rep") // 2) % 2
    groups = bit_groups(shards)

    matrices = (query_weight, key_weight, value_weight, control_weight, output_weight)
    matrices += (expand_weight, contract_weight)
    biases = (gain_first, shift_first, gain_second, shift_second, contract_bias, expand_bias)
    mixer, branch = call_pack(shards, matrices, biases, valid_mask)

    def along_z(payload):
        held = [payload[None]]
        for low, bits in groups:
            if len(held) > 1:
                held = [jnp.concatenate(held, axis=0)]
            held += [swap(held[0], "shard", a << low) for a in range(1, 1 << bits)]
        return held

    def halves(held):
        if len(held) == 4:
            return jnp.concatenate(held[:2], axis=0), jnp.concatenate(held[2:], axis=0)
        joined = jnp.concatenate(held, axis=0)
        half = joined.shape[0] // 2
        return joined[:half], joined[half:]

    def step_one(first, second):
        return swap(first, "shard", 1), swap(second, "rep", 2)

    def join(first, second, arrived):
        return jnp.concatenate([first, arrived[0]]), jnp.concatenate([second, arrived[1]])

    def step_two(first, second):
        return swap(first, "rep", 2), swap(second, "shard", 1)

    first, second = halves(along_z(mixer))
    first, second = join(first, second, step_one(first, second))
    arrived = step_two(first, second)
    held_b = along_z(branch)
    first_b, second_b = halves(held_b)
    pending = step_one(first_b, second_b)
    mine_a = jnp.concatenate([first, arrived[0] + zero_of(held_b[1:]), second, arrived[1]])
    theirs_a = swap(mine_a, "rep", 1)

    x = inputs.reshape(length, width)
    forward_0 = call_forward(
        0, shards, segments, x, (mine_a, theirs_a), (first_b, second_b)
    )
    weights, vectors, bias, count = forward_0[10:]
    bit = 4
    while bit < reps:
        count = count + swap(count, "rep", bit)
        bit *= 2
    pending = after(pending, forward_0[7])
    first_b, second_b = join(first_b, second_b, pending)
    pending = step_two(first_b, second_b)
    forward_1 = call_forward(1, shards, segments, x, (weights, vectors), (first_b, second_b))
    pending = after(pending, forward_1[7])
    mine_b = jnp.concatenate([first_b, pending[0], second_b, pending[1]])
    theirs_b = swap(mine_b, "rep", 1)
    mixed = (forward_0[7], forward_1[7])

    layer_out, grad_hidden, grad_mix, keep_f, send_f = call_feed_forward(
        shards,
        reps,
        float(length * shards * reps),
        x,
        *mixed,
        teacher.reshape(length, width),
        valid_mask,
        vectors,
        bias,
        count,
        mine_b,
        theirs_b,
    )

    def split(parts):
        return add_low(*(part[0] for part in parts)), add_low(*(part[1] for part in parts))

    def cross_first(parts):
        keep, send = split(parts)
        return keep, swap(send, "rep", 2)

    def row_first(parts):
        keep, send = split(parts)
        return keep, swap(send, "shard", 1)

    def z_stage(parts_list):
        current = parts_list
        for low, bits in reversed(groups):
            span = 1 << (low - 1)
            pieces = [
                jnp.concatenate(
                    [
                        add_low(*(part[a * span : (a + 1) * span] for part in parts))
                        for parts in current
                    ],
                    axis=1,
                )
                for a in range(1 << bits)
            ]
            arrived = [swap(pieces[a], "shard", a << low) for a in range(1, 1 << bits)]
            current = [(pieces[0], *arrived)]
        return current[0]

    def finish(parts):
        total = add_low(*(part[0] for part in parts))
        bit = 4
        while bit < reps:
            total = add_low(total, swap(total, "rep", bit))
            bit *= 2
        return [total] + [swap(total, "rep", a) for a in range(1, 4)]

    def back(quad, saved, extra, earlier):
        return call_backward(
            quad,
            shards,
            segments,
            x,
            *saved[:7],
            grad_mix,
            *saved[8:10],
            weights,
            vectors,
            extra=extra,
            earlier=earlier,
        )

    summed = add_low(keep_f, swap(send_f, "rep", 1))
    every = summed.reshape(reps * shards, *summed.shape[2:])
    arrived_f = lax.all_to_all(every, ("rep", "shard"), 0, 0).reshape(summed.shape)
    part, keep_0, send_0 = back(0, forward_0, (), (every,))
    late_0 = swap(send_0, "rep", 1)
    grad_inputs, keep_1, send_1 = back(1, forward_1, (part, grad_hidden), ())
    late_1 = swap(send_1, "rep", 1)
    parts_0, parts_1 = row_first((keep_0, late_0)), cross_first((keep_1, late_1))
    parts_0, parts_1 = cross_first(parts_0), row_first(parts_1)
    q_pieces = z_stage([parts_0, parts_1])
    total_f = call_add_arrived(shards, arrived_f, q_pieces[0])
    parts_f = [total_f] + [swap(total_f, "rep", a) for a in range(1, reps)]
    parts_q = finish(q_pieces)
    grad_contract, grad_expand, grad_output, bias_1, bias_2, gain_2, shift_2, loss = assemble(
        assemble_branch,
        shards,
        [count, *parts_f],
        [(4 * r, 512), (r, 2048), (r, 512), (1, 4 * r), (1, r), (1, r), (1, r), (1, 1)],
        [pltpu.VMEM((reps, *total_f.shape), BF16)],
    )
    *mats, gain_1, shift_1 = assemble(
        assemble_mixer, shards, parts_q, [(r, 512)] * 4 + [(1, r)] * 2
    )
    return (
        layer_out.reshape(inputs.shape),
        grad_inputs.reshape(inputs.shape),
        loss.reshape(()),
        *mats,
        grad_output,
        gain_1.reshape(r),
        shift_1.reshape(r),
        grad_expand,
        bias_1.reshape(4 * r),
        grad_contract,
        bias_2.reshape(r),
        gain_2.reshape(r),
        shift_2.reshape(r),
    )


def solution(mesh):
    every = P(("rep", "shard"), None, None)
    every_row = P(("rep", "shard"), None)
    matrix, vector = P("shard", None), P("shard")
    in_specs = (
        every,
        every_row,
        every_row,
        every,
        *[matrix] * 5,
        *[vector] * 2,
        matrix,
        vector,
        matrix,
        *[vector] * 3,
    )
    out_specs = (
        every,
        every,
        P(),
        *[matrix] * 5,
        *[vector] * 2,
        matrix,
        vector,
        matrix,
        *[vector] * 3,
    )
    return jax.shard_map(local, mesh=mesh, in_specs=in_specs, out_specs=out_specs, check_vma=False)
```

```python
import functools

import jax
import jax.numpy as jnp
from jax import lax
from jax.experimental import pallas as pl
from jax.experimental.pallas import tpu as pltpu
from jax.sharding import PartitionSpec as P

HEADS = 8
EPSILON = 1e-05
CHUNK = 256
SUB = 128
BACK = 512
ROWS = 512
QUAD = 256
F32 = jnp.float32
BF16 = jnp.bfloat16
VMEM_LIMIT = 60 << 20
LOSS_DIGITS = 30
LOSS_ZERO = 10
COST = pl.CostEstimate(flops=1000, bytes_accessed=1000, transcendentals=0)


def ordered(kernel, at, count, *refs):
    kernel(*refs[:at], *refs[at + count :])


def place():
    rep = lax.axis_index("rep")
    return lax.axis_index("shard"), rep % 2, (rep // 2) % 2


def slots_of(shards):
    ways = shards // 2
    low, high = range(ways // 2), range(ways // 2, ways)
    first = [(z, y, x) for x in (0, 1) for y in (0, 1) for z in low]
    second = [(z, y, x) for y in (0, 1) for x in (0, 1) for z in high]
    return first + second


def nn(left, right):
    return jnp.dot(left, right, preferred_element_type=F32)


def nt(left, right):
    return lax.dot_general(left, right, (((1,), (1,)), ((), ())), preferred_element_type=F32)


def tn(left, right):
    return lax.dot_general(left, right, (((0,), (0,)), ((), ())), preferred_element_type=F32)


def head_lanes():
    lane = lax.broadcasted_iota(jnp.int32, (1, QUAD), 1) // 64
    return [jnp.where(lane == h, 1.0, 0.0).astype(BF16) for h in range(4)]


def block_diagonal():
    rows = lax.broadcasted_iota(jnp.int32, (QUAD, QUAD), 0) // 64
    columns = lax.broadcasted_iota(jnp.int32, (QUAD, QUAD), 1) // 64
    return jnp.where(rows == columns, 1.0, 0.0)


def as_column(row, width):
    tile = jnp.broadcast_to(row, (128, row.shape[1])).T
    return jnp.concatenate([tile] * (width // 128), axis=1)


def causal_mask(column, row):
    at = lax.broadcasted_iota(jnp.int32, (SUB, SUB), 0)
    source = lax.broadcasted_iota(jnp.int32, (SUB, SUB), 1)
    return jnp.where((column[:, :SUB] == row) & (source <= at), 1.0, 0.0).astype(BF16)


def causal_mask_transposed(column, row):
    source = lax.broadcasted_iota(jnp.int32, (SUB, SUB), 0)
    at = lax.broadcasted_iota(jnp.int32, (SUB, SUB), 1)
    return jnp.where((column[:, :SUB] == row) & (source <= at), 1.0, 0.0).astype(BF16)


def head_stack(values):
    return jnp.concatenate([values * lanes for lanes in head_lanes()], axis=0)


def four_times(mask):
    return jnp.concatenate([mask] * 4, axis=1)


def per_head(values, reduce, fill):
    lane = lax.broadcasted_iota(jnp.int32, (1, 128), 1)
    first = lane < 64
    tiles = []
    for tile in range(values.shape[1] // 128):
        part = values[:, tile * 128 : (tile + 1) * 128]
        one = reduce(jnp.where(first, part, fill), axis=-1, keepdims=True)
        two = reduce(jnp.where(first, fill, part), axis=-1, keepdims=True)
        tiles.append(jnp.where(first, one, two))
    return jnp.concatenate(tiles, axis=1)


def standardise(values):
    mean = jnp.mean(values, axis=-1, keepdims=True)
    centred = values - mean
    variance = jnp.mean(centred * centred, axis=-1, keepdims=True)
    scale = lax.rsqrt(variance + EPSILON)
    return centred * scale, scale


def norm_backward(gradient, gain, normal, scale):
    upstream = gradient * gain
    one = jnp.mean(upstream, axis=-1, keepdims=True)
    two = jnp.mean(upstream * normal, axis=-1, keepdims=True)
    return (upstream - one - normal * two) * scale


def spread(rows, shards):
    width = 512 // shards
    lane = lax.broadcasted_iota(jnp.int32, (8, 128), 1)
    tiles = [None] * 4
    for s in range(shards):
        tile, offset = divmod(s * width, 128)
        moved = pltpu.roll(rows[s], offset, 1) if offset else rows[s]
        inside = (lane >= offset) & (lane < offset + width)
        tiles[tile] = jnp.where(inside, moved, 0.0 if tiles[tile] is None else tiles[tile])
    return jnp.concatenate(tiles, axis=1)


def digits_of(value):
    lane = lax.broadcasted_iota(jnp.int32, (8, 128), 1)
    scale = jnp.zeros((8, 128), F32)
    for k in range(LOSS_DIGITS):
        scale = jnp.where(lane == k, 8.0 ** (LOSS_ZERO - k), scale)
    shifted = value * scale
    return jnp.floor(shifted) - 8.0 * jnp.floor(shifted * 0.125)


def piece_of(vectors, s, width):
    tile, offset = divmod(s * width, 128)
    part = vectors[:, tile * 128 : (tile + 1) * 128]
    return pltpu.roll(part, 128 - offset, 1) if offset else part


def pack(shards, *refs):
    query, key, value, control, output, expand, contract = refs[:7]
    gain_1, shift_1, gain_2, shift_2, bias_2, bias_1, valid = refs[7:14]
    mixer_ref, branch_ref = refs[14:]
    r = 512 // shards
    _, core, cross = place()

    def write(half, third):
        at = slice(half * 256, half * 256 + 256)
        for m, ref in enumerate(((query, key), (value, control))[third]):
            mixer_ref[m * r : (m + 1) * r] = ref[:, at]
        if third == 0:
            for b in range(4):
                part = expand[:, b * 512 + half * 256 : b * 512 + half * 256 + 256]
                branch_ref[b * r : (b + 1) * r] = part
        else:
            branch_ref[0 : 4 * r] = contract[:, at]
        branch_ref[4 * r : 4 * r + r // 2] = output[third * (r // 2) : (third + 1) * (r // 2), at]

    for half in range(2):
        for third in range(2):
            pl.when((core == half) & (cross == third))(functools.partial(write, half, third))

    row = lax.broadcasted_iota(jnp.int32, (16, 256), 0)
    lane = lax.broadcasted_iota(jnp.int32, (16, 256), 1)
    block = jnp.zeros((16, 256), F32)
    for k, ref in ((0, gain_1), (1, shift_1), (2, gain_2), (3, shift_2), (4, bias_2), (8, bias_1)):
        part = ref[...].astype(F32)
        width = part.shape[1]
        if width < 256:
            part = jnp.concatenate([part, jnp.zeros((1, 256 - width), F32)], axis=1)
        block = jnp.where(row == k, part, block)
    count = jnp.sum(valid[...].astype(F32))
    high = jnp.floor(count / 256.0)
    block = jnp.where((row == 6) & (lane == 0), high, block)
    block = jnp.where((row == 6) & (lane == 1), count - 256.0 * high, block)
    mixer_ref[2 * r : 2 * r + 16] = block.astype(BF16)


def attention_forward(quad, shards, seg_s, x_ref, seg_ref, *refs):
    step = pl.program_id(0)
    r = 512 // shards
    at = slice(quad * QUAD, (quad + 1) * QUAD)
    if quad == 0:
        mine_ref, theirs_ref = refs[:2]
        q_ref, k_ref, v_ref, e_ref, p_ref, s_ref, rz_ref, mix_ref, one_ref, two_ref = refs[2:12]
        w_ref, vec_ref, eb_ref, count_ref = refs[12:16]
        held, first_state, second_state, total_state, sems = refs[16:]
        weight = lambda m: w_ref[m, :, at]
    else:
        w_ref, vec_ref = refs[:2]
        q_ref, k_ref, v_ref, e_ref, p_ref, s_ref, rz_ref, mix_ref, one_ref, two_ref = refs[2:12]
        first_state, second_state, total_state = refs[12:]
        weight = lambda m: w_ref[m]

    @pl.when(step == 0)
    def _():
        first_state[...] = jnp.zeros_like(first_state)
        second_state[...] = jnp.zeros_like(second_state)
        total_state[...] = jnp.zeros_like(total_state)

    def assemble():
        me, core, cross = place()
        for half, source in enumerate((mine_ref, theirs_ref)):
            column = pl.multiple_of(((core + half) % 2) * 256, 256)
            for slot, (z, y, x) in enumerate(slots_of(shards)):
                owner = me ^ (2 * z + y)
                third = cross ^ x
                for m in range(2):
                    pltpu.make_async_copy(
                        source.at[slot, pl.ds(m * r, r)],
                        w_ref.at[
                            2 * third + m,
                            pl.ds(pl.multiple_of(owner * r, r), r),
                            pl.ds(column, 256),
                        ],
                        sems.at[0],
                    ).start()
                pltpu.make_async_copy(
                    source.at[slot, pl.ds(2 * r, 16)], held.at[2 * half + x, owner], sems.at[1]
                ).start()
        pltpu.make_async_copy(held, held, sems.at[1]).wait()
        own = [held[0, s].astype(F32) for s in range(shards)]
        count = sum(part[:8, :128] for part in own)
        for k in range(1, 4):
            count += jnp.sum(held[k, :, :8, :128].astype(F32), axis=0)
        count_ref[...] = count
        vec_ref[...] = spread([part[:8, :128] for part in own], shards)
        width = 2048 // shards
        lane = lax.broadcasted_iota(jnp.int32, (8, 128), 1)
        if width >= 128:
            for s in range(shards):
                eb_ref[:, s * width : (s + 1) * width] = own[s][8:16, :width]
        else:
            for tile in range(16):
                built = jnp.zeros((8, 128), F32)
                for k in range(128 // width):
                    part = own[tile * (128 // width) + k][8:16, :128]
                    moved = pltpu.roll(part, k * width, 1) if k else part
                    built = jnp.where((lane >= k * width) & (lane < (k + 1) * width), moved, built)
                eb_ref[:, tile * 128 : (tile + 1) * 128] = built
        pltpu.make_async_copy(w_ref, w_ref, sems.at[0]).wait()

    if quad == 0:
        pl.when(step == 0)(assemble)

    row_all = seg_ref[...].astype(F32)
    diagonal = block_diagonal()
    normal, _ = standardise(x_ref[...].astype(F32))
    normed = (normal * vec_ref[0:1, :] + vec_ref[1:2, :]).astype(BF16)
    q_ref[...] = nn(normed, weight(0)).astype(BF16)
    k_ref[...] = nn(normed, weight(1)).astype(BF16)
    v_ref[...] = nn(normed, weight(2)).astype(BF16)
    e_ref[...] = jnp.exp(nn(normed, weight(3))).astype(BF16)
    subs = range(CHUNK // SUB)
    spans = [slice(sub * SUB, (sub + 1) * SUB) for sub in subs]
    q, k, v, e = ([ref[rows] for rows in spans] for ref in (q_ref, k_ref, v_ref, e_ref))
    causal, causal_4, enters, one, two, totals = [], [], [], [], [], []
    first, second, running = first_state[...], second_state[...], total_state[0:1, :]
    for sub in subs:
        start = step * CHUNK + sub * SUB
        segment_last = seg_s[0, start + SUB - 1]
        segment_before = jnp.where(start == 0, -1, seg_s[0, jnp.maximum(start - 1, 0)])
        keep = jnp.where(segment_last == segment_before, 1.0, 0.0)
        row = row_all[:, spans[sub]]
        column = as_column(row, QUAD)
        causal.append(causal_mask(column, row))
        causal_4.append(four_times(causal[sub]))
        enters.append(jnp.where(column == segment_before.astype(F32), 1.0, 0.0))
        leaves = jnp.where(column == segment_last.astype(F32), 1.0, 0.0).astype(BF16)
        one.append(first.astype(BF16))
        two.append(second.astype(BF16))
        one_ref[sub] = one[sub]
        two_ref[sub] = two[sub]
        totals.append(nn(causal[sub], e[sub]) + enters[sub] * running)
        running = totals[sub][SUB - 1 : SUB, :]
        first = keep * first + diagonal * tn(k[sub] * leaves, e[sub])
        second = keep * second + diagonal * tn(e[sub] * leaves, v[sub])
    first_state[...] = first
    second_state[...] = second
    total_state[0:1, :] = running

    def each(function, *lists):
        return [function(*values) for values in zip(*lists)]

    def store(ref, values):
        for rows, value in zip(spans, values):
            ref[rows] = value

    inverse = each(lambda a: 1.0 / a, totals)
    store(rz_ref, inverse)
    e_stack = each(head_stack, e)
    scores = each(lambda a, b, c: nt(a, head_stack(b)).astype(BF16) * c, q, k, causal_4)
    gathered = each(
        lambda a, b, c, d, f: nn(a, b) + c * nn(d, f), scores, e_stack, enters, q, one
    )
    slot_scores = each(lambda a, b: a * (b * 0.125), gathered, inverse)
    raised = each(lambda a: jnp.exp(a - per_head(a, jnp.max, -jnp.inf)), slot_scores)
    shares = each(lambda a: a / per_head(a, jnp.sum, 0.0), raised)
    scaled = each(lambda a, b: (a * b).astype(BF16), shares, inverse)
    mixing = each(lambda a, b, c: nt(a, b).astype(BF16) * c, scaled, e_stack, causal_4)
    mixed = each(
        lambda a, b, c, d, f: nn(a, head_stack(b)) + c * nn(d, f), mixing, v, enters, scaled, two
    )
    store(s_ref, each(lambda a: a.astype(BF16), slot_scores))
    store(p_ref, each(lambda a: a.astype(BF16), shares))
    store(mix_ref, each(lambda a: a.astype(BF16), mixed))


def feed_forward(
    shards,
    tokens,
    x_ref,
    mix_0_ref,
    mix_1_ref,
    teacher_ref,
    valid_ref,
    vec_ref,
    eb_ref,
    count_ref,
    mine_ref,
    theirs_ref,
    out_ref,
    hidden_ref,
    grad_mix_ref,
    keep_ref,
    send_ref,
    wo,
    we,
    wc,
    act,
    d_wo,
    d_we,
    d_wc,
    d_vec,
    d_eb,
    loss_ref,
    sems,
):
    step = pl.program_id(0)
    r = 512 // shards
    me, core, cross = place()

    @pl.when(step == 0)
    def _():
        loss_ref[...] = jnp.zeros_like(loss_ref)
        for half, source in enumerate((mine_ref, theirs_ref)):
            column = pl.multiple_of(((core + half) % 2) * 256, 256)
            for slot, (z, y, x) in enumerate(slots_of(shards)):
                owner = me ^ (2 * z + y)
                third = cross ^ x
                pltpu.make_async_copy(
                    source.at[slot, pl.ds(4 * r, r // 2)],
                    wo.at[2 * owner + third, :, pl.ds(column, 256)],
                    sems.at[0],
                ).start()

                def expansion():
                    for b in range(4):
                        pltpu.make_async_copy(
                            source.at[slot, pl.ds(b * r, r)],
                            we.at[
                                b, pl.ds(pl.multiple_of(owner * r, r), r), pl.ds(column, 256)
                            ],
                            sems.at[1],
                        ).start()

                def contraction():
                    pltpu.make_async_copy(
                        source.at[slot, pl.ds(0, 4 * r)],
                        wc.at[
                            pl.ds(pl.multiple_of(owner * 4 * r, 4 * r), 4 * r), pl.ds(column, 256)
                        ],
                        sems.at[2],
                    ).start()

                pl.when(third == 0)(expansion)
                pl.when(third == 1)(contraction)
        for ref in (d_wo, d_we, d_wc, d_vec, d_eb):
            ref[...] = jnp.zeros_like(ref)
        pltpu.make_async_copy(wo, wo, sems.at[0]).wait()

    gain, shift, bias = vec_ref[2:3, :], vec_ref[3:4, :], vec_ref[4:5, :]
    weight_out = wo[...].reshape(512, 512)
    mixed = jnp.concatenate([mix_0_ref[...], mix_1_ref[...]], axis=1)
    hidden = x_ref[...].astype(F32) + nn(mixed, weight_out)
    normal, scale = standardise(hidden)
    normed = (normal * gain + shift).astype(BF16)
    pl.when(step == 0)(lambda: pltpu.make_async_copy(we, we, sems.at[1]).wait())
    for b in range(4):
        at = slice(b * 512, (b + 1) * 512)
        before = nn(normed, we[b]) + eb_ref[0:1, at]
        act[:, at] = jnp.maximum(before, 0.0).astype(BF16)
    pl.when(step == 0)(lambda: pltpu.make_async_copy(wc, wc, sems.at[2]).wait())
    result = hidden + (nn(act[...], wc[...]) + bias)
    out_ref[...] = result.astype(BF16)
    valid = as_column(valid_ref[...].astype(F32), 512)
    error = result - teacher_ref[...].astype(F32)
    masked = valid * error
    loss_ref[...] += jnp.sum(masked * error)
    count = 256.0 * count_ref[6:7, 0:1] + count_ref[6:7, 1:2]
    grad_result = masked * (tokens / count)
    low = grad_result.astype(BF16)
    d_normed = None
    for b in range(4):
        at = slice(b * 512, (b + 1) * 512)
        active = act[:, at]
        d_wc[at, :] += tn(active, low)
        grad = jnp.where(active > 0, nt(low, wc[at, :]), 0.0)
        grad = grad.astype(BF16)
        d_we[b] += tn(normed, grad)
        d_eb[0:1, at] += jnp.sum(grad.astype(F32), axis=0, keepdims=True)
        part = nt(grad, we[b])
        d_normed = part if d_normed is None else d_normed + part
    d_vec[0:1, :] += jnp.sum(d_normed * normal, axis=0, keepdims=True)
    d_vec[1:2, :] += jnp.sum(d_normed, axis=0, keepdims=True)
    d_vec[2:3, :] += jnp.sum(low.astype(F32), axis=0, keepdims=True)
    grad_hidden = grad_result + norm_backward(d_normed, gain, normal, scale)
    hidden_ref[...] = grad_hidden
    grad_low = grad_hidden.astype(BF16)
    d_wo[...] += tn(mixed, grad_low)
    grad_mix_ref[...] = nt(grad_low, weight_out).astype(BF16)

    @pl.when(step == pl.num_programs(0) - 1)
    def _():
        width = 2048 // shards
        digits = digits_of(loss_ref[...])

        _, rows = branch_rows(shards, keep_ref.shape[0])

        def write(ref, at):
            for s in range(shards):
                top = jnp.concatenate([piece_of(d_vec[...], s, r), digits], axis=1)
                if width >= 128:
                    low_rows = d_eb[:, s * width : (s + 1) * width]
                else:
                    low_rows = piece_of(d_eb[...], s, width)
                if low_rows.shape[1] < 256:
                    pad = jnp.zeros((8, 256 - low_rows.shape[1]), F32)
                    low_rows = jnp.concatenate([low_rows, pad], axis=1)
                both = jnp.concatenate([top, low_rows], axis=0)
                for name, done, part, offset, size in rows:
                    if name == "contract":
                        value = d_wc[s * 4 * r + done : s * 4 * r + done + size, at]
                    elif name == "output":
                        value = d_wo[s * r + done : s * r + done + size, at]
                    elif name == "vectors":
                        value = both[done : done + size]
                    elif name == "none":
                        value = jnp.zeros((size, 256), F32)
                    else:
                        value = d_we[name, s * r + done : s * r + done + size, at]
                    ref[part, s, offset : offset + size, :] = value.astype(BF16)

        left, right = slice(0, 256), slice(256, 512)

        @pl.when(core == 0)
        def _():
            write(keep_ref, left)
            write(send_ref, right)

        @pl.when(core == 1)
        def _():
            write(keep_ref, right)
            write(send_ref, left)


def attention_backward(shards, seg_s, x_ref, seg_ref, *refs):
    sides, refs = (refs[:9], refs[9:18]), refs[18:]
    g_ref, w_ref, vec_ref, hidden_ref, out_ref, keep_ref, send_ref = refs[:7]
    first_state, second_state, total_state, d_w, d_vec = refs[7:]
    step = pl.program_id(0)
    chunks = pl.num_programs(0)
    chunk = chunks - 1 - step
    r = 512 // shards
    me, core, cross = place()

    @pl.when(step == 0)
    def _():
        for ref in (first_state, second_state, total_state, d_w, d_vec):
            ref[...] = jnp.zeros_like(ref)

    length = chunks * BACK
    row_all = seg_ref[...].astype(F32)
    diagonal = block_diagonal()
    found = [[], []]
    for sub in reversed(range(BACK // SUB)):
        rows = slice(sub * SUB, (sub + 1) * SUB)
        start = chunk * BACK + sub * SUB
        segment_first = seg_s[0, start]
        segment_before = jnp.where(start == 0, -1, seg_s[0, jnp.maximum(start - 1, 0)])
        after_at = jnp.minimum(start + SUB, length - 1)
        segment_after = jnp.where(start + SUB == length, -1, seg_s[0, after_at])
        keep = jnp.where(segment_first == segment_after, 1.0, 0.0)
        row = row_all[:, rows]
        column = as_column(row, QUAD)
        causal_4 = four_times(causal_mask(column, row))
        turned = causal_mask_transposed(column, row)
        turned_4 = four_times(turned)
        enters = jnp.where(column == segment_before.astype(F32), 1.0, 0.0)
        goes_on = jnp.where(column == segment_after.astype(F32), 1.0, 0.0)
        opens = jnp.where(column == segment_first.astype(F32), 1.0, 0.0).astype(BF16)

        def both(function, *lists):
            return [function(*values) for values in zip(*lists)]

        q, k, v, e = ([side[n][rows] for side in sides] for n in range(4))
        grad = [g_ref[rows, g * QUAD : (g + 1) * QUAD] for g in range(2)]
        shares = [side[4][rows].astype(F32) for side in sides]
        slot_scores = [side[5][rows].astype(F32) for side in sides]
        inverse = [side[6][rows] for side in sides]
        one = [side[7][sub] for side in sides]
        two = [side[8][sub] for side in sides]
        scaled = both(lambda a, b: a * b, shares, inverse)
        scaled_low = [a.astype(BF16) for a in scaled]
        one_back = [first_state[g].astype(BF16) for g in range(2)]
        two_back = [second_state[g].astype(BF16) for g in range(2)]
        e_stack = both(head_stack, e)

        d_mixing = both(lambda a, b: nt(a, head_stack(b)).astype(BF16) * causal_4, grad, v)
        d_scaled = both(
            lambda a, b, c, d: nn(a, b) + enters * nt(c, d), d_mixing, e_stack, grad, two
        )
        q_stack, grad_stack = both(head_stack, q), both(head_stack, grad)
        scaled_stack = both(head_stack, scaled_low)
        mixing_t = both(lambda a, b: nt(a, b).astype(BF16) * turned_4, e, scaled_stack)
        d_mixing_t = both(lambda a, b: nt(a, b).astype(BF16) * turned_4, v, grad_stack)
        scores_t = both(lambda a, b: nt(a, b).astype(BF16) * turned_4, k, q_stack)
        d_shares = both(lambda a, b: a * b, d_scaled, inverse)
        product = both(lambda a, b: a * b, shares, d_shares)
        d_scores = both(lambda a, b: a - b * per_head(a, jnp.sum, 0.0), product, shares)
        d_low = both(lambda a, b: (a * b * 0.125).astype(BF16), d_scores, inverse)
        d_totals = both(
            lambda a, b, c, d, i: -(a * b + c * d) * i,
            d_scaled,
            scaled,
            d_scores,
            slot_scores,
            inverse,
        )
        d_values = both(
            lambda a, b, c, d: nn(a, b) + goes_on * nn(c, d), mixing_t, grad_stack, e, two_back
        )
        d_slots = both(nn, d_mixing_t, scaled_stack)
        d_low_stack = both(head_stack, d_low)
        d_raw = both(lambda a, b: nt(a, b).astype(BF16) * causal_4, d_low, e_stack)
        d_raw_t = both(lambda a, b: nt(a, b).astype(BF16) * turned_4, e, d_low_stack)
        d_slots = both(lambda a, b, c: a + nn(b, c), d_slots, scores_t, d_low_stack)
        d_queries = both(
            lambda a, b, c, d: nn(a, head_stack(b)) + enters * nt(c, d), d_raw, k, d_low, one
        )
        d_keys = both(
            lambda a, b, c, d: nn(a, b) + goes_on * nt(c, d), d_raw_t, q_stack, e, one_back
        )
        totals_low = [a.astype(BF16) for a in d_totals]
        rest = both(lambda a, b: (a - b.astype(F32)).astype(BF16), d_totals, totals_low)
        sums = [
            nn(turned, totals_low[g]) + nn(turned, rest[g]) + goes_on * total_state[g, 0:1, :]
            for g in range(2)
        ]
        d_slots = both(
            lambda a, b, c, d, f, h: a + goes_on * (nn(b, c) + nt(d, f)) + h,
            d_slots,
            k,
            one_back,
            v,
            two_back,
            sums,
        )
        d_control = both(lambda a, b: a * b.astype(F32), d_slots, e)
        for g in range(2):
            total_state[g, 0:1, :] = sums[g][0:1, :]
            first_state[g] = keep * first_state[g] + diagonal * tn(q[g] * opens, d_low[g])
            second_state[g] = keep * second_state[g] + diagonal * tn(
                scaled_low[g] * opens, grad[g]
            )
            parts = (d_queries[g], d_keys[g], d_values[g], d_control[g])
            found[g].append([part.astype(BF16) for part in parts])
    grads = [
        jnp.concatenate([part[m] for part in reversed(found[g])], axis=0)
        for g in range(2)
        for m in range(4)
    ]

    normal, scale = standardise(x_ref[...].astype(F32))
    gain = vec_ref[0:1, :]
    normed = (normal * gain + vec_ref[1:2, :]).astype(BF16)
    d_w[...] += tn(normed, jnp.concatenate(grads, axis=1))
    d_normed = sum(
        nt(jnp.concatenate([grads[m], grads[4 + m]], axis=1), w_ref[m]) for m in range(4)
    )
    d_vec[0:1, :] += jnp.sum(d_normed * normal, axis=0, keepdims=True)
    d_vec[1:2, :] += jnp.sum(d_normed, axis=0, keepdims=True)
    out_ref[...] = hidden_ref[...] + norm_backward(d_normed, gain, normal, scale)

    @pl.when(step == chunks - 1)
    def _():
        def write(ref, half):
            for s in range(shards):
                y, z = (me ^ s) & 1, (me ^ s) >> 1
                top = piece_of(d_vec[...], s, r)
                both_rows = jnp.concatenate([top, jnp.zeros_like(top)], axis=0).astype(BF16)
                for g in range(2):
                    for m in range(4):
                        x = cross ^ (m // 2)
                        lead = (g, x, y, z) if g else (g, y, x, z)
                        at = (4 * g + m) * QUAD + half * 128
                        part = d_w[s * r : (s + 1) * r, at : at + 128].astype(BF16)
                        ref[(*lead, slice((m % 2) * r, (m % 2 + 1) * r), slice(None))] = part
                    for x in range(2):
                        lead = (g, x, y, z) if g else (g, y, x, z)
                        ref[(*lead, slice(2 * r, 2 * r + 16), slice(None))] = both_rows

        @pl.when(core == 0)
        def _():
            write(keep_ref, 0)
            write(send_ref, 1)

        @pl.when(core == 1)
        def _():
            write(keep_ref, 1)
            write(send_ref, 0)


def whole(shape):
    return pl.BlockSpec(shape, lambda *_: (0,) * len(shape))


def anywhere():
    return pl.BlockSpec(memory_space=pl.ANY)


def shaped(shape, dtype):
    return jax.ShapeDtypeStruct(shape, dtype)


def params():
    return pltpu.CompilerParams(
        dimension_semantics=("arbitrary",), vmem_limit_bytes=VMEM_LIMIT
    )


def call_pack(shards, matrices, vectors, valid):
    r = 512 // shards
    operands = [*matrices, *[v[None] for v in vectors], valid]
    mixer, branch = (2 * r + 16, 256), (4 * r + r // 2, 256)
    return pl.pallas_call(
        functools.partial(pack, shards),
        grid=(1,),
        in_specs=[whole(v.shape) for v in operands],
        out_specs=[whole(mixer), whole(branch)],
        out_shape=[shaped(mixer, BF16), shaped(branch, BF16)],
        compiler_params=params(),
        cost_estimate=COST,
        name="pack",
    )(*operands)


def call_forward(quad, shards, segments, x, operands, earlier):
    length = x.shape[0]
    chunks = length // CHUNK
    wide = pl.BlockSpec((CHUNK, 512), lambda c, *_: (c, 0))
    tile = pl.BlockSpec((CHUNK, QUAD), lambda c, *_: (c, 0))
    state = pl.BlockSpec((CHUNK // SUB, QUAD, QUAD), lambda c, *_: (c, 0, 0))
    low = shaped((length, QUAD), BF16)
    states = shaped((length // SUB, QUAD, QUAD), BF16)
    if quad == 0:
        in_specs = [anywhere(), anywhere()]
        out_specs = [whole((4, 512, 512)), whole((8, 512)), whole((8, 2048)), whole((8, 128))]
        out_shape = [shaped((4, 512, 512), BF16), shaped((8, 512), F32)]
        out_shape += [shaped((8, 2048), F32), shaped((8, 128), F32)]
        first = [pltpu.VMEM((4, shards, 16, 256), BF16)]
        last = [pltpu.SemaphoreType.DMA((2,))]
    else:
        in_specs = [pl.BlockSpec((4, 512, QUAD), lambda c, *_: (0, 0, 1)), whole((8, 512))]
        out_specs, out_shape, first, last = [], [], [], []
    grid_spec = pltpu.PrefetchScalarGridSpec(
        num_scalar_prefetch=1,
        grid=(chunks,),
        in_specs=[wide, pl.BlockSpec((1, CHUNK), lambda c, *_: (0, c)), *in_specs]
        + [anywhere()] * len(earlier),
        out_specs=[tile] * 8 + [state] * 2 + out_specs,
        scratch_shapes=first
        + [
            pltpu.VMEM((QUAD, QUAD), F32),
            pltpu.VMEM((QUAD, QUAD), F32),
            pltpu.VMEM((8, QUAD), F32),
        ]
        + last,
    )
    return pl.pallas_call(
        functools.partial(
            ordered,
            functools.partial(attention_forward, quad, shards),
            3 + len(operands),
            len(earlier),
        ),
        grid_spec=grid_spec,
        out_shape=[low] * 6 + [shaped((length, QUAD), F32), low, states, states]
        + out_shape,
        compiler_params=params(),
        cost_estimate=COST,
        name=f"attention_forward_{quad}",
    )(segments, x, segments, *operands, *earlier)


def call_feed_forward(shards, reps, tokens, *operands):
    length = operands[0].shape[0]
    chunks = length // ROWS
    r = 512 // shards
    tile = lambda width: pl.BlockSpec((ROWS, width), lambda c: (c, 0))
    payload = (reps, shards, branch_rows(shards, reps)[0], 256)
    return pl.pallas_call(
        functools.partial(feed_forward, shards, tokens),
        grid=(chunks,),
        in_specs=[
            tile(512),
            tile(QUAD),
            tile(QUAD),
            tile(512),
            pl.BlockSpec((1, ROWS), lambda c: (0, c)),
            whole((8, 512)),
            whole((8, 2048)),
            whole((8, 128)),
            anywhere(),
            anywhere(),
        ],
        out_specs=[tile(512)] * 3 + [whole(payload)] * 2,
        out_shape=[
            shaped((length, 512), BF16),
            shaped((length, 512), F32),
            shaped((length, 512), BF16),
            *[shaped(payload, BF16)] * 2,
        ],
        scratch_shapes=[
            pltpu.VMEM((2 * shards, r // 2, 512), BF16),
            pltpu.VMEM((4, 512, 512), BF16),
            pltpu.VMEM((2048, 512), BF16),
            pltpu.VMEM((ROWS, 2048), BF16),
            pltpu.VMEM((512, 512), F32),
            pltpu.VMEM((4, 512, 512), F32),
            pltpu.VMEM((2048, 512), F32),
            pltpu.VMEM((8, 512), F32),
            pltpu.VMEM((8, 2048), F32),
            pltpu.VMEM((8, 128), F32),
            pltpu.SemaphoreType.DMA((3,)),
        ],
        compiler_params=params(),
        cost_estimate=COST,
        name="feed_forward",
    )(*operands)


def call_backward(shards, segments, x, sides, operands, earlier):
    length = x.shape[0]
    chunks = length // BACK
    r = 512 // shards
    back = lambda c: chunks - 1 - c
    wide = pl.BlockSpec((BACK, 512), lambda c, *_: (back(c), 0))
    own = pl.BlockSpec((BACK, QUAD), lambda c, *_: (back(c), 0))
    state = pl.BlockSpec((BACK // SUB, QUAD, QUAD), lambda c, *_: (back(c), 0, 0))
    payload = (2, 2, 2, shards // 2, 2 * r + 16, 128)
    grid_spec = pltpu.PrefetchScalarGridSpec(
        num_scalar_prefetch=1,
        grid=(chunks,),
        in_specs=[
            wide,
            pl.BlockSpec((1, BACK), lambda c, *_: (0, back(c))),
            *([own] * 7 + [state] * 2) * 2,
            wide,
            whole((4, 512, 512)),
            whole((8, 512)),
            wide,
            *[anywhere()] * len(earlier),
        ],
        out_specs=[wide, whole(payload), whole(payload)],
        scratch_shapes=[
            pltpu.VMEM((2, QUAD, QUAD), F32),
            pltpu.VMEM((2, QUAD, QUAD), F32),
            pltpu.VMEM((2, 8, QUAD), F32),
            pltpu.VMEM((512, 8 * QUAD), F32),
            pltpu.VMEM((8, 512), F32),
        ],
    )
    return pl.pallas_call(
        functools.partial(
            ordered, functools.partial(attention_backward, shards), 25, len(earlier)
        ),
        grid_spec=grid_spec,
        out_shape=[shaped((length, 512), F32), shaped(payload, BF16), shaped(payload, BF16)],
        compiler_params=params(),
        cost_estimate=COST,
        name="attention_backward",
    )(segments, x, segments, *sides[0], *sides[1], *operands, *earlier)


def swap(value, axis, bit):
    n = lax.axis_size(axis)
    return lax.ppermute(value, axis, [(i, i ^ bit) for i in range(n)])


def bit_groups(shards):
    bits = shards.bit_length() - 1
    return [(low, min(2, bits - low)) for low in range(1, bits, 2)]


def branch_rows(shards, reps):
    r = 512 // shards
    piece = -(-(9 * r + 16) // (16 * reps)) * 16
    names = [("contract", 4 * r)] + [(b, r) for b in range(4)] + [("output", r), ("vectors", 16)]
    rows, at = [], 0
    for name, height in names + [("none", piece * reps - 9 * r - 16)]:
        done = 0
        while done < height:
            part, offset = divmod(at, piece)
            size = min(height - done, piece - offset)
            rows.append((name, done, part, offset, size))
            done += size
            at += size
    return piece, rows


def add_arrived(shards, *refs):
    source, target = refs[0], refs[-1]
    for half in range(2):
        total = 0.0
        for rep in range(half, source.shape[0], 2):
            for s in range(shards):
                total = total + source[rep, s].astype(F32)
        target[half] = total.astype(BF16)


def call_add_arrived(shards, arrived, *others):
    reps, _, piece, width = arrived.shape
    return pl.pallas_call(
        functools.partial(add_arrived, shards),
        in_specs=[pl.BlockSpec(memory_space=pltpu.VMEM)] + [anywhere()] * len(others),
        out_specs=pl.BlockSpec(memory_space=pltpu.VMEM),
        out_shape=shaped((2, piece, width), BF16),
        compiler_params=pltpu.CompilerParams(vmem_limit_bytes=VMEM_LIMIT),
        cost_estimate=COST,
        name="add_arrived",
    )(arrived, *others)


def zero_of(arrays):
    return sum(array[(0,) * array.ndim] for array in arrays) * jnp.zeros((), BF16)


def after(value, *others):
    return lax.optimization_barrier((value, *others))[0]


def quarters(refs):
    _, core, cross = place()

    def quarter(rows, half, third):
        parts = [ref[rows, :] for ref in refs]
        near = jnp.where(core == half, parts[0], parts[1])
        far = jnp.where(core == half, parts[2], parts[3])
        return jnp.where(cross == third, near, far).astype(F32)

    def both(rows, third):
        return jnp.concatenate([quarter(rows, half, third) for half in range(2)], axis=1)

    return both


def assemble_branch(shards, count_ref, *refs):
    held = refs[-1]
    reps = held.shape[0]
    me = lax.axis_index("rep")
    for a in range(reps):
        held[me ^ a] = refs[a][...]
    contract_ref, expand_ref, output_ref, bias_1_ref, bias_2_ref, gain_ref, shift_ref, loss_ref = (
        refs[reps:-1]
    )
    r = 512 // shards
    _, rows = branch_rows(shards, reps)
    vectors = []
    for name, done, part, offset, size in rows:
        value = jnp.concatenate(
            [held[part, half, offset : offset + size, :] for half in range(2)], axis=1
        ).astype(F32)
        if name == "contract":
            contract_ref[done : done + size, :] = value
        elif name == "output":
            output_ref[done : done + size, :] = value
        elif name == "vectors":
            vectors.append(value[:, :256])
        elif name != "none":
            expand_ref[done : done + size, name * 512 : (name + 1) * 512] = value
    vectors = vectors[0] if len(vectors) == 1 else jnp.concatenate(vectors, axis=0)
    bias_1_ref[...] = vectors[8:9, : 4 * r]
    gain_ref[...] = vectors[0:1, :r]
    shift_ref[...] = vectors[1:2, :r]
    bias_2_ref[...] = vectors[2:3, :r]
    lane = lax.broadcasted_iota(jnp.int32, (1, 128), 1)
    power = jnp.zeros((1, 128), F32)
    for k in range(LOSS_DIGITS):
        power = jnp.where(lane == k, 8.0 ** (k - LOSS_ZERO), power)
    total = jnp.sum(vectors[0:1, 128:256] * power, axis=1, keepdims=True)
    count = 256.0 * count_ref[6:7, 0:1] + count_ref[6:7, 1:2]
    loss_ref[...] = total / (2.0 * count)


def assemble_mixer(shards, *refs):
    both = quarters(refs[:4])
    gain_ref, shift_ref = refs[8:]
    r = 512 // shards
    for m, ref in enumerate(refs[4:8]):
        for quad in range(2):
            at = quad * (2 * r + 16) + (m % 2) * r
            ref[:, quad * 256 : (quad + 1) * 256] = both(slice(at, at + r), m // 2)
    vectors = both(slice(4 * r + 16, 4 * r + 32), 0)
    gain_ref[...] = vectors[0:1, :r]
    shift_ref[...] = vectors[1:2, :r]


def assemble(body, shards, parts, shapes, scratch=()):
    return pl.pallas_call(
        functools.partial(body, shards),
        in_specs=[pl.BlockSpec(memory_space=pltpu.VMEM)] * len(parts),
        out_specs=[pl.BlockSpec(memory_space=pltpu.VMEM)] * len(shapes),
        out_shape=[shaped(shape, F32) for shape in shapes],
        scratch_shapes=list(scratch),
        cost_estimate=COST,
        name="assemble",
    )(*parts)


def add_low(*parts):
    return sum(part.astype(F32) for part in parts).astype(BF16)


def local(
    inputs,
    segments,
    valid_mask,
    teacher,
    query_weight,
    key_weight,
    value_weight,
    control_weight,
    output_weight,
    gain_first,
    shift_first,
    expand_weight,
    expand_bias,
    contract_weight,
    contract_bias,
    gain_second,
    shift_second,
):
    _, length, width = inputs.shape
    shards, reps = lax.axis_size("shard"), lax.axis_size("rep")
    r = width // shards
    core = lax.axis_index("rep") % 2
    cross = (lax.axis_index("rep") // 2) % 2
    groups = bit_groups(shards)

    matrices = (query_weight, key_weight, value_weight, control_weight, output_weight)
    matrices += (expand_weight, contract_weight)
    biases = (gain_first, shift_first, gain_second, shift_second, contract_bias, expand_bias)
    mixer, branch = call_pack(shards, matrices, biases, valid_mask)

    def along_z(payload):
        held = [payload[None]]
        for low, bits in groups:
            if len(held) > 1:
                held = [jnp.concatenate(held, axis=0)]
            held += [swap(held[0], "shard", a << low) for a in range(1, 1 << bits)]
        return held

    def halves(held):
        if len(held) == 4:
            return jnp.concatenate(held[:2], axis=0), jnp.concatenate(held[2:], axis=0)
        joined = jnp.concatenate(held, axis=0)
        half = joined.shape[0] // 2
        return joined[:half], joined[half:]

    def step_one(first, second):
        return swap(first, "shard", 1), swap(second, "rep", 2)

    def join(first, second, arrived):
        return jnp.concatenate([first, arrived[0]]), jnp.concatenate([second, arrived[1]])

    def step_two(first, second):
        return swap(first, "rep", 2), swap(second, "shard", 1)

    first, second = halves(along_z(mixer))
    first, second = join(first, second, step_one(first, second))
    arrived = step_two(first, second)
    held_b = along_z(branch)
    first_b, second_b = halves(held_b)
    pending = step_one(first_b, second_b)
    mine_a = jnp.concatenate([first, arrived[0], second, arrived[1] + zero_of(held_b[1:])])
    theirs_a = swap(mine_a, "rep", 1)

    x = inputs.reshape(length, width)
    forward_0 = call_forward(
        0, shards, segments, x, (mine_a, theirs_a), (first_b, second_b)
    )
    weights, vectors, bias, count = forward_0[10:]
    bit = 4
    while bit < reps:
        count = count + swap(count, "rep", bit)
        bit *= 2
    pending = after(pending, forward_0[7])
    first_b, second_b = join(first_b, second_b, pending)
    pending = step_two(first_b, second_b)
    forward_1 = call_forward(1, shards, segments, x, (weights, vectors), (first_b, second_b))
    pending = after(pending, forward_1[7])
    mine_b = jnp.concatenate([first_b, pending[0], second_b, pending[1]])
    theirs_b = swap(mine_b, "rep", 1)
    mixed = (forward_0[7], forward_1[7])

    layer_out, grad_hidden, grad_mix, keep_f, send_f = call_feed_forward(
        shards,
        reps,
        float(length * shards * reps),
        x,
        *mixed,
        teacher.reshape(length, width),
        valid_mask,
        vectors,
        bias,
        count,
        mine_b,
        theirs_b,
    )

    def split(parts):
        return add_low(*(part[0] for part in parts)), add_low(*(part[1] for part in parts))

    def cross_first(parts):
        keep, send = split(parts)
        return keep, swap(send, "rep", 2)

    def row_first(parts):
        keep, send = split(parts)
        return keep, swap(send, "shard", 1)

    def z_stage(parts_list):
        current = parts_list
        for low, bits in reversed(groups):
            span = 1 << (low - 1)
            pieces = [
                jnp.concatenate(
                    [
                        add_low(*(part[a * span : (a + 1) * span] for part in parts))
                        for parts in current
                    ],
                    axis=1,
                )
                for a in range(1 << bits)
            ]
            arrived = [swap(pieces[a], "shard", a << low) for a in range(1, 1 << bits)]
            current = [(pieces[0], *arrived)]
        return current[0]

    def finish(parts):
        total = add_low(*(part[0] for part in parts))
        bit = 4
        while bit < reps:
            total = add_low(total, swap(total, "rep", bit))
            bit *= 2
        return [total] + [swap(total, "rep", a) for a in range(1, 4)]

    summed = add_low(keep_f, swap(send_f, "rep", 1))
    every = summed.reshape(reps * shards, *summed.shape[2:])
    arrived_f = lax.all_to_all(every, ("rep", "shard"), 0, 0).reshape(summed.shape)
    sides = [(*saved[:7], *saved[8:10]) for saved in (forward_0, forward_1)]
    grad_inputs, keep_q, send_q = call_backward(
        shards, segments, x, sides, (grad_mix, weights, vectors, grad_hidden), (every,)
    )
    late_q = swap(send_q, "rep", 1)
    parts_0, parts_1 = row_first((keep_q[0], late_q[0])), cross_first((keep_q[1], late_q[1]))
    parts_0, parts_1 = cross_first(parts_0), row_first(parts_1)
    q_pieces = z_stage([parts_0, parts_1])
    total_f = call_add_arrived(shards, arrived_f, q_pieces[0])
    parts_f = [total_f] + [swap(total_f, "rep", a) for a in range(1, reps)]
    parts_q = finish(q_pieces)
    grad_contract, grad_expand, grad_output, bias_1, bias_2, gain_2, shift_2, loss = assemble(
        assemble_branch,
        shards,
        [count, *parts_f],
        [(4 * r, 512), (r, 2048), (r, 512), (1, 4 * r), (1, r), (1, r), (1, r), (1, 1)],
        [pltpu.VMEM((reps, *total_f.shape), BF16)],
    )
    *mats, gain_1, shift_1 = assemble(
        assemble_mixer, shards, parts_q, [(r, 512)] * 4 + [(1, r)] * 2
    )
    return (
        layer_out.reshape(inputs.shape),
        grad_inputs.reshape(inputs.shape),
        loss.reshape(()),
        *mats,
        grad_output,
        gain_1.reshape(r),
        shift_1.reshape(r),
        grad_expand,
        bias_1.reshape(4 * r),
        grad_contract,
        bias_2.reshape(r),
        gain_2.reshape(r),
        shift_2.reshape(r),
    )


def solution(mesh):
    every = P(("rep", "shard"), None, None)
    every_row = P(("rep", "shard"), None)
    matrix, vector = P("shard", None), P("shard")
    in_specs = (
        every,
        every_row,
        every_row,
        every,
        *[matrix] * 5,
        *[vector] * 2,
        matrix,
        vector,
        matrix,
        *[vector] * 3,
    )
    out_specs = (
        every,
        every,
        P(),
        *[matrix] * 5,
        *[vector] * 2,
        matrix,
        vector,
        matrix,
        *[vector] * 3,
    )
    return jax.shard_map(local, mesh=mesh, in_specs=in_specs, out_specs=out_specs, check_vma=False)
```

```python
import functools

import jax
import jax.numpy as jnp
from jax import lax
from jax.experimental import pallas as pl
from jax.experimental.pallas import tpu as pltpu
from jax.sharding import PartitionSpec as P

HEADS = 8
EPSILON = 1e-05
CHUNK = 256
SUB = 128
BACK = 512
QUAD = 256
F32 = jnp.float32
BF16 = jnp.bfloat16
VMEM_LIMIT = 60 << 20
LOSS_DIGITS = 30
LOSS_ZERO = 10
COST = pl.CostEstimate(flops=1000, bytes_accessed=1000, transcendentals=0)


def ordered(kernel, at, count, *refs):
    kernel(*refs[:at], *refs[at + count :])


def place():
    rep = lax.axis_index("rep")
    return lax.axis_index("shard"), rep % 2, (rep // 2) % 2


def slots_of(shards):
    ways = shards // 2
    low, high = range(ways // 2), range(ways // 2, ways)
    first = [(z, y, x) for x in (0, 1) for y in (0, 1) for z in low]
    second = [(z, y, x) for y in (0, 1) for x in (0, 1) for z in high]
    return first + second


def nn(left, right):
    return jnp.dot(left, right, preferred_element_type=F32)


def nt(left, right):
    return lax.dot_general(left, right, (((1,), (1,)), ((), ())), preferred_element_type=F32)


def tn(left, right):
    return lax.dot_general(left, right, (((0,), (0,)), ((), ())), preferred_element_type=F32)


def head_lanes():
    lane = lax.broadcasted_iota(jnp.int32, (1, QUAD), 1) // 64
    return [jnp.where(lane == h, 1.0, 0.0).astype(BF16) for h in range(4)]


def block_diagonal():
    rows = lax.broadcasted_iota(jnp.int32, (QUAD, QUAD), 0) // 64
    columns = lax.broadcasted_iota(jnp.int32, (QUAD, QUAD), 1) // 64
    return jnp.where(rows == columns, 1.0, 0.0)


def as_column(row, width):
    tile = jnp.broadcast_to(row, (128, row.shape[1])).T
    return jnp.concatenate([tile] * (width // 128), axis=1)


def causal_mask(column, row):
    at = lax.broadcasted_iota(jnp.int32, (SUB, SUB), 0)
    source = lax.broadcasted_iota(jnp.int32, (SUB, SUB), 1)
    return jnp.where((column[:, :SUB] == row) & (source <= at), 1.0, 0.0).astype(BF16)


def causal_mask_transposed(column, row):
    source = lax.broadcasted_iota(jnp.int32, (SUB, SUB), 0)
    at = lax.broadcasted_iota(jnp.int32, (SUB, SUB), 1)
    return jnp.where((column[:, :SUB] == row) & (source <= at), 1.0, 0.0).astype(BF16)


def head_stack(values):
    return jnp.concatenate([values * lanes for lanes in head_lanes()], axis=0)


def four_times(mask):
    return jnp.concatenate([mask] * 4, axis=1)


def per_head(values, reduce, fill):
    lane = lax.broadcasted_iota(jnp.int32, (1, 128), 1)
    first = lane < 64
    tiles = []
    for tile in range(values.shape[1] // 128):
        part = values[:, tile * 128 : (tile + 1) * 128]
        one = reduce(jnp.where(first, part, fill), axis=-1, keepdims=True)
        two = reduce(jnp.where(first, fill, part), axis=-1, keepdims=True)
        tiles.append(jnp.where(first, one, two))
    return jnp.concatenate(tiles, axis=1)


def standardise(values):
    mean = jnp.mean(values, axis=-1, keepdims=True)
    centred = values - mean
    variance = jnp.mean(centred * centred, axis=-1, keepdims=True)
    scale = lax.rsqrt(variance + EPSILON)
    return centred * scale, scale


def norm_backward(gradient, gain, normal, scale):
    upstream = gradient * gain
    one = jnp.mean(upstream, axis=-1, keepdims=True)
    two = jnp.mean(upstream * normal, axis=-1, keepdims=True)
    return (upstream - one - normal * two) * scale


def spread(rows, shards):
    width = 512 // shards
    lane = lax.broadcasted_iota(jnp.int32, (8, 128), 1)
    tiles = [None] * 4
    for s in range(shards):
        tile, offset = divmod(s * width, 128)
        moved = pltpu.roll(rows[s], offset, 1) if offset else rows[s]
        inside = (lane >= offset) & (lane < offset + width)
        tiles[tile] = jnp.where(inside, moved, 0.0 if tiles[tile] is None else tiles[tile])
    return jnp.concatenate(tiles, axis=1)


def digits_of(value):
    lane = lax.broadcasted_iota(jnp.int32, (8, 128), 1)
    scale = jnp.zeros((8, 128), F32)
    for k in range(LOSS_DIGITS):
        scale = jnp.where(lane == k, 8.0 ** (LOSS_ZERO - k), scale)
    shifted = value * scale
    return jnp.floor(shifted) - 8.0 * jnp.floor(shifted * 0.125)


def piece_of(vectors, s, width):
    tile, offset = divmod(s * width, 128)
    part = vectors[:, tile * 128 : (tile + 1) * 128]
    return pltpu.roll(part, 128 - offset, 1) if offset else part


def pack(shards, *refs):
    query, key, value, control, output, expand, contract = refs[:7]
    gain_1, shift_1, gain_2, shift_2, bias_2, bias_1, valid = refs[7:14]
    mixer_ref, branch_ref = refs[14:]
    r = 512 // shards
    _, core, cross = place()

    def write(half, third):
        at = slice(half * 256, half * 256 + 256)
        for m, ref in enumerate(((query, key), (value, control))[third]):
            mixer_ref[m * r : (m + 1) * r] = ref[:, at]
        if third == 0:
            for b in range(4):
                part = expand[:, b * 512 + half * 256 : b * 512 + half * 256 + 256]
                branch_ref[b * r : (b + 1) * r] = part
        else:
            branch_ref[0 : 4 * r] = contract[:, at]
        branch_ref[4 * r : 4 * r + r // 2] = output[third * (r // 2) : (third + 1) * (r // 2), at]

    for half in range(2):
        for third in range(2):
            pl.when((core == half) & (cross == third))(functools.partial(write, half, third))

    row = lax.broadcasted_iota(jnp.int32, (16, 256), 0)
    lane = lax.broadcasted_iota(jnp.int32, (16, 256), 1)
    block = jnp.zeros((16, 256), F32)
    for k, ref in ((0, gain_1), (1, shift_1), (2, gain_2), (3, shift_2), (4, bias_2), (8, bias_1)):
        part = ref[...].astype(F32)
        part = jnp.concatenate([part[n : n + 1] for n in range(part.shape[0])], axis=1)
        width = part.shape[1]
        if width < 256:
            part = jnp.concatenate([part, jnp.zeros((1, 256 - width), F32)], axis=1)
        block = jnp.where(row == k, part, block)
    count = jnp.sum(valid[...].astype(F32))
    high = jnp.floor(count / 256.0)
    block = jnp.where((row == 6) & (lane == 0), high, block)
    block = jnp.where((row == 6) & (lane == 1), count - 256.0 * high, block)
    mixer_ref[2 * r : 2 * r + 16] = block.astype(BF16)


def attention_forward(quad, shards, seg_s, x_ref, seg_ref, *refs):
    step = pl.program_id(0)
    r = 512 // shards
    at = slice(quad * QUAD, (quad + 1) * QUAD)
    if quad == 0:
        mine_ref, theirs_ref = refs[:2]
        q_ref, k_ref, v_ref, e_ref, p_ref, s_ref, rz_ref, mix_ref, one_ref, two_ref = refs[2:12]
        w_ref, vec_ref, eb_ref, count_ref = refs[12:16]
        held, first_state, second_state, total_state, sems = refs[16:]
        weight = lambda m: w_ref[m, :, at]
    else:
        w_ref, vec_ref = refs[:2]
        q_ref, k_ref, v_ref, e_ref, p_ref, s_ref, rz_ref, mix_ref, one_ref, two_ref = refs[2:12]
        first_state, second_state, total_state = refs[12:]
        weight = lambda m: w_ref[m]

    @pl.when(step == 0)
    def _():
        first_state[...] = jnp.zeros_like(first_state)
        second_state[...] = jnp.zeros_like(second_state)
        total_state[...] = jnp.zeros_like(total_state)

    def assemble():
        me, core, cross = place()
        for half, source in enumerate((mine_ref, theirs_ref)):
            column = pl.multiple_of(((core + half) % 2) * 256, 256)
            for slot, (z, y, x) in enumerate(slots_of(shards)):
                owner = me ^ (2 * z + y)
                third = cross ^ x
                for m in range(2):
                    pltpu.make_async_copy(
                        source.at[slot, pl.ds(m * r, r)],
                        w_ref.at[
                            2 * third + m,
                            pl.ds(pl.multiple_of(owner * r, r), r),
                            pl.ds(column, 256),
                        ],
                        sems.at[0],
                    ).start()
                pltpu.make_async_copy(
                    source.at[slot, pl.ds(2 * r, 16)], held.at[2 * half + x, owner], sems.at[1]
                ).start()
        pltpu.make_async_copy(held, held, sems.at[1]).wait()
        own = [held[0, s].astype(F32) for s in range(shards)]
        count = sum(part[:8, :128] for part in own)
        for k in range(1, 4):
            count += jnp.sum(held[k, :, :8, :128].astype(F32), axis=0)
        count_ref[...] = count
        vec_ref[...] = spread([part[:8, :128] for part in own], shards)
        width = 2048 // shards
        lane = lax.broadcasted_iota(jnp.int32, (8, 128), 1)
        if width >= 128:
            for s in range(shards):
                eb_ref[:, s * width : (s + 1) * width] = own[s][8:16, :width]
        else:
            for tile in range(16):
                built = jnp.zeros((8, 128), F32)
                for k in range(128 // width):
                    part = own[tile * (128 // width) + k][8:16, :128]
                    moved = pltpu.roll(part, k * width, 1) if k else part
                    built = jnp.where((lane >= k * width) & (lane < (k + 1) * width), moved, built)
                eb_ref[:, tile * 128 : (tile + 1) * 128] = built
        pltpu.make_async_copy(w_ref, w_ref, sems.at[0]).wait()

    if quad == 0:
        pl.when(step == 0)(assemble)

    row_all = seg_ref[...].astype(F32)
    diagonal = block_diagonal()
    normal, _ = standardise(x_ref[...].astype(F32))
    normed = (normal * vec_ref[0:1, :] + vec_ref[1:2, :]).astype(BF16)
    q_ref[...] = nn(normed, weight(0)).astype(BF16)
    k_ref[...] = nn(normed, weight(1)).astype(BF16)
    v_ref[...] = nn(normed, weight(2)).astype(BF16)
    e_ref[...] = jnp.exp(nn(normed, weight(3))).astype(BF16)
    subs = range(CHUNK // SUB)
    spans = [slice(sub * SUB, (sub + 1) * SUB) for sub in subs]
    q, k, v, e = ([ref[rows] for rows in spans] for ref in (q_ref, k_ref, v_ref, e_ref))
    causal, causal_4, enters, one, two, totals = [], [], [], [], [], []
    first, second, running = first_state[...], second_state[...], total_state[0:1, :]
    for sub in subs:
        start = step * CHUNK + sub * SUB
        segment_last = seg_s[0, start + SUB - 1]
        segment_before = jnp.where(start == 0, -1, seg_s[0, jnp.maximum(start - 1, 0)])
        keep = jnp.where(segment_last == segment_before, 1.0, 0.0)
        row = row_all[:, spans[sub]]
        column = as_column(row, QUAD)
        causal.append(causal_mask(column, row))
        causal_4.append(four_times(causal[sub]))
        enters.append(jnp.where(column == segment_before.astype(F32), 1.0, 0.0))
        leaves = jnp.where(column == segment_last.astype(F32), 1.0, 0.0).astype(BF16)
        one.append(first.astype(BF16))
        two.append(second.astype(BF16))
        one_ref[sub] = one[sub]
        two_ref[sub] = two[sub]
        totals.append(nn(causal[sub], e[sub]) + enters[sub] * running)
        running = totals[sub][SUB - 1 : SUB, :]
        first = keep * first + diagonal * tn(k[sub] * leaves, e[sub])
        second = keep * second + diagonal * tn(e[sub] * leaves, v[sub])
    first_state[...] = first
    second_state[...] = second
    total_state[0:1, :] = running

    def each(function, *lists):
        return [function(*values) for values in zip(*lists)]

    def store(ref, values):
        for rows, value in zip(spans, values):
            ref[rows] = value

    inverse = each(lambda a: 1.0 / a, totals)
    store(rz_ref, inverse)
    e_stack = each(head_stack, e)
    scores = each(lambda a, b, c: nt(a, head_stack(b)).astype(BF16) * c, q, k, causal_4)
    gathered = each(
        lambda a, b, c, d, f: nn(a, b) + c * nn(d, f), scores, e_stack, enters, q, one
    )
    slot_scores = each(lambda a, b: a * (b * 0.125), gathered, inverse)
    raised = each(lambda a: jnp.exp(a - per_head(a, jnp.max, -jnp.inf)), slot_scores)
    shares = each(lambda a: a / per_head(a, jnp.sum, 0.0), raised)
    scaled = each(lambda a, b: (a * b).astype(BF16), shares, inverse)
    mixing = each(lambda a, b, c: nt(a, b).astype(BF16) * c, scaled, e_stack, causal_4)
    mixed = each(
        lambda a, b, c, d, f: nn(a, head_stack(b)) + c * nn(d, f), mixing, v, enters, scaled, two
    )
    store(s_ref, each(lambda a: a.astype(BF16), slot_scores))
    store(p_ref, each(lambda a: a.astype(BF16), shares))
    store(mix_ref, each(lambda a: a.astype(BF16), mixed))


def feed_forward(
    shards,
    tokens,
    x_ref,
    mix_0_ref,
    mix_1_ref,
    teacher_ref,
    valid_ref,
    vec_ref,
    eb_ref,
    count_ref,
    mine_ref,
    theirs_ref,
    out_ref,
    hidden_ref,
    grad_mix_ref,
    keep_out_ref,
    send_out_ref,
    x,
    mix,
    teacher,
    wo,
    we,
    wc,
    act,
    out,
    hidden_grad,
    grad_mix,
    keep_ref,
    send_ref,
    normed,
    low,
    d_normed,
    d_wo,
    d_we,
    d_wc,
    d_vec,
    d_eb,
    sems,
):
    r = 512 // shards
    me, core, cross = place()
    copies = [
        pltpu.make_async_copy(mix_0_ref, mix.at[:, pl.ds(0, QUAD)], sems.at[0]),
        pltpu.make_async_copy(mix_1_ref, mix.at[:, pl.ds(QUAD, QUAD)], sems.at[1]),
        pltpu.make_async_copy(x_ref, x, sems.at[2]),
        pltpu.make_async_copy(teacher_ref, teacher, sems.at[3]),
    ]
    sources = list(enumerate((mine_ref, theirs_ref)))
    columns = [pl.multiple_of(((core + half) % 2) * 256, 256) for half, _ in sources]
    for copy in copies[:2]:
        copy.start()
    for half, source in sources:
        for slot, (z, y, cross_slot) in enumerate(slots_of(shards)):
            pltpu.make_async_copy(
                source.at[slot, pl.ds(4 * r, r // 2)],
                wo.at[2 * (me ^ (2 * z + y)) + (cross ^ cross_slot), :, pl.ds(columns[half], 256)],
                sems.at[4],
            ).start()
    copies[2].start()
    for half, source in sources:
        for slot, (z, y, cross_slot) in enumerate(slots_of(shards)):
            owner = me ^ (2 * z + y)

            def expansion():
                for b in range(4):
                    pltpu.make_async_copy(
                        source.at[slot, pl.ds(b * r, r)],
                        we.at[
                            b, pl.ds(pl.multiple_of(owner * r, r), r), pl.ds(columns[half], 256)
                        ],
                        sems.at[5],
                    ).start()

            def contraction():
                pltpu.make_async_copy(
                    source.at[slot, pl.ds(0, 4 * r)],
                    wc.at[
                        pl.ds(pl.multiple_of(owner * 4 * r, 4 * r), 4 * r),
                        pl.ds(columns[half], 256),
                    ],
                    sems.at[6],
                ).start()

            pl.when((cross ^ cross_slot) == 0)(expansion)
            pl.when((cross ^ cross_slot) == 1)(contraction)
    copies[3].start()

    gain, shift, bias = vec_ref[2:3, :], vec_ref[3:4, :], vec_ref[4:5, :]
    copies[0].wait()
    copies[1].wait()
    pltpu.make_async_copy(wo, wo, sems.at[4]).wait()
    copies[2].wait()
    weight_out = wo[...].reshape(512, 512)
    hidden = x[...].astype(F32) + nn(mix[...], weight_out)
    normal, scale = standardise(hidden)
    normed[...] = (normal * gain + shift).astype(BF16)
    pltpu.make_async_copy(we, we, sems.at[5]).wait()
    for b in range(4):
        before = nn(normed[...], we[b]) + eb_ref[0:1, b * 512 : (b + 1) * 512]
        act[b] = jnp.maximum(before, 0.0).astype(BF16)
    pltpu.make_async_copy(wc, wc, sems.at[6]).wait()
    active = jnp.concatenate([act[b] for b in range(4)], axis=1)
    result = hidden + (nn(active, wc[...]) + bias)
    out[...] = result.astype(BF16)
    out_copy = pltpu.make_async_copy(out, out_ref, sems.at[7])
    out_copy.start()
    copies[3].wait()
    valid = as_column(valid_ref[...].astype(F32), 512)
    error = result - teacher[...].astype(F32)
    masked = valid * error
    loss = jnp.sum(masked * error)
    count = 256.0 * count_ref[6:7, 0:1] + count_ref[6:7, 1:2]
    grad_result = masked * (tokens / count)
    hidden_grad[...] = grad_result
    low[...] = grad_result.astype(BF16)
    d_normed[...] = jnp.zeros_like(d_normed)

    @pl.loop(0, 4)
    def _(b):
        at = pl.ds(pl.multiple_of(b * 512, 512), 512)
        d_wc[at, :] = tn(act[b], low[...]).astype(BF16)
        grad = jnp.where(act[b] > 0, nt(low[...], wc[at, :]), 0.0).astype(BF16)
        d_we[b] = tn(normed[...], grad).astype(BF16)
        d_eb[b, 0:1, :] = jnp.sum(grad.astype(F32), axis=0, keepdims=True)
        d_normed[...] += nt(grad, we[b])

    incoming = d_normed[...]
    hidden = x[...].astype(F32) + nn(mix[...], weight_out)
    normal, scale = standardise(hidden)
    d_vec[0:1, :] = jnp.sum(incoming * normal, axis=0, keepdims=True)
    d_vec[1:2, :] = jnp.sum(incoming, axis=0, keepdims=True)
    d_vec[2:3, :] = jnp.sum(low[...].astype(F32), axis=0, keepdims=True)
    d_vec[3:8, :] = jnp.zeros((5, 512), F32)
    grad_hidden = hidden_grad[...] + norm_backward(incoming, gain, normal, scale)
    hidden_grad[...] = grad_hidden
    hidden_copy = pltpu.make_async_copy(hidden_grad, hidden_ref, sems.at[8])
    hidden_copy.start()
    grad_low = grad_hidden.astype(BF16)
    grad_mix[...] = nt(grad_low, weight_out).astype(BF16)
    mix_copy = pltpu.make_async_copy(grad_mix, grad_mix_ref, sems.at[9])
    mix_copy.start()
    d_wo[...] = tn(mix[...], grad_low).astype(BF16)

    width = 2048 // shards
    digits = digits_of(jnp.zeros((8, 128), F32) + loss)
    _, rows = branch_rows(shards, keep_ref.shape[0])
    d_eb_all = jnp.concatenate([d_eb[b] for b in range(4)], axis=1)
    extra = []
    for s in range(shards):
        top = jnp.concatenate([piece_of(d_vec[...], s, r), digits], axis=1)
        if width >= 128:
            low_rows = d_eb_all[:, s * width : (s + 1) * width]
        else:
            low_rows = piece_of(d_eb_all, s, width)
        if low_rows.shape[1] < 256:
            pad = jnp.zeros((8, 256 - low_rows.shape[1]), F32)
            low_rows = jnp.concatenate([low_rows, pad], axis=1)
        extra.append(jnp.concatenate([top, low_rows], axis=0).astype(BF16))

    def write(ref, at, wanted):
        for s in range(shards):
            for name, done, part, offset, size in rows:
                if part != wanted:
                    continue
                if name == "contract":
                    value = d_wc[s * 4 * r + done : s * 4 * r + done + size, at]
                elif name == "output":
                    value = d_wo[s * r + done : s * r + done + size, at]
                elif name == "vectors":
                    value = extra[s][done : done + size]
                elif name == "none":
                    value = jnp.zeros((size, 256), BF16)
                else:
                    value = d_we[name, s * r + done : s * r + done + size, at]
                ref[part, s, offset : offset + size, :] = value

    left, right = slice(0, 256), slice(256, 512)
    reps = keep_ref.shape[0]
    flights = []
    for part in range(reps):

        @pl.when(core == 0)
        def _():
            write(send_ref, right, part)
            write(keep_ref, left, part)

        @pl.when(core == 1)
        def _():
            write(send_ref, left, part)
            write(keep_ref, right, part)

        for n, (source, target) in enumerate(
            ((send_ref, send_out_ref), (keep_ref, keep_out_ref))
        ):
            copy = pltpu.make_async_copy(
                source.at[part], target.at[part], sems.at[10 + 2 * part + n]
            )
            copy.start()
            flights.append(copy)
    for copy in [out_copy, hidden_copy, mix_copy, *flights]:
        copy.wait()


def attention_backward(shards, seg_s, x_ref, seg_ref, *refs):
    sides, refs = (refs[:9], refs[9:18]), refs[18:]
    g_ref, w_ref, vec_ref, hidden_ref, out_ref, keep_ref, send_ref = refs[:7]
    first_state, second_state, total_state, d_w, d_vec = refs[7:]
    step = pl.program_id(0)
    chunks = pl.num_programs(0)
    chunk = chunks - 1 - step
    r = 512 // shards
    me, core, cross = place()

    @pl.when(step == 0)
    def _():
        for ref in (first_state, second_state, total_state, d_w, d_vec):
            ref[...] = jnp.zeros_like(ref)

    length = chunks * BACK
    row_all = seg_ref[...].astype(F32)
    diagonal = block_diagonal()
    found = [[], []]
    for sub in reversed(range(BACK // SUB)):
        rows = slice(sub * SUB, (sub + 1) * SUB)
        start = chunk * BACK + sub * SUB
        segment_first = seg_s[0, start]
        segment_before = jnp.where(start == 0, -1, seg_s[0, jnp.maximum(start - 1, 0)])
        after_at = jnp.minimum(start + SUB, length - 1)
        segment_after = jnp.where(start + SUB == length, -1, seg_s[0, after_at])
        keep = jnp.where(segment_first == segment_after, 1.0, 0.0)
        row = row_all[:, rows]
        column = as_column(row, QUAD)
        causal_4 = four_times(causal_mask(column, row))
        turned = causal_mask_transposed(column, row)
        turned_4 = four_times(turned)
        enters = jnp.where(column == segment_before.astype(F32), 1.0, 0.0)
        goes_on = jnp.where(column == segment_after.astype(F32), 1.0, 0.0)
        opens = jnp.where(column == segment_first.astype(F32), 1.0, 0.0).astype(BF16)

        def both(function, *lists):
            return [function(*values) for values in zip(*lists)]

        q, k, v, e = ([side[n][rows] for side in sides] for n in range(4))
        grad = [g_ref[rows, g * QUAD : (g + 1) * QUAD] for g in range(2)]
        shares = [side[4][rows].astype(F32) for side in sides]
        slot_scores = [side[5][rows].astype(F32) for side in sides]
        inverse = [side[6][rows] for side in sides]
        one = [side[7][sub] for side in sides]
        two = [side[8][sub] for side in sides]
        scaled = both(lambda a, b: a * b, shares, inverse)
        scaled_low = [a.astype(BF16) for a in scaled]
        one_back = [first_state[g].astype(BF16) for g in range(2)]
        two_back = [second_state[g].astype(BF16) for g in range(2)]
        e_stack = both(head_stack, e)

        d_mixing = both(lambda a, b: nt(a, head_stack(b)).astype(BF16) * causal_4, grad, v)
        d_scaled = both(
            lambda a, b, c, d: nn(a, b) + enters * nt(c, d), d_mixing, e_stack, grad, two
        )
        q_stack, grad_stack = both(head_stack, q), both(head_stack, grad)
        scaled_stack = both(head_stack, scaled_low)
        mixing_t = both(lambda a, b: nt(a, b).astype(BF16) * turned_4, e, scaled_stack)
        d_mixing_t = both(lambda a, b: nt(a, b).astype(BF16) * turned_4, v, grad_stack)
        scores_t = both(lambda a, b: nt(a, b).astype(BF16) * turned_4, k, q_stack)
        d_shares = both(lambda a, b: a * b, d_scaled, inverse)
        product = both(lambda a, b: a * b, shares, d_shares)
        d_scores = both(lambda a, b: a - b * per_head(a, jnp.sum, 0.0), product, shares)
        d_low = both(lambda a, b: (a * b * 0.125).astype(BF16), d_scores, inverse)
        d_totals = both(
            lambda a, b, c, d, i: -(a * b + c * d) * i,
            d_scaled,
            scaled,
            d_scores,
            slot_scores,
            inverse,
        )
        d_values = both(
            lambda a, b, c, d: nn(a, b) + goes_on * nn(c, d), mixing_t, grad_stack, e, two_back
        )
        d_slots = both(nn, d_mixing_t, scaled_stack)
        d_low_stack = both(head_stack, d_low)
        d_raw = both(lambda a, b: nt(a, b).astype(BF16) * causal_4, d_low, e_stack)
        d_raw_t = both(lambda a, b: nt(a, b).astype(BF16) * turned_4, e, d_low_stack)
        d_slots = both(lambda a, b, c: a + nn(b, c), d_slots, scores_t, d_low_stack)
        d_queries = both(
            lambda a, b, c, d: nn(a, head_stack(b)) + enters * nt(c, d), d_raw, k, d_low, one
        )
        d_keys = both(
            lambda a, b, c, d: nn(a, b) + goes_on * nt(c, d), d_raw_t, q_stack, e, one_back
        )
        totals_low = [a.astype(BF16) for a in d_totals]
        rest = both(lambda a, b: (a - b.astype(F32)).astype(BF16), d_totals, totals_low)
        sums = [
            nn(turned, totals_low[g]) + nn(turned, rest[g]) + goes_on * total_state[g, 0:1, :]
            for g in range(2)
        ]
        d_slots = both(
            lambda a, b, c, d, f, h: a + goes_on * (nn(b, c) + nt(d, f)) + h,
            d_slots,
            k,
            one_back,
            v,
            two_back,
            sums,
        )
        d_control = both(lambda a, b: a * b.astype(F32), d_slots, e)
        for g in range(2):
            total_state[g, 0:1, :] = sums[g][0:1, :]
            first_state[g] = keep * first_state[g] + diagonal * tn(q[g] * opens, d_low[g])
            second_state[g] = keep * second_state[g] + diagonal * tn(
                scaled_low[g] * opens, grad[g]
            )
            parts = (d_queries[g], d_keys[g], d_values[g], d_control[g])
            found[g].append([part.astype(BF16) for part in parts])
    grads = [
        jnp.concatenate([part[m] for part in reversed(found[g])], axis=0)
        for g in range(2)
        for m in range(4)
    ]

    normal, scale = standardise(x_ref[...].astype(F32))
    gain = vec_ref[0:1, :]
    normed = (normal * gain + vec_ref[1:2, :]).astype(BF16)
    d_w[...] += tn(normed, jnp.concatenate(grads, axis=1))
    d_normed = sum(
        nt(jnp.concatenate([grads[m], grads[4 + m]], axis=1), w_ref[m]) for m in range(4)
    )
    d_vec[0:1, :] += jnp.sum(d_normed * normal, axis=0, keepdims=True)
    d_vec[1:2, :] += jnp.sum(d_normed, axis=0, keepdims=True)
    out_ref[...] = hidden_ref[...] + norm_backward(d_normed, gain, normal, scale)

    @pl.when(step == chunks - 1)
    def _():
        def write(ref, half):
            for s in range(shards):
                y, z = (me ^ s) & 1, (me ^ s) >> 1
                top = piece_of(d_vec[...], s, r)
                both_rows = jnp.concatenate([top, jnp.zeros_like(top)], axis=0).astype(BF16)
                for g in range(2):
                    for m in range(4):
                        x = cross ^ (m // 2)
                        lead = (g, x, y, z) if g else (g, y, x, z)
                        at = (4 * g + m) * QUAD + half * 128
                        part = d_w[s * r : (s + 1) * r, at : at + 128].astype(BF16)
                        ref[(*lead, slice((m % 2) * r, (m % 2 + 1) * r), slice(None))] = part
                    for x in range(2):
                        lead = (g, x, y, z) if g else (g, y, x, z)
                        ref[(*lead, slice(2 * r, 2 * r + 16), slice(None))] = both_rows

        @pl.when(core == 0)
        def _():
            write(keep_ref, 0)
            write(send_ref, 1)

        @pl.when(core == 1)
        def _():
            write(keep_ref, 1)
            write(send_ref, 0)


def whole(shape):
    return pl.BlockSpec(shape, lambda *_: (0,) * len(shape))


def anywhere():
    return pl.BlockSpec(memory_space=pl.ANY)


def shaped(shape, dtype):
    return jax.ShapeDtypeStruct(shape, dtype)


def params():
    return pltpu.CompilerParams(
        dimension_semantics=("arbitrary",), vmem_limit_bytes=VMEM_LIMIT
    )


def call_pack(shards, matrices, vectors, valid):
    r = 512 // shards
    operands = [*matrices, *[v.reshape(-1, min(128, v.shape[0])) for v in vectors], valid]
    mixer, branch = (2 * r + 16, 256), (4 * r + r // 2, 256)
    return pl.pallas_call(
        functools.partial(pack, shards),
        grid=(1,),
        in_specs=[whole(v.shape) for v in operands],
        out_specs=[whole(mixer), whole(branch)],
        out_shape=[shaped(mixer, BF16), shaped(branch, BF16)],
        compiler_params=params(),
        cost_estimate=COST,
        name="pack",
    )(*operands)


def call_forward(quad, shards, segments, x, operands, earlier):
    length = x.shape[0]
    chunks = length // CHUNK
    wide = pl.BlockSpec((CHUNK, 512), lambda c, *_: (c, 0))
    tile = pl.BlockSpec((CHUNK, QUAD), lambda c, *_: (c, 0))
    state = pl.BlockSpec((CHUNK // SUB, QUAD, QUAD), lambda c, *_: (c, 0, 0))
    low = shaped((length, QUAD), BF16)
    states = shaped((length // SUB, QUAD, QUAD), BF16)
    if quad == 0:
        in_specs = [anywhere(), anywhere()]
        out_specs = [whole((4, 512, 512)), whole((8, 512)), whole((8, 2048)), whole((8, 128))]
        out_shape = [shaped((4, 512, 512), BF16), shaped((8, 512), F32)]
        out_shape += [shaped((8, 2048), F32), shaped((8, 128), F32)]
        first = [pltpu.VMEM((4, shards, 16, 256), BF16)]
        last = [pltpu.SemaphoreType.DMA((2,))]
    else:
        in_specs = [pl.BlockSpec((4, 512, QUAD), lambda c, *_: (0, 0, 1)), whole((8, 512))]
        out_specs, out_shape, first, last = [], [], [], []
    grid_spec = pltpu.PrefetchScalarGridSpec(
        num_scalar_prefetch=1,
        grid=(chunks,),
        in_specs=[wide, pl.BlockSpec((1, CHUNK), lambda c, *_: (0, c)), *in_specs]
        + [anywhere()] * len(earlier),
        out_specs=[tile] * 8 + [state] * 2 + out_specs,
        scratch_shapes=first
        + [
            pltpu.VMEM((QUAD, QUAD), F32),
            pltpu.VMEM((QUAD, QUAD), F32),
            pltpu.VMEM((8, QUAD), F32),
        ]
        + last,
    )
    return pl.pallas_call(
        functools.partial(
            ordered,
            functools.partial(attention_forward, quad, shards),
            3 + len(operands),
            len(earlier),
        ),
        grid_spec=grid_spec,
        out_shape=[low] * 6 + [shaped((length, QUAD), F32), low, states, states]
        + out_shape,
        compiler_params=params(),
        cost_estimate=COST,
        name=f"attention_forward_{quad}",
    )(segments, x, segments, *operands, *earlier)


def call_feed_forward(shards, reps, tokens, *operands):
    length = operands[0].shape[0]
    r = 512 // shards
    payload = (reps, shards, branch_rows(shards, reps)[0], 256)
    vmem = pl.BlockSpec(memory_space=pltpu.VMEM)
    wide = (length, 512)
    return pl.pallas_call(
        functools.partial(feed_forward, shards, tokens),
        in_specs=[anywhere()] * 4 + [vmem] * 4 + [anywhere()] * 2,
        out_specs=[anywhere()] * 5,
        out_shape=[
            shaped(wide, BF16),
            shaped(wide, F32),
            shaped(wide, BF16),
            shaped(payload, BF16),
            shaped(payload, BF16),
        ],
        scratch_shapes=[
            pltpu.VMEM(wide, BF16),
            pltpu.VMEM(wide, BF16),
            pltpu.VMEM(wide, BF16),
            pltpu.VMEM((2 * shards, r // 2, 512), BF16),
            pltpu.VMEM((4, 512, 512), BF16),
            pltpu.VMEM((2048, 512), BF16),
            pltpu.VMEM((4, length, 512), BF16),
            pltpu.VMEM(wide, BF16),
            pltpu.VMEM(wide, F32),
            pltpu.VMEM(wide, BF16),
            pltpu.VMEM(payload, BF16),
            pltpu.VMEM(payload, BF16),
            pltpu.VMEM(wide, BF16),
            pltpu.VMEM(wide, BF16),
            pltpu.VMEM(wide, F32),
            pltpu.VMEM((512, 512), BF16),
            pltpu.VMEM((4, 512, 512), BF16),
            pltpu.VMEM((2048, 512), BF16),
            pltpu.VMEM((8, 512), F32),
            pltpu.VMEM((4, 8, 512), F32),
            pltpu.SemaphoreType.DMA((10 + 2 * reps,)),
        ],
        compiler_params=pltpu.CompilerParams(vmem_limit_bytes=VMEM_LIMIT),
        cost_estimate=COST,
        name="feed_forward",
    )(*operands)


def call_backward(shards, segments, x, sides, operands, earlier):
    length = x.shape[0]
    chunks = length // BACK
    r = 512 // shards
    back = lambda c: chunks - 1 - c
    wide = pl.BlockSpec((BACK, 512), lambda c, *_: (back(c), 0))
    own = pl.BlockSpec((BACK, QUAD), lambda c, *_: (back(c), 0))
    state = pl.BlockSpec((BACK // SUB, QUAD, QUAD), lambda c, *_: (back(c), 0, 0))
    payload = (2, 2, 2, shards // 2, 2 * r + 16, 128)
    grid_spec = pltpu.PrefetchScalarGridSpec(
        num_scalar_prefetch=1,
        grid=(chunks,),
        in_specs=[
            wide,
            pl.BlockSpec((1, BACK), lambda c, *_: (0, back(c))),
            *([own] * 7 + [state] * 2) * 2,
            wide,
            whole((4, 512, 512)),
            whole((8, 512)),
            wide,
            *[anywhere()] * len(earlier),
        ],
        out_specs=[wide, whole(payload), whole(payload)],
        scratch_shapes=[
            pltpu.VMEM((2, QUAD, QUAD), F32),
            pltpu.VMEM((2, QUAD, QUAD), F32),
            pltpu.VMEM((2, 8, QUAD), F32),
            pltpu.VMEM((512, 8 * QUAD), F32),
            pltpu.VMEM((8, 512), F32),
        ],
    )
    return pl.pallas_call(
        functools.partial(
            ordered, functools.partial(attention_backward, shards), 25, len(earlier)
        ),
        grid_spec=grid_spec,
        out_shape=[shaped((length, 512), F32), shaped(payload, BF16), shaped(payload, BF16)],
        compiler_params=params(),
        cost_estimate=COST,
        name="attention_backward",
    )(segments, x, segments, *sides[0], *sides[1], *operands, *earlier)


def swap(value, axis, bit):
    n = lax.axis_size(axis)
    return lax.ppermute(value, axis, [(i, i ^ bit) for i in range(n)])


def bit_groups(shards):
    bits = shards.bit_length() - 1
    return [(low, min(2, bits - low)) for low in range(1, bits, 2)]


def branch_rows(shards, reps):
    r = 512 // shards
    piece = -(-(9 * r + 16) // (16 * reps)) * 16
    names = [("contract", 4 * r)] + [(b, r) for b in range(4)] + [("output", r), ("vectors", 16)]
    rows, at = [], 0
    for name, height in names + [("none", piece * reps - 9 * r - 16)]:
        done = 0
        while done < height:
            part, offset = divmod(at, piece)
            size = min(height - done, piece - offset)
            rows.append((name, done, part, offset, size))
            done += size
            at += size
    return piece, rows


def add_arrived(shards, *refs):
    source, target = refs[0], refs[-1]
    for half in range(2):
        total = 0.0
        for rep in range(half, source.shape[0], 2):
            for s in range(shards):
                total = total + source[rep, s].astype(F32)
        target[half] = total.astype(BF16)


def call_add_arrived(shards, arrived, *others):
    reps, _, piece, width = arrived.shape
    return pl.pallas_call(
        functools.partial(add_arrived, shards),
        in_specs=[pl.BlockSpec(memory_space=pltpu.VMEM)] + [anywhere()] * len(others),
        out_specs=pl.BlockSpec(memory_space=pltpu.VMEM),
        out_shape=shaped((2, piece, width), BF16),
        compiler_params=pltpu.CompilerParams(vmem_limit_bytes=VMEM_LIMIT),
        cost_estimate=COST,
        name="add_arrived",
    )(arrived, *others)


def zero_of(arrays):
    return sum(array[(0,) * array.ndim] for array in arrays) * jnp.zeros((), BF16)


def after(value, *others):
    return lax.optimization_barrier((value, *others))[0]


def quarters(refs):
    _, core, cross = place()

    def quarter(rows, half, third):
        parts = [ref[rows, :] for ref in refs]
        near = jnp.where(core == half, parts[0], parts[1])
        far = jnp.where(core == half, parts[2], parts[3])
        return jnp.where(cross == third, near, far).astype(F32)

    def both(rows, third):
        return jnp.concatenate([quarter(rows, half, third) for half in range(2)], axis=1)

    return both


def assemble_branch(shards, count_ref, *refs):
    held = refs[-1]
    reps = held.shape[0]
    me = lax.axis_index("rep")
    for a in range(reps):
        held[me ^ a] = refs[a][...]
    contract_ref, expand_ref, output_ref, bias_1_ref, bias_2_ref, gain_ref, shift_ref, loss_ref = (
        refs[reps:-1]
    )
    r = 512 // shards
    _, rows = branch_rows(shards, reps)
    vectors = []
    for name, done, part, offset, size in rows:
        value = jnp.concatenate(
            [held[part, half, offset : offset + size, :] for half in range(2)], axis=1
        ).astype(F32)
        if name == "contract":
            contract_ref[done : done + size, :] = value
        elif name == "output":
            output_ref[done : done + size, :] = value
        elif name == "vectors":
            vectors.append(value[:, :256])
        elif name != "none":
            expand_ref[done : done + size, name * 512 : (name + 1) * 512] = value
    vectors = vectors[0] if len(vectors) == 1 else jnp.concatenate(vectors, axis=0)
    bias_1_ref[...] = vectors[8:9, : 4 * r]
    gain_ref[...] = vectors[0:1, :r]
    shift_ref[...] = vectors[1:2, :r]
    bias_2_ref[...] = vectors[2:3, :r]
    lane = lax.broadcasted_iota(jnp.int32, (1, 128), 1)
    power = jnp.zeros((1, 128), F32)
    for k in range(LOSS_DIGITS):
        power = jnp.where(lane == k, 8.0 ** (k - LOSS_ZERO), power)
    total = jnp.sum(vectors[0:1, 128:256] * power, axis=1, keepdims=True)
    count = 256.0 * count_ref[6:7, 0:1] + count_ref[6:7, 1:2]
    loss_ref[...] = total / (2.0 * count)


def assemble_mixer(shards, *refs):
    both = quarters(refs[:4])
    gain_ref, shift_ref = refs[8:]
    r = 512 // shards
    for m, ref in enumerate(refs[4:8]):
        for quad in range(2):
            at = quad * (2 * r + 16) + (m % 2) * r
            ref[:, quad * 256 : (quad + 1) * 256] = both(slice(at, at + r), m // 2)
    vectors = both(slice(4 * r + 16, 4 * r + 32), 0)
    gain_ref[...] = vectors[0:1, :r]
    shift_ref[...] = vectors[1:2, :r]


def assemble_all(shards, reps, count_ref, *refs):
    parts_q, parts_f, refs = refs[:4], refs[4 : 4 + reps], refs[4 + reps :]
    assemble_mixer(shards, *parts_q, *refs[:6])
    assemble_branch(shards, count_ref, *parts_f, *refs[6:])


def assemble(shards, count, parts_q, parts_f):
    reps = len(parts_f)
    r = 512 // shards
    shapes = [(r, 512)] * 4 + [(1, r)] * 2
    shapes += [(4 * r, 512), (r, 2048), (r, 512), (1, 4 * r), (1, r), (1, r), (1, r), (1, 1)]
    return pl.pallas_call(
        functools.partial(assemble_all, shards, reps),
        in_specs=[pl.BlockSpec(memory_space=pltpu.VMEM)] * (5 + reps),
        out_specs=[pl.BlockSpec(memory_space=pltpu.VMEM)] * len(shapes),
        out_shape=[shaped(shape, F32) for shape in shapes],
        scratch_shapes=[pltpu.VMEM((reps, *parts_f[0].shape), BF16)],
        cost_estimate=COST,
        name="assemble",
    )(count, *parts_q, *parts_f)


def add_low(*parts):
    return sum(part.astype(F32) for part in parts).astype(BF16)


def local(
    inputs,
    segments,
    valid_mask,
    teacher,
    query_weight,
    key_weight,
    value_weight,
    control_weight,
    output_weight,
    gain_first,
    shift_first,
    expand_weight,
    expand_bias,
    contract_weight,
    contract_bias,
    gain_second,
    shift_second,
):
    _, length, width = inputs.shape
    shards, reps = lax.axis_size("shard"), lax.axis_size("rep")
    r = width // shards
    core = lax.axis_index("rep") % 2
    cross = (lax.axis_index("rep") // 2) % 2
    groups = bit_groups(shards)

    matrices = (query_weight, key_weight, value_weight, control_weight, output_weight)
    matrices += (expand_weight, contract_weight)
    biases = (gain_first, shift_first, gain_second, shift_second, contract_bias, expand_bias)
    mixer, branch = call_pack(shards, matrices, biases, valid_mask)

    def along_z(payload):
        held = [payload[None]]
        for low, bits in groups:
            if len(held) > 1:
                held = [jnp.concatenate(held, axis=0)]
            held += [swap(held[0], "shard", a << low) for a in range(1, 1 << bits)]
        return held

    def halves(held):
        if len(held) == 4:
            return jnp.concatenate(held[:2], axis=0), jnp.concatenate(held[2:], axis=0)
        joined = jnp.concatenate(held, axis=0)
        half = joined.shape[0] // 2
        return joined[:half], joined[half:]

    def step_one(first, second):
        return swap(first, "shard", 1), swap(second, "rep", 2)

    def join(first, second, arrived):
        return jnp.concatenate([first, arrived[0]]), jnp.concatenate([second, arrived[1]])

    def step_two(first, second):
        return swap(first, "rep", 2), swap(second, "shard", 1)

    first, second = halves(along_z(mixer))
    first, second = join(first, second, step_one(first, second))
    arrived = step_two(first, second)
    held_b = along_z(branch)
    first_b, second_b = halves(held_b)
    pending = step_one(first_b, second_b)
    mine_a = jnp.concatenate([first, arrived[0], second, arrived[1] + zero_of(held_b[1:])])
    theirs_a = swap(mine_a, "rep", 1)

    x = inputs.reshape(length, width)
    forward_0 = call_forward(
        0, shards, segments, x, (mine_a, theirs_a), (first_b, second_b)
    )
    weights, vectors, bias, count = forward_0[10:]
    bit = 4
    while bit < reps:
        count = count + swap(count, "rep", bit)
        bit *= 2
    pending = after(pending, forward_0[7])
    first_b, second_b = join(first_b, second_b, pending)
    pending = step_two(first_b, second_b)
    forward_1 = call_forward(1, shards, segments, x, (weights, vectors), (first_b, second_b))
    pending = after(pending, forward_1[7])
    mine_b = jnp.concatenate([first_b, pending[0], second_b, pending[1]])
    theirs_b = swap(mine_b, "rep", 1)
    mixed = (forward_0[7], forward_1[7])

    layer_out, grad_hidden, grad_mix, keep_f, send_f = call_feed_forward(
        shards,
        reps,
        float(length * shards * reps),
        x,
        *mixed,
        teacher.reshape(length, width),
        valid_mask,
        vectors,
        bias,
        count,
        mine_b,
        theirs_b,
    )

    def split(parts):
        return add_low(*(part[0] for part in parts)), add_low(*(part[1] for part in parts))

    def cross_first(parts):
        keep, send = split(parts)
        return keep, swap(send, "rep", 2)

    def row_first(parts):
        keep, send = split(parts)
        return keep, swap(send, "shard", 1)

    def z_stage(parts_list):
        current = parts_list
        for low, bits in reversed(groups):
            span = 1 << (low - 1)
            pieces = [
                jnp.concatenate(
                    [
                        add_low(*(part[a * span : (a + 1) * span] for part in parts))
                        for parts in current
                    ],
                    axis=1,
                )
                for a in range(1 << bits)
            ]
            arrived = [swap(pieces[a], "shard", a << low) for a in range(1, 1 << bits)]
            current = [(pieces[0], *arrived)]
        return current[0]

    def finish(parts):
        total = add_low(*(part[0] for part in parts))
        bit = 4
        while bit < reps:
            total = add_low(total, swap(total, "rep", bit))
            bit *= 2
        return [total] + [swap(total, "rep", a) for a in range(1, 4)]

    summed = add_low(keep_f, swap(send_f, "rep", 1))
    every = summed.reshape(reps * shards, *summed.shape[2:])
    arrived_f = lax.all_to_all(every, ("rep", "shard"), 0, 0).reshape(summed.shape)
    sides = [(*saved[:7], *saved[8:10]) for saved in (forward_0, forward_1)]
    grad_inputs, keep_q, send_q = call_backward(
        shards, segments, x, sides, (grad_mix, weights, vectors, grad_hidden), (every,)
    )
    late_q = swap(send_q, "rep", 1)
    parts_0, parts_1 = row_first((keep_q[0], late_q[0])), cross_first((keep_q[1], late_q[1]))
    parts_0, parts_1 = cross_first(parts_0), row_first(parts_1)
    q_pieces = z_stage([parts_0, parts_1])
    total_f = call_add_arrived(shards, arrived_f, q_pieces[0])
    parts_f = [total_f] + [swap(total_f, "rep", a) for a in range(1, reps)]
    parts_q = finish(q_pieces)
    results = assemble(shards, count, parts_q, parts_f)
    mats, (gain_1, shift_1) = results[:4], results[4:6]
    grad_contract, grad_expand, grad_output, bias_1, bias_2, gain_2, shift_2, loss = results[6:]
    return (
        layer_out.reshape(inputs.shape),
        grad_inputs.reshape(inputs.shape),
        loss.reshape(()),
        *mats,
        grad_output,
        gain_1.reshape(r),
        shift_1.reshape(r),
        grad_expand,
        bias_1.reshape(4 * r),
        grad_contract,
        bias_2.reshape(r),
        gain_2.reshape(r),
        shift_2.reshape(r),
    )


def solution(mesh):
    every = P(("rep", "shard"), None, None)
    every_row = P(("rep", "shard"), None)
    matrix, vector = P("shard", None), P("shard")
    in_specs = (
        every,
        every_row,
        every_row,
        every,
        *[matrix] * 5,
        *[vector] * 2,
        matrix,
        vector,
        matrix,
        *[vector] * 3,
    )
    out_specs = (
        every,
        every,
        P(),
        *[matrix] * 5,
        *[vector] * 2,
        matrix,
        vector,
        matrix,
        *[vector] * 3,
    )
    return jax.shard_map(local, mesh=mesh, in_specs=in_specs, out_specs=out_specs, check_vma=False)
```

```python
import functools

import jax
import jax.numpy as jnp
from jax import lax
from jax.experimental import pallas as pl
from jax.experimental.pallas import tpu as pltpu
from jax.sharding import PartitionSpec as P

HEADS = 8
EPSILON = 1e-05
CHUNK = 256
SUB = 128
BACK = 512
QUAD = 256
F32 = jnp.float32
BF16 = jnp.bfloat16
VMEM_LIMIT = 60 << 20
LOSS_DIGITS = 30
LOSS_ZERO = 10
COST = pl.CostEstimate(flops=1000, bytes_accessed=1000, transcendentals=0)


def ordered(kernel, at, count, *refs):
    kernel(*refs[:at], *refs[at + count :])


def place():
    rep = lax.axis_index("rep")
    return lax.axis_index("shard"), rep % 2, (rep // 2) % 2


def slots_of(shards):
    ways = shards // 2
    low, high = range(ways // 2), range(ways // 2, ways)
    first = [(z, y, x) for x in (0, 1) for y in (0, 1) for z in low]
    second = [(z, y, x) for y in (0, 1) for x in (0, 1) for z in high]
    return first + second


def block_of(pieces, slot):
    each = pieces[0].shape[0]
    return pieces[slot // each].at[slot % each]


def nn(left, right):
    return jnp.dot(left, right, preferred_element_type=F32)


def nt(left, right):
    return lax.dot_general(left, right, (((1,), (1,)), ((), ())), preferred_element_type=F32)


def tn(left, right):
    return lax.dot_general(left, right, (((0,), (0,)), ((), ())), preferred_element_type=F32)


def head_lanes():
    lane = lax.broadcasted_iota(jnp.int32, (1, QUAD), 1) // 64
    return [jnp.where(lane == h, 1.0, 0.0).astype(BF16) for h in range(4)]


def block_diagonal():
    rows = lax.broadcasted_iota(jnp.int32, (QUAD, QUAD), 0) // 64
    columns = lax.broadcasted_iota(jnp.int32, (QUAD, QUAD), 1) // 64
    return jnp.where(rows == columns, 1.0, 0.0)


def as_column(row, width):
    tile = jnp.broadcast_to(row, (128, row.shape[1])).T
    return jnp.concatenate([tile] * (width // 128), axis=1)


def causal_mask(column, row):
    at = lax.broadcasted_iota(jnp.int32, (SUB, SUB), 0)
    source = lax.broadcasted_iota(jnp.int32, (SUB, SUB), 1)
    return jnp.where((column[:, :SUB] == row) & (source <= at), 1.0, 0.0).astype(BF16)


def causal_mask_transposed(column, row):
    source = lax.broadcasted_iota(jnp.int32, (SUB, SUB), 0)
    at = lax.broadcasted_iota(jnp.int32, (SUB, SUB), 1)
    return jnp.where((column[:, :SUB] == row) & (source <= at), 1.0, 0.0).astype(BF16)


def head_stack(values):
    return jnp.concatenate([values * lanes for lanes in head_lanes()], axis=0)


def four_times(mask):
    return jnp.concatenate([mask] * 4, axis=1)


def per_head(values, reduce, fill):
    lane = lax.broadcasted_iota(jnp.int32, (1, 128), 1)
    first = lane < 64
    tiles = []
    for tile in range(values.shape[1] // 128):
        part = values[:, tile * 128 : (tile + 1) * 128]
        one = reduce(jnp.where(first, part, fill), axis=-1, keepdims=True)
        two = reduce(jnp.where(first, fill, part), axis=-1, keepdims=True)
        tiles.append(jnp.where(first, one, two))
    return jnp.concatenate(tiles, axis=1)


def standardise(values):
    mean = jnp.mean(values, axis=-1, keepdims=True)
    centred = values - mean
    variance = jnp.mean(centred * centred, axis=-1, keepdims=True)
    scale = lax.rsqrt(variance + EPSILON)
    return centred * scale, scale


def norm_backward(gradient, gain, normal, scale):
    upstream = gradient * gain
    one = jnp.mean(upstream, axis=-1, keepdims=True)
    two = jnp.mean(upstream * normal, axis=-1, keepdims=True)
    return (upstream - one - normal * two) * scale


def spread(rows, shards):
    width = 512 // shards
    lane = lax.broadcasted_iota(jnp.int32, (8, 128), 1)
    tiles = [None] * 4
    for s in range(shards):
        tile, offset = divmod(s * width, 128)
        moved = pltpu.roll(rows[s], offset, 1) if offset else rows[s]
        inside = (lane >= offset) & (lane < offset + width)
        tiles[tile] = jnp.where(inside, moved, 0.0 if tiles[tile] is None else tiles[tile])
    return jnp.concatenate(tiles, axis=1)


def digits_of(value):
    lane = lax.broadcasted_iota(jnp.int32, (8, 128), 1)
    scale = jnp.zeros((8, 128), F32)
    for k in range(LOSS_DIGITS):
        scale = jnp.where(lane == k, 8.0 ** (LOSS_ZERO - k), scale)
    shifted = value * scale
    return jnp.floor(shifted) - 8.0 * jnp.floor(shifted * 0.125)


def piece_of(vectors, s, width):
    tile, offset = divmod(s * width, 128)
    part = vectors[:, tile * 128 : (tile + 1) * 128]
    return pltpu.roll(part, 128 - offset, 1) if offset else part


def pack(shards, *refs):
    query, key, value, control, output, expand, contract = refs[:7]
    gain_1, shift_1, gain_2, shift_2, bias_2, bias_1, valid = refs[7:14]
    mixer_ref, branch_ref = refs[14:]
    r = 512 // shards
    _, core, cross = place()

    def write(half, third):
        at = slice(half * 256, half * 256 + 256)
        for m, ref in enumerate(((query, key), (value, control))[third]):
            mixer_ref[m * r : (m + 1) * r] = ref[:, at]
        if third == 0:
            for b in range(4):
                part = expand[:, b * 512 + half * 256 : b * 512 + half * 256 + 256]
                branch_ref[b * r : (b + 1) * r] = part
        else:
            branch_ref[0 : 4 * r] = contract[:, at]
        branch_ref[4 * r : 4 * r + r // 2] = output[third * (r // 2) : (third + 1) * (r // 2), at]

    for half in range(2):
        for third in range(2):
            pl.when((core == half) & (cross == third))(functools.partial(write, half, third))

    row = lax.broadcasted_iota(jnp.int32, (16, 256), 0)
    lane = lax.broadcasted_iota(jnp.int32, (16, 256), 1)
    block = jnp.zeros((16, 256), F32)
    for k, ref in ((0, gain_1), (1, shift_1), (2, gain_2), (3, shift_2), (4, bias_2), (8, bias_1)):
        part = ref[...].astype(F32)
        part = jnp.concatenate([part[n : n + 1] for n in range(part.shape[0])], axis=1)
        width = part.shape[1]
        if width < 256:
            part = jnp.concatenate([part, jnp.zeros((1, 256 - width), F32)], axis=1)
        block = jnp.where(row == k, part, block)
    count = jnp.sum(valid[...].astype(F32))
    high = jnp.floor(count / 256.0)
    block = jnp.where((row == 6) & (lane == 0), high, block)
    block = jnp.where((row == 6) & (lane == 1), count - 256.0 * high, block)
    mixer_ref[2 * r : 2 * r + 16] = block.astype(BF16)


def attention_forward(quad, shards, seg_s, x_ref, seg_ref, *refs):
    step = pl.program_id(0)
    r = 512 // shards
    at = slice(quad * QUAD, (quad + 1) * QUAD)
    if quad == 0:
        pieces, refs = (refs[:4], refs[4:8]), refs[8:]
        q_ref, k_ref, v_ref, e_ref, p_ref, s_ref, rz_ref, mix_ref, one_ref, two_ref = refs[:10]
        w_ref, vec_ref, eb_ref, count_ref = refs[10:14]
        held, first_state, second_state, total_state, sems = refs[14:]
        weight = lambda m: w_ref[m, :, at]
    else:
        w_ref, vec_ref = refs[:2]
        q_ref, k_ref, v_ref, e_ref, p_ref, s_ref, rz_ref, mix_ref, one_ref, two_ref = refs[2:12]
        first_state, second_state, total_state = refs[12:]
        weight = lambda m: w_ref[m]

    @pl.when(step == 0)
    def _():
        first_state[...] = jnp.zeros_like(first_state)
        second_state[...] = jnp.zeros_like(second_state)
        total_state[...] = jnp.zeros_like(total_state)

    def assemble():
        me, core, cross = place()
        for half, source in enumerate(pieces):
            column = pl.multiple_of(((core + half) % 2) * 256, 256)
            for slot, (z, y, x) in enumerate(slots_of(shards)):
                owner = me ^ (2 * z + y)
                third = cross ^ x
                for m in range(2):
                    pltpu.make_async_copy(
                        block_of(source, slot).at[pl.ds(m * r, r)],
                        w_ref.at[
                            2 * third + m,
                            pl.ds(pl.multiple_of(owner * r, r), r),
                            pl.ds(column, 256),
                        ],
                        sems.at[0],
                    ).start()
                pltpu.make_async_copy(
                    block_of(source, slot).at[pl.ds(2 * r, 16)], held.at[2 * half + x, owner], sems.at[1]
                ).start()
        pltpu.make_async_copy(held, held, sems.at[1]).wait()
        own = [held[0, s].astype(F32) for s in range(shards)]
        count = sum(part[:8, :128] for part in own)
        for k in range(1, 4):
            count += jnp.sum(held[k, :, :8, :128].astype(F32), axis=0)
        count_ref[...] = count
        vec_ref[...] = spread([part[:8, :128] for part in own], shards)
        width = 2048 // shards
        lane = lax.broadcasted_iota(jnp.int32, (8, 128), 1)
        if width >= 128:
            for s in range(shards):
                eb_ref[:, s * width : (s + 1) * width] = own[s][8:16, :width]
        else:
            for tile in range(16):
                built = jnp.zeros((8, 128), F32)
                for k in range(128 // width):
                    part = own[tile * (128 // width) + k][8:16, :128]
                    moved = pltpu.roll(part, k * width, 1) if k else part
                    built = jnp.where((lane >= k * width) & (lane < (k + 1) * width), moved, built)
                eb_ref[:, tile * 128 : (tile + 1) * 128] = built
        pltpu.make_async_copy(w_ref, w_ref, sems.at[0]).wait()

    if quad == 0:
        pl.when(step == 0)(assemble)

    row_all = seg_ref[...].astype(F32)
    diagonal = block_diagonal()
    normal, _ = standardise(x_ref[...].astype(F32))
    normed = (normal * vec_ref[0:1, :] + vec_ref[1:2, :]).astype(BF16)
    q_ref[...] = nn(normed, weight(0)).astype(BF16)
    k_ref[...] = nn(normed, weight(1)).astype(BF16)
    v_ref[...] = nn(normed, weight(2)).astype(BF16)
    e_ref[...] = jnp.exp(nn(normed, weight(3))).astype(BF16)
    subs = range(CHUNK // SUB)
    spans = [slice(sub * SUB, (sub + 1) * SUB) for sub in subs]
    q, k, v, e = ([ref[rows] for rows in spans] for ref in (q_ref, k_ref, v_ref, e_ref))
    causal, causal_4, enters, one, two, totals = [], [], [], [], [], []
    first, second, running = first_state[...], second_state[...], total_state[0:1, :]
    for sub in subs:
        start = step * CHUNK + sub * SUB
        segment_last = seg_s[0, start + SUB - 1]
        segment_before = jnp.where(start == 0, -1, seg_s[0, jnp.maximum(start - 1, 0)])
        keep = jnp.where(segment_last == segment_before, 1.0, 0.0)
        row = row_all[:, spans[sub]]
        column = as_column(row, QUAD)
        causal.append(causal_mask(column, row))
        causal_4.append(four_times(causal[sub]))
        enters.append(jnp.where(column == segment_before.astype(F32), 1.0, 0.0))
        leaves = jnp.where(column == segment_last.astype(F32), 1.0, 0.0).astype(BF16)
        one.append(first.astype(BF16))
        two.append(second.astype(BF16))
        one_ref[sub] = one[sub]
        two_ref[sub] = two[sub]
        totals.append(nn(causal[sub], e[sub]) + enters[sub] * running)
        running = totals[sub][SUB - 1 : SUB, :]
        first = keep * first + diagonal * tn(k[sub] * leaves, e[sub])
        second = keep * second + diagonal * tn(e[sub] * leaves, v[sub])
    first_state[...] = first
    second_state[...] = second
    total_state[0:1, :] = running

    def each(function, *lists):
        return [function(*values) for values in zip(*lists)]

    def store(ref, values):
        for rows, value in zip(spans, values):
            ref[rows] = value

    inverse = each(lambda a: 1.0 / a, totals)
    store(rz_ref, inverse)
    e_stack = each(head_stack, e)
    scores = each(lambda a, b, c: nt(a, head_stack(b)).astype(BF16) * c, q, k, causal_4)
    gathered = each(
        lambda a, b, c, d, f: nn(a, b) + c * nn(d, f), scores, e_stack, enters, q, one
    )
    slot_scores = each(lambda a, b: a * (b * 0.125), gathered, inverse)
    raised = each(lambda a: jnp.exp(a - per_head(a, jnp.max, -jnp.inf)), slot_scores)
    shares = each(lambda a: a / per_head(a, jnp.sum, 0.0), raised)
    scaled = each(lambda a, b: (a * b).astype(BF16), shares, inverse)
    mixing = each(lambda a, b, c: nt(a, b).astype(BF16) * c, scaled, e_stack, causal_4)
    mixed = each(
        lambda a, b, c, d, f: nn(a, head_stack(b)) + c * nn(d, f), mixing, v, enters, scaled, two
    )
    store(s_ref, each(lambda a: a.astype(BF16), slot_scores))
    store(p_ref, each(lambda a: a.astype(BF16), shares))
    store(mix_ref, each(lambda a: a.astype(BF16), mixed))


def feed_forward(
    shards,
    tokens,
    x_ref,
    mix_0_ref,
    mix_1_ref,
    teacher_ref,
    valid_ref,
    vec_ref,
    eb_ref,
    count_ref,
    *refs,
):
    pieces, refs = (refs[:4], refs[4:8]), refs[8:]
    out_ref, hidden_ref, grad_mix_ref, keep_out_ref, send_out_ref = refs[:5]
    x, mix, teacher, wo, we, wc, act, out, hidden_grad, grad_mix = refs[5:15]
    keep_ref, send_ref, normed, low, d_normed, d_wo, d_we, d_wc, d_vec, d_eb, sems = refs[15:]
    r = 512 // shards
    me, core, cross = place()
    copies = [
        pltpu.make_async_copy(mix_0_ref, mix.at[:, pl.ds(0, QUAD)], sems.at[0]),
        pltpu.make_async_copy(mix_1_ref, mix.at[:, pl.ds(QUAD, QUAD)], sems.at[1]),
        pltpu.make_async_copy(x_ref, x, sems.at[2]),
        pltpu.make_async_copy(teacher_ref, teacher, sems.at[3]),
    ]
    sources = list(enumerate(pieces))
    columns = [pl.multiple_of(((core + half) % 2) * 256, 256) for half, _ in sources]
    for copy in copies[:2]:
        copy.start()
    for half, source in sources:
        for slot, (z, y, cross_slot) in enumerate(slots_of(shards)):
            pltpu.make_async_copy(
                block_of(source, slot).at[pl.ds(4 * r, r // 2)],
                wo.at[2 * (me ^ (2 * z + y)) + (cross ^ cross_slot), :, pl.ds(columns[half], 256)],
                sems.at[4],
            ).start()
    copies[2].start()
    for half, source in sources:
        for slot, (z, y, cross_slot) in enumerate(slots_of(shards)):
            owner = me ^ (2 * z + y)

            def expansion():
                for b in range(4):
                    pltpu.make_async_copy(
                        block_of(source, slot).at[pl.ds(b * r, r)],
                        we.at[
                            b, pl.ds(pl.multiple_of(owner * r, r), r), pl.ds(columns[half], 256)
                        ],
                        sems.at[5],
                    ).start()

            def contraction():
                pltpu.make_async_copy(
                    block_of(source, slot).at[pl.ds(0, 4 * r)],
                    wc.at[
                        pl.ds(pl.multiple_of(owner * 4 * r, 4 * r), 4 * r),
                        pl.ds(columns[half], 256),
                    ],
                    sems.at[6],
                ).start()

            pl.when((cross ^ cross_slot) == 0)(expansion)
            pl.when((cross ^ cross_slot) == 1)(contraction)
    copies[3].start()

    gain, shift, bias = vec_ref[2:3, :], vec_ref[3:4, :], vec_ref[4:5, :]
    copies[0].wait()
    copies[1].wait()
    pltpu.make_async_copy(wo, wo, sems.at[4]).wait()
    copies[2].wait()
    weight_out = wo[...].reshape(512, 512)
    hidden = x[...].astype(F32) + nn(mix[...], weight_out)
    normal, scale = standardise(hidden)
    normed[...] = (normal * gain + shift).astype(BF16)
    pltpu.make_async_copy(we, we, sems.at[5]).wait()
    for b in range(4):
        before = nn(normed[...], we[b]) + eb_ref[0:1, b * 512 : (b + 1) * 512]
        act[b] = jnp.maximum(before, 0.0).astype(BF16)
    pltpu.make_async_copy(wc, wc, sems.at[6]).wait()
    active = jnp.concatenate([act[b] for b in range(4)], axis=1)
    result = hidden + (nn(active, wc[...]) + bias)
    out[...] = result.astype(BF16)
    out_copy = pltpu.make_async_copy(out, out_ref, sems.at[7])
    out_copy.start()
    copies[3].wait()
    valid = as_column(valid_ref[...].astype(F32), 512)
    error = result - teacher[...].astype(F32)
    masked = valid * error
    loss = jnp.sum(masked * error)
    count = 256.0 * count_ref[6:7, 0:1] + count_ref[6:7, 1:2]
    grad_result = masked * (tokens / count)
    hidden_grad[...] = grad_result
    low[...] = grad_result.astype(BF16)
    d_normed[...] = jnp.zeros_like(d_normed)

    @pl.loop(0, 4)
    def _(b):
        at = pl.ds(pl.multiple_of(b * 512, 512), 512)
        d_wc[at, :] = tn(act[b], low[...]).astype(BF16)
        grad = jnp.where(act[b] > 0, nt(low[...], wc[at, :]), 0.0).astype(BF16)
        d_we[b] = tn(normed[...], grad).astype(BF16)
        d_eb[b, 0:1, :] = jnp.sum(grad.astype(F32), axis=0, keepdims=True)
        d_normed[...] += nt(grad, we[b])

    incoming = d_normed[...]
    hidden = x[...].astype(F32) + nn(mix[...], weight_out)
    normal, scale = standardise(hidden)
    d_vec[0:1, :] = jnp.sum(incoming * normal, axis=0, keepdims=True)
    d_vec[1:2, :] = jnp.sum(incoming, axis=0, keepdims=True)
    d_vec[2:3, :] = jnp.sum(low[...].astype(F32), axis=0, keepdims=True)
    d_vec[3:8, :] = jnp.zeros((5, 512), F32)
    grad_hidden = hidden_grad[...] + norm_backward(incoming, gain, normal, scale)
    hidden_grad[...] = grad_hidden
    hidden_copy = pltpu.make_async_copy(hidden_grad, hidden_ref, sems.at[8])
    hidden_copy.start()
    grad_low = grad_hidden.astype(BF16)
    grad_mix[...] = nt(grad_low, weight_out).astype(BF16)
    mix_copy = pltpu.make_async_copy(grad_mix, grad_mix_ref, sems.at[9])
    mix_copy.start()
    d_wo[...] = tn(mix[...], grad_low).astype(BF16)

    width = 2048 // shards
    digits = digits_of(jnp.zeros((8, 128), F32) + loss)
    _, rows = branch_rows(shards, keep_ref.shape[0])
    d_eb_all = jnp.concatenate([d_eb[b] for b in range(4)], axis=1)
    extra = []
    for s in range(shards):
        top = jnp.concatenate([piece_of(d_vec[...], s, r), digits], axis=1)
        if width >= 128:
            low_rows = d_eb_all[:, s * width : (s + 1) * width]
        else:
            low_rows = piece_of(d_eb_all, s, width)
        if low_rows.shape[1] < 256:
            pad = jnp.zeros((8, 256 - low_rows.shape[1]), F32)
            low_rows = jnp.concatenate([low_rows, pad], axis=1)
        extra.append(jnp.concatenate([top, low_rows], axis=0).astype(BF16))

    def write(ref, at, wanted):
        for s in range(shards):
            for name, done, part, offset, size in rows:
                if part != wanted:
                    continue
                if name == "contract":
                    value = d_wc[s * 4 * r + done : s * 4 * r + done + size, at]
                elif name == "output":
                    value = d_wo[s * r + done : s * r + done + size, at]
                elif name == "vectors":
                    value = extra[s][done : done + size]
                elif name == "none":
                    value = jnp.zeros((size, 256), BF16)
                else:
                    value = d_we[name, s * r + done : s * r + done + size, at]
                ref[part, s, offset : offset + size, :] = value

    left, right = slice(0, 256), slice(256, 512)
    reps = keep_ref.shape[0]
    flights = []
    for part in range(reps):

        @pl.when(core == 0)
        def _():
            write(send_ref, right, part)
            write(keep_ref, left, part)

        @pl.when(core == 1)
        def _():
            write(send_ref, left, part)
            write(keep_ref, right, part)

        for n, (source, target) in enumerate(
            ((send_ref, send_out_ref), (keep_ref, keep_out_ref))
        ):
            copy = pltpu.make_async_copy(
                source.at[part], target.at[part], sems.at[10 + 2 * part + n]
            )
            copy.start()
            flights.append(copy)
    for copy in [out_copy, hidden_copy, mix_copy, *flights]:
        copy.wait()


def attention_backward(shards, seg_s, x_ref, seg_ref, *refs):
    sides, refs = (refs[:9], refs[9:18]), refs[18:]
    g_ref, w_ref, vec_ref, hidden_ref, out_ref, keep_ref, send_ref = refs[:7]
    first_state, second_state, total_state, d_w, d_vec = refs[7:]
    step = pl.program_id(0)
    chunks = pl.num_programs(0)
    chunk = chunks - 1 - step
    r = 512 // shards
    me, core, cross = place()

    @pl.when(step == 0)
    def _():
        for ref in (first_state, second_state, total_state, d_w, d_vec):
            ref[...] = jnp.zeros_like(ref)

    length = chunks * BACK
    row_all = seg_ref[...].astype(F32)
    diagonal = block_diagonal()
    found = [[], []]
    for sub in reversed(range(BACK // SUB)):
        rows = slice(sub * SUB, (sub + 1) * SUB)
        start = chunk * BACK + sub * SUB
        segment_first = seg_s[0, start]
        segment_before = jnp.where(start == 0, -1, seg_s[0, jnp.maximum(start - 1, 0)])
        after_at = jnp.minimum(start + SUB, length - 1)
        segment_after = jnp.where(start + SUB == length, -1, seg_s[0, after_at])
        keep = jnp.where(segment_first == segment_after, 1.0, 0.0)
        row = row_all[:, rows]
        column = as_column(row, QUAD)
        causal_4 = four_times(causal_mask(column, row))
        turned = causal_mask_transposed(column, row)
        turned_4 = four_times(turned)
        enters = jnp.where(column == segment_before.astype(F32), 1.0, 0.0)
        goes_on = jnp.where(column == segment_after.astype(F32), 1.0, 0.0)
        opens = jnp.where(column == segment_first.astype(F32), 1.0, 0.0).astype(BF16)

        def both(function, *lists):
            return [function(*values) for values in zip(*lists)]

        q, k, v, e = ([side[n][rows] for side in sides] for n in range(4))
        grad = [g_ref[rows, g * QUAD : (g + 1) * QUAD] for g in range(2)]
        shares = [side[4][rows].astype(F32) for side in sides]
        slot_scores = [side[5][rows].astype(F32) for side in sides]
        inverse = [side[6][rows] for side in sides]
        one = [side[7][sub] for side in sides]
        two = [side[8][sub] for side in sides]
        scaled = both(lambda a, b: a * b, shares, inverse)
        scaled_low = [a.astype(BF16) for a in scaled]
        one_back = [first_state[g].astype(BF16) for g in range(2)]
        two_back = [second_state[g].astype(BF16) for g in range(2)]
        e_stack = both(head_stack, e)

        d_mixing = both(lambda a, b: nt(a, head_stack(b)).astype(BF16) * causal_4, grad, v)
        d_scaled = both(
            lambda a, b, c, d: nn(a, b) + enters * nt(c, d), d_mixing, e_stack, grad, two
        )
        q_stack, grad_stack = both(head_stack, q), both(head_stack, grad)
        scaled_stack = both(head_stack, scaled_low)
        mixing_t = both(lambda a, b: nt(a, b).astype(BF16) * turned_4, e, scaled_stack)
        d_mixing_t = both(lambda a, b: nt(a, b).astype(BF16) * turned_4, v, grad_stack)
        scores_t = both(lambda a, b: nt(a, b).astype(BF16) * turned_4, k, q_stack)
        d_shares = both(lambda a, b: a * b, d_scaled, inverse)
        product = both(lambda a, b: a * b, shares, d_shares)
        d_scores = both(lambda a, b: a - b * per_head(a, jnp.sum, 0.0), product, shares)
        d_low = both(lambda a, b: (a * b * 0.125).astype(BF16), d_scores, inverse)
        d_totals = both(
            lambda a, b, c, d, i: -(a * b + c * d) * i,
            d_scaled,
            scaled,
            d_scores,
            slot_scores,
            inverse,
        )
        d_values = both(
            lambda a, b, c, d: nn(a, b) + goes_on * nn(c, d), mixing_t, grad_stack, e, two_back
        )
        d_slots = both(nn, d_mixing_t, scaled_stack)
        d_low_stack = both(head_stack, d_low)
        d_raw = both(lambda a, b: nt(a, b).astype(BF16) * causal_4, d_low, e_stack)
        d_raw_t = both(lambda a, b: nt(a, b).astype(BF16) * turned_4, e, d_low_stack)
        d_slots = both(lambda a, b, c: a + nn(b, c), d_slots, scores_t, d_low_stack)
        d_queries = both(
            lambda a, b, c, d: nn(a, head_stack(b)) + enters * nt(c, d), d_raw, k, d_low, one
        )
        d_keys = both(
            lambda a, b, c, d: nn(a, b) + goes_on * nt(c, d), d_raw_t, q_stack, e, one_back
        )
        totals_low = [a.astype(BF16) for a in d_totals]
        rest = both(lambda a, b: (a - b.astype(F32)).astype(BF16), d_totals, totals_low)
        sums = [
            nn(turned, totals_low[g]) + nn(turned, rest[g]) + goes_on * total_state[g, 0:1, :]
            for g in range(2)
        ]
        d_slots = both(
            lambda a, b, c, d, f, h: a + goes_on * (nn(b, c) + nt(d, f)) + h,
            d_slots,
            k,
            one_back,
            v,
            two_back,
            sums,
        )
        d_control = both(lambda a, b: a * b.astype(F32), d_slots, e)
        for g in range(2):
            total_state[g, 0:1, :] = sums[g][0:1, :]
            first_state[g] = keep * first_state[g] + diagonal * tn(q[g] * opens, d_low[g])
            second_state[g] = keep * second_state[g] + diagonal * tn(
                scaled_low[g] * opens, grad[g]
            )
            parts = (d_queries[g], d_keys[g], d_values[g], d_control[g])
            found[g].append([part.astype(BF16) for part in parts])
    grads = [
        jnp.concatenate([part[m] for part in reversed(found[g])], axis=0)
        for g in range(2)
        for m in range(4)
    ]

    normal, scale = standardise(x_ref[...].astype(F32))
    gain = vec_ref[0:1, :]
    normed = (normal * gain + vec_ref[1:2, :]).astype(BF16)
    d_w[...] += tn(normed, jnp.concatenate(grads, axis=1))
    d_normed = sum(
        nt(jnp.concatenate([grads[m], grads[4 + m]], axis=1), w_ref[m]) for m in range(4)
    )
    d_vec[0:1, :] += jnp.sum(d_normed * normal, axis=0, keepdims=True)
    d_vec[1:2, :] += jnp.sum(d_normed, axis=0, keepdims=True)
    out_ref[...] = hidden_ref[...] + norm_backward(d_normed, gain, normal, scale)

    @pl.when(step == chunks - 1)
    def _():
        def write(ref, half):
            for s in range(shards):
                y, z = (me ^ s) & 1, (me ^ s) >> 1
                top = piece_of(d_vec[...], s, r)
                both_rows = jnp.concatenate([top, jnp.zeros_like(top)], axis=0).astype(BF16)
                for g in range(2):
                    for m in range(4):
                        x = cross ^ (m // 2)
                        lead = (g, x, y, z) if g else (g, y, x, z)
                        at = (4 * g + m) * QUAD + half * 128
                        part = d_w[s * r : (s + 1) * r, at : at + 128].astype(BF16)
                        ref[(*lead, slice((m % 2) * r, (m % 2 + 1) * r), slice(None))] = part
                    for x in range(2):
                        lead = (g, x, y, z) if g else (g, y, x, z)
                        ref[(*lead, slice(2 * r, 2 * r + 16), slice(None))] = both_rows

        @pl.when(core == 0)
        def _():
            write(keep_ref, 0)
            write(send_ref, 1)

        @pl.when(core == 1)
        def _():
            write(keep_ref, 1)
            write(send_ref, 0)


def whole(shape):
    return pl.BlockSpec(shape, lambda *_: (0,) * len(shape))


def anywhere():
    return pl.BlockSpec(memory_space=pl.ANY)


def shaped(shape, dtype):
    return jax.ShapeDtypeStruct(shape, dtype)


def params():
    return pltpu.CompilerParams(
        dimension_semantics=("arbitrary",), vmem_limit_bytes=VMEM_LIMIT
    )


def call_pack(shards, matrices, vectors, valid):
    r = 512 // shards
    operands = [*matrices, *[v.reshape(-1, min(128, v.shape[0])) for v in vectors], valid]
    mixer, branch = (2 * r + 16, 256), (4 * r + r // 2, 256)
    return pl.pallas_call(
        functools.partial(pack, shards),
        grid=(1,),
        in_specs=[whole(v.shape) for v in operands],
        out_specs=[whole(mixer), whole(branch)],
        out_shape=[shaped(mixer, BF16), shaped(branch, BF16)],
        compiler_params=params(),
        cost_estimate=COST,
        name="pack",
    )(*operands)


def call_forward(quad, shards, segments, x, operands, earlier):
    length = x.shape[0]
    chunks = length // CHUNK
    wide = pl.BlockSpec((CHUNK, 512), lambda c, *_: (c, 0))
    tile = pl.BlockSpec((CHUNK, QUAD), lambda c, *_: (c, 0))
    state = pl.BlockSpec((CHUNK // SUB, QUAD, QUAD), lambda c, *_: (c, 0, 0))
    low = shaped((length, QUAD), BF16)
    states = shaped((length // SUB, QUAD, QUAD), BF16)
    if quad == 0:
        in_specs = [anywhere()] * 8
        out_specs = [whole((4, 512, 512)), whole((8, 512)), whole((8, 2048)), whole((8, 128))]
        out_shape = [shaped((4, 512, 512), BF16), shaped((8, 512), F32)]
        out_shape += [shaped((8, 2048), F32), shaped((8, 128), F32)]
        first = [pltpu.VMEM((4, shards, 16, 256), BF16)]
        last = [pltpu.SemaphoreType.DMA((2,))]
    else:
        in_specs = [pl.BlockSpec((4, 512, QUAD), lambda c, *_: (0, 0, 1)), whole((8, 512))]
        out_specs, out_shape, first, last = [], [], [], []
    grid_spec = pltpu.PrefetchScalarGridSpec(
        num_scalar_prefetch=1,
        grid=(chunks,),
        in_specs=[wide, pl.BlockSpec((1, CHUNK), lambda c, *_: (0, c)), *in_specs]
        + [anywhere()] * len(earlier),
        out_specs=[tile] * 8 + [state] * 2 + out_specs,
        scratch_shapes=first
        + [
            pltpu.VMEM((QUAD, QUAD), F32),
            pltpu.VMEM((QUAD, QUAD), F32),
            pltpu.VMEM((8, QUAD), F32),
        ]
        + last,
    )
    return pl.pallas_call(
        functools.partial(
            ordered,
            functools.partial(attention_forward, quad, shards),
            3 + len(operands),
            len(earlier),
        ),
        grid_spec=grid_spec,
        out_shape=[low] * 6 + [shaped((length, QUAD), F32), low, states, states]
        + out_shape,
        compiler_params=params(),
        cost_estimate=COST,
        name=f"attention_forward_{quad}",
    )(segments, x, segments, *operands, *earlier)


def call_feed_forward(shards, reps, tokens, *operands):
    length = operands[0].shape[0]
    r = 512 // shards
    payload = (reps, shards, branch_rows(shards, reps)[0], 256)
    vmem = pl.BlockSpec(memory_space=pltpu.VMEM)
    wide = (length, 512)
    return pl.pallas_call(
        functools.partial(feed_forward, shards, tokens),
        in_specs=[anywhere()] * 4 + [vmem] * 4 + [anywhere()] * 8,
        out_specs=[anywhere()] * 5,
        out_shape=[
            shaped(wide, BF16),
            shaped(wide, F32),
            shaped(wide, BF16),
            shaped(payload, BF16),
            shaped(payload, BF16),
        ],
        scratch_shapes=[
            pltpu.VMEM(wide, BF16),
            pltpu.VMEM(wide, BF16),
            pltpu.VMEM(wide, BF16),
            pltpu.VMEM((2 * shards, r // 2, 512), BF16),
            pltpu.VMEM((4, 512, 512), BF16),
            pltpu.VMEM((2048, 512), BF16),
            pltpu.VMEM((4, length, 512), BF16),
            pltpu.VMEM(wide, BF16),
            pltpu.VMEM(wide, F32),
            pltpu.VMEM(wide, BF16),
            pltpu.VMEM(payload, BF16),
            pltpu.VMEM(payload, BF16),
            pltpu.VMEM(wide, BF16),
            pltpu.VMEM(wide, BF16),
            pltpu.VMEM(wide, F32),
            pltpu.VMEM((512, 512), BF16),
            pltpu.VMEM((4, 512, 512), BF16),
            pltpu.VMEM((2048, 512), BF16),
            pltpu.VMEM((8, 512), F32),
            pltpu.VMEM((4, 8, 512), F32),
            pltpu.SemaphoreType.DMA((10 + 2 * reps,)),
        ],
        compiler_params=pltpu.CompilerParams(vmem_limit_bytes=VMEM_LIMIT),
        cost_estimate=COST,
        name="feed_forward",
    )(*operands)


def call_backward(shards, segments, x, sides, operands, earlier):
    length = x.shape[0]
    chunks = length // BACK
    r = 512 // shards
    back = lambda c: chunks - 1 - c
    wide = pl.BlockSpec((BACK, 512), lambda c, *_: (back(c), 0))
    own = pl.BlockSpec((BACK, QUAD), lambda c, *_: (back(c), 0))
    state = pl.BlockSpec((BACK // SUB, QUAD, QUAD), lambda c, *_: (back(c), 0, 0))
    payload = (2, 2, 2, shards // 2, 2 * r + 16, 128)
    grid_spec = pltpu.PrefetchScalarGridSpec(
        num_scalar_prefetch=1,
        grid=(chunks,),
        in_specs=[
            wide,
            pl.BlockSpec((1, BACK), lambda c, *_: (0, back(c))),
            *([own] * 7 + [state] * 2) * 2,
            wide,
            whole((4, 512, 512)),
            whole((8, 512)),
            wide,
            *[anywhere()] * len(earlier),
        ],
        out_specs=[wide, whole(payload), whole(payload)],
        scratch_shapes=[
            pltpu.VMEM((2, QUAD, QUAD), F32),
            pltpu.VMEM((2, QUAD, QUAD), F32),
            pltpu.VMEM((2, 8, QUAD), F32),
            pltpu.VMEM((512, 8 * QUAD), F32),
            pltpu.VMEM((8, 512), F32),
        ],
    )
    return pl.pallas_call(
        functools.partial(
            ordered, functools.partial(attention_backward, shards), 25, len(earlier)
        ),
        grid_spec=grid_spec,
        out_shape=[shaped((length, 512), F32), shaped(payload, BF16), shaped(payload, BF16)],
        compiler_params=params(),
        cost_estimate=COST,
        name="attention_backward",
    )(segments, x, segments, *sides[0], *sides[1], *operands, *earlier)


def swap(value, axis, bit):
    n = lax.axis_size(axis)
    return lax.ppermute(value, axis, [(i, i ^ bit) for i in range(n)])


def bit_groups(shards):
    bits = shards.bit_length() - 1
    return [(low, min(2, bits - low)) for low in range(1, bits, 2)]


def branch_rows(shards, reps):
    r = 512 // shards
    piece = -(-(9 * r + 16) // (16 * reps)) * 16
    names = [("contract", 4 * r)] + [(b, r) for b in range(4)] + [("output", r), ("vectors", 16)]
    rows, at = [], 0
    for name, height in names + [("none", piece * reps - 9 * r - 16)]:
        done = 0
        while done < height:
            part, offset = divmod(at, piece)
            size = min(height - done, piece - offset)
            rows.append((name, done, part, offset, size))
            done += size
            at += size
    return piece, rows


def add_arrived(shards, *refs):
    source, target = refs[0], refs[-1]
    for half in range(2):
        total = 0.0
        for rep in range(half, source.shape[0], 2):
            for s in range(shards):
                total = total + source[rep, s].astype(F32)
        target[half] = total.astype(BF16)


def call_add_arrived(shards, arrived, *others):
    reps, _, piece, width = arrived.shape
    return pl.pallas_call(
        functools.partial(add_arrived, shards),
        in_specs=[pl.BlockSpec(memory_space=pltpu.VMEM)] + [anywhere()] * len(others),
        out_specs=pl.BlockSpec(memory_space=pltpu.VMEM),
        out_shape=shaped((2, piece, width), BF16),
        compiler_params=pltpu.CompilerParams(vmem_limit_bytes=VMEM_LIMIT),
        cost_estimate=COST,
        name="add_arrived",
    )(arrived, *others)


def zero_of(arrays):
    return sum(array[(0,) * array.ndim] for array in arrays) * jnp.zeros((), BF16)


def after(value, *others):
    return lax.optimization_barrier((value, *others))[0]


def quarters(refs):
    _, core, cross = place()

    def quarter(rows, half, third):
        parts = [ref[rows, :] for ref in refs]
        near = jnp.where(core == half, parts[0], parts[1])
        far = jnp.where(core == half, parts[2], parts[3])
        return jnp.where(cross == third, near, far).astype(F32)

    def both(rows, third):
        return jnp.concatenate([quarter(rows, half, third) for half in range(2)], axis=1)

    return both


def assemble_branch(shards, count_ref, *refs):
    held = refs[-1]
    reps = held.shape[0]
    me = lax.axis_index("rep")
    for a in range(reps):
        held[me ^ a] = refs[a][...]
    contract_ref, expand_ref, output_ref, bias_1_ref, bias_2_ref, gain_ref, shift_ref, loss_ref = (
        refs[reps:-1]
    )
    r = 512 // shards
    _, rows = branch_rows(shards, reps)
    vectors = []
    for name, done, part, offset, size in rows:
        value = jnp.concatenate(
            [held[part, half, offset : offset + size, :] for half in range(2)], axis=1
        ).astype(F32)
        if name == "contract":
            contract_ref[done : done + size, :] = value
        elif name == "output":
            output_ref[done : done + size, :] = value
        elif name == "vectors":
            vectors.append(value[:, :256])
        elif name != "none":
            expand_ref[done : done + size, name * 512 : (name + 1) * 512] = value
    vectors = vectors[0] if len(vectors) == 1 else jnp.concatenate(vectors, axis=0)
    bias_1_ref[...] = vectors[8:9, : 4 * r]
    gain_ref[...] = vectors[0:1, :r]
    shift_ref[...] = vectors[1:2, :r]
    bias_2_ref[...] = vectors[2:3, :r]
    lane = lax.broadcasted_iota(jnp.int32, (1, 128), 1)
    power = jnp.zeros((1, 128), F32)
    for k in range(LOSS_DIGITS):
        power = jnp.where(lane == k, 8.0 ** (k - LOSS_ZERO), power)
    total = jnp.sum(vectors[0:1, 128:256] * power, axis=1, keepdims=True)
    count = 256.0 * count_ref[6:7, 0:1] + count_ref[6:7, 1:2]
    loss_ref[...] = total / (2.0 * count)


def assemble_mixer(shards, *refs):
    both = quarters(refs[:4])
    gain_ref, shift_ref = refs[8:]
    r = 512 // shards
    for m, ref in enumerate(refs[4:8]):
        for quad in range(2):
            at = quad * (2 * r + 16) + (m % 2) * r
            ref[:, quad * 256 : (quad + 1) * 256] = both(slice(at, at + r), m // 2)
    vectors = both(slice(4 * r + 16, 4 * r + 32), 0)
    gain_ref[...] = vectors[0:1, :r]
    shift_ref[...] = vectors[1:2, :r]


def assemble_all(shards, reps, count_ref, *refs):
    parts_q, parts_f, refs = refs[:4], refs[4 : 4 + reps], refs[4 + reps :]
    assemble_mixer(shards, *parts_q, *refs[:6])
    assemble_branch(shards, count_ref, *parts_f, *refs[6:])


def assemble(shards, count, parts_q, parts_f):
    reps = len(parts_f)
    r = 512 // shards
    shapes = [(r, 512)] * 4 + [(1, r)] * 2
    shapes += [(4 * r, 512), (r, 2048), (r, 512), (1, 4 * r), (1, r), (1, r), (1, r), (1, 1)]
    return pl.pallas_call(
        functools.partial(assemble_all, shards, reps),
        in_specs=[pl.BlockSpec(memory_space=pltpu.VMEM)] * (5 + reps),
        out_specs=[pl.BlockSpec(memory_space=pltpu.VMEM)] * len(shapes),
        out_shape=[shaped(shape, F32) for shape in shapes],
        scratch_shapes=[pltpu.VMEM((reps, *parts_f[0].shape), BF16)],
        cost_estimate=COST,
        name="assemble",
    )(count, *parts_q, *parts_f)


def add_low(*parts):
    return sum(part.astype(F32) for part in parts).astype(BF16)


def local(
    inputs,
    segments,
    valid_mask,
    teacher,
    query_weight,
    key_weight,
    value_weight,
    control_weight,
    output_weight,
    gain_first,
    shift_first,
    expand_weight,
    expand_bias,
    contract_weight,
    contract_bias,
    gain_second,
    shift_second,
):
    _, length, width = inputs.shape
    shards, reps = lax.axis_size("shard"), lax.axis_size("rep")
    r = width // shards
    core = lax.axis_index("rep") % 2
    cross = (lax.axis_index("rep") // 2) % 2
    groups = bit_groups(shards)

    matrices = (query_weight, key_weight, value_weight, control_weight, output_weight)
    matrices += (expand_weight, contract_weight)
    biases = (gain_first, shift_first, gain_second, shift_second, contract_bias, expand_bias)
    mixer, branch = call_pack(shards, matrices, biases, valid_mask)

    def along_z(payload):
        held = [payload[None]]
        for low, bits in groups:
            if len(held) > 1:
                held = [jnp.concatenate(held, axis=0)]
            held += [swap(held[0], "shard", a << low) for a in range(1, 1 << bits)]
        return held

    def halves(held):
        if len(held) == 4:
            return jnp.concatenate(held[:2], axis=0), jnp.concatenate(held[2:], axis=0)
        joined = jnp.concatenate(held, axis=0)
        half = joined.shape[0] // 2
        return joined[:half], joined[half:]

    def step_one(first, second):
        return swap(first, "shard", 1), swap(second, "rep", 2)

    def join(first, second, arrived):
        return jnp.concatenate([first, arrived[0]]), jnp.concatenate([second, arrived[1]])

    def step_two(first, second):
        return swap(first, "rep", 2), swap(second, "shard", 1)

    first, second = halves(along_z(mixer))
    held_b = along_z(branch + zero_of([second]))
    first, second = join(first, second, step_one(first, second))
    arrived = step_two(first, second)
    first_b, second_b = halves(held_b)
    pending = step_one(first_b, second_b)
    last = arrived[1] + zero_of(held_b[1:])
    mine_a = (first, arrived[0], second, last)
    theirs_a = tuple(swap(part, "rep", 1) for part in mine_a)

    x = inputs.reshape(length, width)
    forward_0 = call_forward(
        0, shards, segments, x, (*mine_a, *theirs_a), (first_b, second_b)
    )
    weights, vectors, bias, count = forward_0[10:]
    bit = 4
    while bit < reps:
        count = count + swap(count, "rep", bit)
        bit *= 2
    pending = after(pending, forward_0[7])
    first_b, second_b = join(first_b, second_b, pending)
    pending = step_two(first_b, second_b)
    near_b = swap(first_b, "rep", 1), swap(second_b, "rep", 1)
    forward_1 = call_forward(
        1, shards, segments, x, (weights, vectors), (first_b, second_b, *near_b)
    )
    pending = after(pending, forward_1[7])
    mine_b = (first_b, pending[0], second_b, pending[1])
    theirs_b = (near_b[0], swap(pending[0], "rep", 1), near_b[1], swap(pending[1], "rep", 1))
    mixed = (forward_0[7], forward_1[7])

    layer_out, grad_hidden, grad_mix, keep_f, send_f = call_feed_forward(
        shards,
        reps,
        float(length * shards * reps),
        x,
        *mixed,
        teacher.reshape(length, width),
        valid_mask,
        vectors,
        bias,
        count,
        *mine_b,
        *theirs_b,
    )

    def split(parts):
        return add_low(*(part[0] for part in parts)), add_low(*(part[1] for part in parts))

    def cross_first(parts):
        keep, send = split(parts)
        return keep, swap(send, "rep", 2)

    def row_first(parts):
        keep, send = split(parts)
        return keep, swap(send, "shard", 1)

    def z_stage(parts_list):
        current = parts_list
        for low, bits in reversed(groups):
            span = 1 << (low - 1)
            pieces = [
                jnp.concatenate(
                    [
                        add_low(*(part[a * span : (a + 1) * span] for part in parts))
                        for parts in current
                    ],
                    axis=1,
                )
                for a in range(1 << bits)
            ]
            arrived = [swap(pieces[a], "shard", a << low) for a in range(1, 1 << bits)]
            current = [(pieces[0], *arrived)]
        return current[0]

    def finish(parts):
        total = add_low(*(part[0] for part in parts))
        bit = 4
        while bit < reps:
            total = add_low(total, swap(total, "rep", bit))
            bit *= 2
        return [total] + [swap(total, "rep", a) for a in range(1, 4)]

    summed = add_low(keep_f, swap(send_f, "rep", 1))
    every = summed.reshape(reps * shards, *summed.shape[2:])
    arrived_f = lax.all_to_all(every, ("rep", "shard"), 0, 0).reshape(summed.shape)
    sides = [(*saved[:7], *saved[8:10]) for saved in (forward_0, forward_1)]
    grad_inputs, keep_q, send_q = call_backward(
        shards, segments, x, sides, (grad_mix, weights, vectors, grad_hidden), (every,)
    )
    late_q = swap(send_q, "rep", 1)
    parts_0, parts_1 = row_first((keep_q[0], late_q[0])), cross_first((keep_q[1], late_q[1]))
    parts_0, parts_1 = cross_first(parts_0), row_first(parts_1)
    q_pieces = z_stage([parts_0, parts_1])
    total_f = call_add_arrived(shards, arrived_f, q_pieces[0])
    parts_f = [total_f] + [swap(total_f, "rep", a) for a in range(1, reps)]
    parts_q = finish(q_pieces)
    results = assemble(shards, count, parts_q, parts_f)
    mats, (gain_1, shift_1) = results[:4], results[4:6]
    grad_contract, grad_expand, grad_output, bias_1, bias_2, gain_2, shift_2, loss = results[6:]
    return (
        layer_out.reshape(inputs.shape),
        grad_inputs.reshape(inputs.shape),
        loss.reshape(()),
        *mats,
        grad_output,
        gain_1.reshape(r),
        shift_1.reshape(r),
        grad_expand,
        bias_1.reshape(4 * r),
        grad_contract,
        bias_2.reshape(r),
        gain_2.reshape(r),
        shift_2.reshape(r),
    )


def solution(mesh):
    every = P(("rep", "shard"), None, None)
    every_row = P(("rep", "shard"), None)
    matrix, vector = P("shard", None), P("shard")
    in_specs = (
        every,
        every_row,
        every_row,
        every,
        *[matrix] * 5,
        *[vector] * 2,
        matrix,
        vector,
        matrix,
        *[vector] * 3,
    )
    out_specs = (
        every,
        every,
        P(),
        *[matrix] * 5,
        *[vector] * 2,
        matrix,
        vector,
        matrix,
        *[vector] * 3,
    )
    return jax.shard_map(local, mesh=mesh, in_specs=in_specs, out_specs=out_specs, check_vma=False)
```

```python
import functools

import jax
import jax.numpy as jnp
from jax import lax
from jax.experimental import pallas as pl
from jax.experimental.pallas import tpu as pltpu
from jax.sharding import PartitionSpec as P

HEADS = 8
EPSILON = 1e-05
CHUNK = 256
SUB = 128
BACK = 512
QUAD = 256
F32 = jnp.float32
BF16 = jnp.bfloat16
VMEM_LIMIT = 60 << 20
LOSS_DIGITS = 30
LOSS_ZERO = 10
COST = pl.CostEstimate(flops=1000, bytes_accessed=1000, transcendentals=0)


def ordered(kernel, at, count, *refs):
    kernel(*refs[:at], *refs[at + count :])


def place():
    rep = lax.axis_index("rep")
    return lax.axis_index("shard"), rep % 2, (rep // 2) % 2


def slots_of(shards):
    ways = shards // 2
    low, high = range(ways // 2), range(ways // 2, ways)
    first = [(z, y, x) for x in (0, 1) for y in (0, 1) for z in low]
    second = [(z, y, x) for y in (0, 1) for x in (0, 1) for z in high]
    return first + second


def block_of(pieces, slot):
    each = pieces[0].shape[0]
    return pieces[slot // each].at[slot % each]


def nn(left, right):
    return jnp.dot(left, right, preferred_element_type=F32)


def nt(left, right):
    return lax.dot_general(left, right, (((1,), (1,)), ((), ())), preferred_element_type=F32)


def tn(left, right):
    return lax.dot_general(left, right, (((0,), (0,)), ((), ())), preferred_element_type=F32)


def head_lanes():
    lane = lax.broadcasted_iota(jnp.int32, (1, QUAD), 1) // 64
    return [jnp.where(lane == h, 1.0, 0.0).astype(BF16) for h in range(4)]


def block_diagonal():
    rows = lax.broadcasted_iota(jnp.int32, (QUAD, QUAD), 0) // 64
    columns = lax.broadcasted_iota(jnp.int32, (QUAD, QUAD), 1) // 64
    return jnp.where(rows == columns, 1.0, 0.0)


def as_column(row, width):
    tile = jnp.broadcast_to(row, (128, row.shape[1])).T
    return jnp.concatenate([tile] * (width // 128), axis=1)


def causal_mask(column, row):
    at = lax.broadcasted_iota(jnp.int32, (SUB, SUB), 0)
    source = lax.broadcasted_iota(jnp.int32, (SUB, SUB), 1)
    return jnp.where((column[:, :SUB] == row) & (source <= at), 1.0, 0.0).astype(BF16)


def causal_mask_transposed(column, row):
    source = lax.broadcasted_iota(jnp.int32, (SUB, SUB), 0)
    at = lax.broadcasted_iota(jnp.int32, (SUB, SUB), 1)
    return jnp.where((column[:, :SUB] == row) & (source <= at), 1.0, 0.0).astype(BF16)


def head_stack(values):
    return jnp.concatenate([values * lanes for lanes in head_lanes()], axis=0)


def four_times(mask):
    return jnp.concatenate([mask] * 4, axis=1)


def per_head(values, reduce, fill):
    lane = lax.broadcasted_iota(jnp.int32, (1, 128), 1)
    first = lane < 64
    tiles = []
    for tile in range(values.shape[1] // 128):
        part = values[:, tile * 128 : (tile + 1) * 128]
        one = reduce(jnp.where(first, part, fill), axis=-1, keepdims=True)
        two = reduce(jnp.where(first, fill, part), axis=-1, keepdims=True)
        tiles.append(jnp.where(first, one, two))
    return jnp.concatenate(tiles, axis=1)


def standardise(values):
    mean = jnp.mean(values, axis=-1, keepdims=True)
    centred = values - mean
    variance = jnp.mean(centred * centred, axis=-1, keepdims=True)
    scale = lax.rsqrt(variance + EPSILON)
    return centred * scale, scale


def norm_backward(gradient, gain, normal, scale):
    upstream = gradient * gain
    one = jnp.mean(upstream, axis=-1, keepdims=True)
    two = jnp.mean(upstream * normal, axis=-1, keepdims=True)
    return (upstream - one - normal * two) * scale


def spread(rows, shards):
    width = 512 // shards
    lane = lax.broadcasted_iota(jnp.int32, (8, 128), 1)
    tiles = [None] * 4
    for s in range(shards):
        tile, offset = divmod(s * width, 128)
        moved = pltpu.roll(rows[s], offset, 1) if offset else rows[s]
        inside = (lane >= offset) & (lane < offset + width)
        tiles[tile] = jnp.where(inside, moved, 0.0 if tiles[tile] is None else tiles[tile])
    return jnp.concatenate(tiles, axis=1)


def digits_of(value):
    lane = lax.broadcasted_iota(jnp.int32, (8, 128), 1)
    scale = jnp.zeros((8, 128), F32)
    for k in range(LOSS_DIGITS):
        scale = jnp.where(lane == k, 8.0 ** (LOSS_ZERO - k), scale)
    shifted = value * scale
    return jnp.floor(shifted) - 8.0 * jnp.floor(shifted * 0.125)


def piece_of(vectors, s, width):
    tile, offset = divmod(s * width, 128)
    part = vectors[:, tile * 128 : (tile + 1) * 128]
    return pltpu.roll(part, 128 - offset, 1) if offset else part


def pack(shards, *refs):
    query, key, value, control, output, expand, contract = refs[:7]
    gain_1, shift_1, gain_2, shift_2, bias_2, bias_1, valid = refs[7:14]
    mixer_ref, branch_ref = refs[14:]
    r = 512 // shards
    _, core, cross = place()

    def write(half, third):
        at = slice(half * 256, half * 256 + 256)
        for m, ref in enumerate(((query, key), (value, control))[third]):
            mixer_ref[m * r : (m + 1) * r] = ref[:, at]
        if third == 0:
            for b in range(4):
                part = expand[:, b * 512 + half * 256 : b * 512 + half * 256 + 256]
                branch_ref[b * r : (b + 1) * r] = part
        else:
            branch_ref[0 : 4 * r] = contract[:, at]
        branch_ref[4 * r : 4 * r + r // 2] = output[third * (r // 2) : (third + 1) * (r // 2), at]

    for half in range(2):
        for third in range(2):
            pl.when((core == half) & (cross == third))(functools.partial(write, half, third))

    row = lax.broadcasted_iota(jnp.int32, (16, 256), 0)
    lane = lax.broadcasted_iota(jnp.int32, (16, 256), 1)
    block = jnp.zeros((16, 256), F32)
    for k, ref in ((0, gain_1), (1, shift_1), (2, gain_2), (3, shift_2), (4, bias_2), (8, bias_1)):
        part = ref[...].astype(F32)
        part = jnp.concatenate([part[n : n + 1] for n in range(part.shape[0])], axis=1)
        width = part.shape[1]
        if width < 256:
            part = jnp.concatenate([part, jnp.zeros((1, 256 - width), F32)], axis=1)
        block = jnp.where(row == k, part, block)
    count = jnp.sum(valid[...].astype(F32))
    high = jnp.floor(count / 256.0)
    block = jnp.where((row == 6) & (lane == 0), high, block)
    block = jnp.where((row == 6) & (lane == 1), count - 256.0 * high, block)
    mixer_ref[2 * r : 2 * r + 16] = block.astype(BF16)


def attention_forward(quad, shards, seg_s, x_ref, seg_ref, *refs):
    step = pl.program_id(0)
    r = 512 // shards
    at = slice(quad * QUAD, (quad + 1) * QUAD)
    if quad == 0:
        pieces, refs = (refs[:4], refs[4:8]), refs[8:]
        q_ref, k_ref, v_ref, e_ref, p_ref, s_ref, rz_ref, mix_ref, one_ref, two_ref = refs[:10]
        w_ref, vec_ref, eb_ref, count_ref = refs[10:14]
        held, first_state, second_state, total_state, sems = refs[14:]
        weight = lambda m: w_ref[m, :, at]
    else:
        w_ref, vec_ref = refs[:2]
        q_ref, k_ref, v_ref, e_ref, p_ref, s_ref, rz_ref, mix_ref, one_ref, two_ref = refs[2:12]
        first_state, second_state, total_state = refs[12:]
        weight = lambda m: w_ref[m]

    @pl.when(step == 0)
    def _():
        first_state[...] = jnp.zeros_like(first_state)
        second_state[...] = jnp.zeros_like(second_state)
        total_state[...] = jnp.zeros_like(total_state)

    def assemble():
        me, core, cross = place()
        for half, source in enumerate(pieces):
            column = pl.multiple_of(((core + half) % 2) * 256, 256)
            for slot, (z, y, x) in enumerate(slots_of(shards)):
                owner = me ^ (2 * z + y)
                third = cross ^ x
                for m in range(2):
                    pltpu.make_async_copy(
                        block_of(source, slot).at[pl.ds(m * r, r)],
                        w_ref.at[
                            2 * third + m,
                            pl.ds(pl.multiple_of(owner * r, r), r),
                            pl.ds(column, 256),
                        ],
                        sems.at[0],
                    ).start()
                pltpu.make_async_copy(
                    block_of(source, slot).at[pl.ds(2 * r, 16)], held.at[2 * half + x, owner], sems.at[1]
                ).start()
        pltpu.make_async_copy(held, held, sems.at[1]).wait()
        own = [held[0, s].astype(F32) for s in range(shards)]
        count = sum(part[:8, :128] for part in own)
        for k in range(1, 4):
            count += jnp.sum(held[k, :, :8, :128].astype(F32), axis=0)
        count_ref[...] = count
        vec_ref[...] = spread([part[:8, :128] for part in own], shards)
        width = 2048 // shards
        lane = lax.broadcasted_iota(jnp.int32, (8, 128), 1)
        if width >= 128:
            for s in range(shards):
                eb_ref[:, s * width : (s + 1) * width] = own[s][8:16, :width]
        else:
            for tile in range(16):
                built = jnp.zeros((8, 128), F32)
                for k in range(128 // width):
                    part = own[tile * (128 // width) + k][8:16, :128]
                    moved = pltpu.roll(part, k * width, 1) if k else part
                    built = jnp.where((lane >= k * width) & (lane < (k + 1) * width), moved, built)
                eb_ref[:, tile * 128 : (tile + 1) * 128] = built
        pltpu.make_async_copy(w_ref, w_ref, sems.at[0]).wait()

    if quad == 0:
        pl.when(step == 0)(assemble)

    row_all = seg_ref[...].astype(F32)
    diagonal = block_diagonal()
    normal, _ = standardise(x_ref[...].astype(F32))
    normed = (normal * vec_ref[0:1, :] + vec_ref[1:2, :]).astype(BF16)
    q_ref[...] = nn(normed, weight(0)).astype(BF16)
    k_ref[...] = nn(normed, weight(1)).astype(BF16)
    v_ref[...] = nn(normed, weight(2)).astype(BF16)
    e_ref[...] = jnp.exp(nn(normed, weight(3))).astype(BF16)
    subs = range(CHUNK // SUB)
    spans = [slice(sub * SUB, (sub + 1) * SUB) for sub in subs]
    q, k, v, e = ([ref[rows] for rows in spans] for ref in (q_ref, k_ref, v_ref, e_ref))
    causal, causal_4, enters, one, two, totals = [], [], [], [], [], []
    first, second, running = first_state[...], second_state[...], total_state[0:1, :]
    for sub in subs:
        start = step * CHUNK + sub * SUB
        segment_last = seg_s[0, start + SUB - 1]
        segment_before = jnp.where(start == 0, -1, seg_s[0, jnp.maximum(start - 1, 0)])
        keep = jnp.where(segment_last == segment_before, 1.0, 0.0)
        row = row_all[:, spans[sub]]
        column = as_column(row, QUAD)
        causal.append(causal_mask(column, row))
        causal_4.append(four_times(causal[sub]))
        enters.append(jnp.where(column == segment_before.astype(F32), 1.0, 0.0))
        leaves = jnp.where(column == segment_last.astype(F32), 1.0, 0.0).astype(BF16)
        one.append(first.astype(BF16))
        two.append(second.astype(BF16))
        one_ref[sub] = one[sub]
        two_ref[sub] = two[sub]
        totals.append(nn(causal[sub], e[sub]) + enters[sub] * running)
        running = totals[sub][SUB - 1 : SUB, :]
        first = keep * first + diagonal * tn(k[sub] * leaves, e[sub])
        second = keep * second + diagonal * tn(e[sub] * leaves, v[sub])
    first_state[...] = first
    second_state[...] = second
    total_state[0:1, :] = running

    def each(function, *lists):
        return [function(*values) for values in zip(*lists)]

    def store(ref, values):
        for rows, value in zip(spans, values):
            ref[rows] = value

    inverse = each(lambda a: 1.0 / a, totals)
    store(rz_ref, inverse)
    e_stack = each(head_stack, e)
    scores = each(lambda a, b, c: nt(a, head_stack(b)).astype(BF16) * c, q, k, causal_4)
    gathered = each(
        lambda a, b, c, d, f: nn(a, b) + c * nn(d, f), scores, e_stack, enters, q, one
    )
    slot_scores = each(lambda a, b: a * (b * 0.125), gathered, inverse)
    raised = each(lambda a: jnp.exp(a - per_head(a, jnp.max, -jnp.inf)), slot_scores)
    shares = each(lambda a: a / per_head(a, jnp.sum, 0.0), raised)
    scaled = each(lambda a, b: (a * b).astype(BF16), shares, inverse)
    mixing = each(lambda a, b, c: nt(a, b).astype(BF16) * c, scaled, e_stack, causal_4)
    mixed = each(
        lambda a, b, c, d, f: nn(a, head_stack(b)) + c * nn(d, f), mixing, v, enters, scaled, two
    )
    store(s_ref, each(lambda a: a.astype(BF16), slot_scores))
    store(p_ref, each(lambda a: a.astype(BF16), shares))
    store(mix_ref, each(lambda a: a.astype(BF16), mixed))


def feed_forward(
    shards,
    tokens,
    x_ref,
    mix_0_ref,
    mix_1_ref,
    teacher_ref,
    valid_ref,
    vec_ref,
    eb_ref,
    count_ref,
    *refs,
):
    pieces, refs = (refs[:4], refs[4:8]), refs[8:]
    out_ref, hidden_ref, grad_mix_ref, keep_out_ref, *sends = refs[:6]
    x, mix, teacher, wo, we, wc, act, out, hidden_grad, grad_mix = refs[6:16]
    keep_ref, send_ref, normed, low, d_normed, d_wo, d_we, d_wc, d_vec, d_eb, sems = refs[16:]
    r = 512 // shards
    me, core, cross = place()
    copies = [
        pltpu.make_async_copy(mix_0_ref, mix.at[:, pl.ds(0, QUAD)], sems.at[0]),
        pltpu.make_async_copy(mix_1_ref, mix.at[:, pl.ds(QUAD, QUAD)], sems.at[1]),
        pltpu.make_async_copy(x_ref, x, sems.at[2]),
        pltpu.make_async_copy(teacher_ref, teacher, sems.at[3]),
    ]
    sources = list(enumerate(pieces))
    columns = [pl.multiple_of(((core + half) % 2) * 256, 256) for half, _ in sources]
    for copy in copies[:2]:
        copy.start()
    for half, source in sources:
        for slot, (z, y, cross_slot) in enumerate(slots_of(shards)):
            pltpu.make_async_copy(
                block_of(source, slot).at[pl.ds(4 * r, r // 2)],
                wo.at[2 * (me ^ (2 * z + y)) + (cross ^ cross_slot), :, pl.ds(columns[half], 256)],
                sems.at[4],
            ).start()
    copies[2].start()
    for half, source in sources:
        for slot, (z, y, cross_slot) in enumerate(slots_of(shards)):
            owner = me ^ (2 * z + y)

            def expansion():
                for b in range(4):
                    pltpu.make_async_copy(
                        block_of(source, slot).at[pl.ds(b * r, r)],
                        we.at[
                            b, pl.ds(pl.multiple_of(owner * r, r), r), pl.ds(columns[half], 256)
                        ],
                        sems.at[5],
                    ).start()

            def contraction():
                pltpu.make_async_copy(
                    block_of(source, slot).at[pl.ds(0, 4 * r)],
                    wc.at[
                        pl.ds(pl.multiple_of(owner * 4 * r, 4 * r), 4 * r),
                        pl.ds(columns[half], 256),
                    ],
                    sems.at[6],
                ).start()

            pl.when((cross ^ cross_slot) == 0)(expansion)
            pl.when((cross ^ cross_slot) == 1)(contraction)
    copies[3].start()

    gain, shift, bias = vec_ref[2:3, :], vec_ref[3:4, :], vec_ref[4:5, :]
    copies[0].wait()
    copies[1].wait()
    pltpu.make_async_copy(wo, wo, sems.at[4]).wait()
    copies[2].wait()
    weight_out = wo[...].reshape(512, 512)
    hidden = x[...].astype(F32) + nn(mix[...], weight_out)
    normal, scale = standardise(hidden)
    normed[...] = (normal * gain + shift).astype(BF16)
    pltpu.make_async_copy(we, we, sems.at[5]).wait()
    for b in range(4):
        before = nn(normed[...], we[b]) + eb_ref[0:1, b * 512 : (b + 1) * 512]
        act[b] = jnp.maximum(before, 0.0).astype(BF16)
    pltpu.make_async_copy(wc, wc, sems.at[6]).wait()
    active = jnp.concatenate([act[b] for b in range(4)], axis=1)
    result = hidden + (nn(active, wc[...]) + bias)
    out[...] = result.astype(BF16)
    out_copy = pltpu.make_async_copy(out, out_ref, sems.at[7])
    out_copy.start()
    copies[3].wait()
    valid = as_column(valid_ref[...].astype(F32), 512)
    error = result - teacher[...].astype(F32)
    masked = valid * error
    loss = jnp.sum(masked * error)
    count = 256.0 * count_ref[6:7, 0:1] + count_ref[6:7, 1:2]
    grad_result = masked * (tokens / count)
    hidden_grad[...] = grad_result
    low[...] = grad_result.astype(BF16)
    d_normed[...] = jnp.zeros_like(d_normed)

    @pl.loop(0, 4)
    def _(b):
        at = pl.ds(pl.multiple_of(b * 512, 512), 512)
        d_wc[at, :] = tn(act[b], low[...]).astype(BF16)
        grad = jnp.where(act[b] > 0, nt(low[...], wc[at, :]), 0.0).astype(BF16)
        d_we[b] = tn(normed[...], grad).astype(BF16)
        d_eb[b, 0:1, :] = jnp.sum(grad.astype(F32), axis=0, keepdims=True)
        d_normed[...] += nt(grad, we[b])

    incoming = d_normed[...]
    hidden = x[...].astype(F32) + nn(mix[...], weight_out)
    normal, scale = standardise(hidden)
    d_vec[0:1, :] = jnp.sum(incoming * normal, axis=0, keepdims=True)
    d_vec[1:2, :] = jnp.sum(incoming, axis=0, keepdims=True)
    d_vec[2:3, :] = jnp.sum(low[...].astype(F32), axis=0, keepdims=True)
    d_vec[3:8, :] = jnp.zeros((5, 512), F32)
    grad_hidden = hidden_grad[...] + norm_backward(incoming, gain, normal, scale)
    hidden_grad[...] = grad_hidden
    hidden_copy = pltpu.make_async_copy(hidden_grad, hidden_ref, sems.at[8])
    hidden_copy.start()
    grad_low = grad_hidden.astype(BF16)
    grad_mix[...] = nt(grad_low, weight_out).astype(BF16)
    mix_copy = pltpu.make_async_copy(grad_mix, grad_mix_ref, sems.at[9])
    mix_copy.start()
    d_wo[...] = tn(mix[...], grad_low).astype(BF16)

    width = 2048 // shards
    digits = digits_of(jnp.zeros((8, 128), F32) + loss)
    _, rows = branch_rows(shards, keep_ref.shape[0])
    d_eb_all = jnp.concatenate([d_eb[b] for b in range(4)], axis=1)
    extra = []
    for s in range(shards):
        top = jnp.concatenate([piece_of(d_vec[...], s, r), digits], axis=1)
        if width >= 128:
            low_rows = d_eb_all[:, s * width : (s + 1) * width]
        else:
            low_rows = piece_of(d_eb_all, s, width)
        if low_rows.shape[1] < 256:
            pad = jnp.zeros((8, 256 - low_rows.shape[1]), F32)
            low_rows = jnp.concatenate([low_rows, pad], axis=1)
        extra.append(jnp.concatenate([top, low_rows], axis=0).astype(BF16))

    def write(ref, at, wanted):
        for s in range(shards):
            for name, done, part, offset, size in rows:
                if part != wanted:
                    continue
                if name == "contract":
                    value = d_wc[s * 4 * r + done : s * 4 * r + done + size, at]
                elif name == "output":
                    value = d_wo[s * r + done : s * r + done + size, at]
                elif name == "vectors":
                    value = extra[s][done : done + size]
                elif name == "none":
                    value = jnp.zeros((size, 256), BF16)
                else:
                    value = d_we[name, s * r + done : s * r + done + size, at]
                ref[part, s, offset : offset + size, :] = value

    left, right = slice(0, 256), slice(256, 512)
    reps = keep_ref.shape[0]
    flights = []
    for part in range(reps):

        @pl.when(core == 0)
        def _():
            write(send_ref, right, part)
            write(keep_ref, left, part)

        @pl.when(core == 1)
        def _():
            write(send_ref, left, part)
            write(keep_ref, right, part)

        for n, (source, target) in enumerate(
            (
                (send_ref, sends[2 * part // reps].at[part % (reps // 2)]),
                (keep_ref, keep_out_ref.at[part]),
            )
        ):
            copy = pltpu.make_async_copy(source.at[part], target, sems.at[10 + 2 * part + n])
            copy.start()
            flights.append(copy)
    for copy in [out_copy, hidden_copy, mix_copy, *flights]:
        copy.wait()


def attention_backward(shards, seg_s, x_ref, seg_ref, *refs):
    sides, refs = (refs[:9], refs[9:18]), refs[18:]
    g_ref, w_ref, vec_ref, hidden_ref, out_ref, keep_ref, send_ref = refs[:7]
    first_state, second_state, total_state, d_w, d_vec = refs[7:]
    step = pl.program_id(0)
    chunks = pl.num_programs(0)
    chunk = chunks - 1 - step
    r = 512 // shards
    me, core, cross = place()

    @pl.when(step == 0)
    def _():
        for ref in (first_state, second_state, total_state, d_w, d_vec):
            ref[...] = jnp.zeros_like(ref)

    length = chunks * BACK
    row_all = seg_ref[...].astype(F32)
    diagonal = block_diagonal()
    found = [[], []]
    for sub in reversed(range(BACK // SUB)):
        rows = slice(sub * SUB, (sub + 1) * SUB)
        start = chunk * BACK + sub * SUB
        segment_first = seg_s[0, start]
        segment_before = jnp.where(start == 0, -1, seg_s[0, jnp.maximum(start - 1, 0)])
        after_at = jnp.minimum(start + SUB, length - 1)
        segment_after = jnp.where(start + SUB == length, -1, seg_s[0, after_at])
        keep = jnp.where(segment_first == segment_after, 1.0, 0.0)
        row = row_all[:, rows]
        column = as_column(row, QUAD)
        causal_4 = four_times(causal_mask(column, row))
        turned = causal_mask_transposed(column, row)
        turned_4 = four_times(turned)
        enters = jnp.where(column == segment_before.astype(F32), 1.0, 0.0)
        goes_on = jnp.where(column == segment_after.astype(F32), 1.0, 0.0)
        opens = jnp.where(column == segment_first.astype(F32), 1.0, 0.0).astype(BF16)

        def both(function, *lists):
            return [function(*values) for values in zip(*lists)]

        q, k, v, e = ([side[n][rows] for side in sides] for n in range(4))
        grad = [g_ref[rows, g * QUAD : (g + 1) * QUAD] for g in range(2)]
        shares = [side[4][rows].astype(F32) for side in sides]
        slot_scores = [side[5][rows].astype(F32) for side in sides]
        inverse = [side[6][rows] for side in sides]
        one = [side[7][sub] for side in sides]
        two = [side[8][sub] for side in sides]
        scaled = both(lambda a, b: a * b, shares, inverse)
        scaled_low = [a.astype(BF16) for a in scaled]
        one_back = [first_state[g].astype(BF16) for g in range(2)]
        two_back = [second_state[g].astype(BF16) for g in range(2)]
        e_stack = both(head_stack, e)

        d_mixing = both(lambda a, b: nt(a, head_stack(b)).astype(BF16) * causal_4, grad, v)
        d_scaled = both(
            lambda a, b, c, d: nn(a, b) + enters * nt(c, d), d_mixing, e_stack, grad, two
        )
        q_stack, grad_stack = both(head_stack, q), both(head_stack, grad)
        scaled_stack = both(head_stack, scaled_low)
        mixing_t = both(lambda a, b: nt(a, b).astype(BF16) * turned_4, e, scaled_stack)
        d_mixing_t = both(lambda a, b: nt(a, b).astype(BF16) * turned_4, v, grad_stack)
        scores_t = both(lambda a, b: nt(a, b).astype(BF16) * turned_4, k, q_stack)
        d_shares = both(lambda a, b: a * b, d_scaled, inverse)
        product = both(lambda a, b: a * b, shares, d_shares)
        d_scores = both(lambda a, b: a - b * per_head(a, jnp.sum, 0.0), product, shares)
        d_low = both(lambda a, b: (a * b * 0.125).astype(BF16), d_scores, inverse)
        d_totals = both(
            lambda a, b, c, d, i: -(a * b + c * d) * i,
            d_scaled,
            scaled,
            d_scores,
            slot_scores,
            inverse,
        )
        d_values = both(
            lambda a, b, c, d: nn(a, b) + goes_on * nn(c, d), mixing_t, grad_stack, e, two_back
        )
        d_slots = both(nn, d_mixing_t, scaled_stack)
        d_low_stack = both(head_stack, d_low)
        d_raw = both(lambda a, b: nt(a, b).astype(BF16) * causal_4, d_low, e_stack)
        d_raw_t = both(lambda a, b: nt(a, b).astype(BF16) * turned_4, e, d_low_stack)
        d_slots = both(lambda a, b, c: a + nn(b, c), d_slots, scores_t, d_low_stack)
        d_queries = both(
            lambda a, b, c, d: nn(a, head_stack(b)) + enters * nt(c, d), d_raw, k, d_low, one
        )
        d_keys = both(
            lambda a, b, c, d: nn(a, b) + goes_on * nt(c, d), d_raw_t, q_stack, e, one_back
        )
        totals_low = [a.astype(BF16) for a in d_totals]
        rest = both(lambda a, b: (a - b.astype(F32)).astype(BF16), d_totals, totals_low)
        sums = [
            nn(turned, totals_low[g]) + nn(turned, rest[g]) + goes_on * total_state[g, 0:1, :]
            for g in range(2)
        ]
        d_slots = both(
            lambda a, b, c, d, f, h: a + goes_on * (nn(b, c) + nt(d, f)) + h,
            d_slots,
            k,
            one_back,
            v,
            two_back,
            sums,
        )
        d_control = both(lambda a, b: a * b.astype(F32), d_slots, e)
        for g in range(2):
            total_state[g, 0:1, :] = sums[g][0:1, :]
            first_state[g] = keep * first_state[g] + diagonal * tn(q[g] * opens, d_low[g])
            second_state[g] = keep * second_state[g] + diagonal * tn(
                scaled_low[g] * opens, grad[g]
            )
            parts = (d_queries[g], d_keys[g], d_values[g], d_control[g])
            found[g].append([part.astype(BF16) for part in parts])
    grads = [
        jnp.concatenate([part[m] for part in reversed(found[g])], axis=0)
        for g in range(2)
        for m in range(4)
    ]

    normal, scale = standardise(x_ref[...].astype(F32))
    gain = vec_ref[0:1, :]
    normed = (normal * gain + vec_ref[1:2, :]).astype(BF16)
    d_w[...] += tn(normed, jnp.concatenate(grads, axis=1))
    d_normed = sum(
        nt(jnp.concatenate([grads[m], grads[4 + m]], axis=1), w_ref[m]) for m in range(4)
    )
    d_vec[0:1, :] += jnp.sum(d_normed * normal, axis=0, keepdims=True)
    d_vec[1:2, :] += jnp.sum(d_normed, axis=0, keepdims=True)
    out_ref[...] = hidden_ref[...] + norm_backward(d_normed, gain, normal, scale)

    @pl.when(step == chunks - 1)
    def _():
        def write(ref, half):
            for s in range(shards):
                y, z = (me ^ s) & 1, (me ^ s) >> 1
                top = piece_of(d_vec[...], s, r)
                both_rows = jnp.concatenate([top, jnp.zeros_like(top)], axis=0).astype(BF16)
                for g in range(2):
                    for m in range(4):
                        x = cross ^ (m // 2)
                        lead = (g, x, y, z) if g else (g, y, x, z)
                        at = (4 * g + m) * QUAD + half * 128
                        part = d_w[s * r : (s + 1) * r, at : at + 128].astype(BF16)
                        ref[(*lead, slice((m % 2) * r, (m % 2 + 1) * r), slice(None))] = part
                    for x in range(2):
                        lead = (g, x, y, z) if g else (g, y, x, z)
                        ref[(*lead, slice(2 * r, 2 * r + 16), slice(None))] = both_rows

        @pl.when(core == 0)
        def _():
            write(keep_ref, 0)
            write(send_ref, 1)

        @pl.when(core == 1)
        def _():
            write(keep_ref, 1)
            write(send_ref, 0)


def whole(shape):
    return pl.BlockSpec(shape, lambda *_: (0,) * len(shape))


def anywhere():
    return pl.BlockSpec(memory_space=pl.ANY)


def shaped(shape, dtype):
    return jax.ShapeDtypeStruct(shape, dtype)


def params():
    return pltpu.CompilerParams(
        dimension_semantics=("arbitrary",), vmem_limit_bytes=VMEM_LIMIT
    )


def call_pack(shards, matrices, vectors, valid):
    r = 512 // shards
    operands = [*matrices, *[v.reshape(-1, min(128, v.shape[0])) for v in vectors], valid]
    mixer, branch = (2 * r + 16, 256), (4 * r + r // 2, 256)
    return pl.pallas_call(
        functools.partial(pack, shards),
        grid=(1,),
        in_specs=[whole(v.shape) for v in operands],
        out_specs=[whole(mixer), whole(branch)],
        out_shape=[shaped(mixer, BF16), shaped(branch, BF16)],
        compiler_params=params(),
        cost_estimate=COST,
        name="pack",
    )(*operands)


def call_forward(quad, shards, segments, x, operands, earlier):
    length = x.shape[0]
    chunks = length // CHUNK
    wide = pl.BlockSpec((CHUNK, 512), lambda c, *_: (c, 0))
    tile = pl.BlockSpec((CHUNK, QUAD), lambda c, *_: (c, 0))
    state = pl.BlockSpec((CHUNK // SUB, QUAD, QUAD), lambda c, *_: (c, 0, 0))
    low = shaped((length, QUAD), BF16)
    states = shaped((length // SUB, QUAD, QUAD), BF16)
    if quad == 0:
        in_specs = [anywhere()] * 8
        out_specs = [whole((4, 512, 512)), whole((8, 512)), whole((8, 2048)), whole((8, 128))]
        out_shape = [shaped((4, 512, 512), BF16), shaped((8, 512), F32)]
        out_shape += [shaped((8, 2048), F32), shaped((8, 128), F32)]
        first = [pltpu.VMEM((4, shards, 16, 256), BF16)]
        last = [pltpu.SemaphoreType.DMA((2,))]
    else:
        in_specs = [pl.BlockSpec((4, 512, QUAD), lambda c, *_: (0, 0, 1)), whole((8, 512))]
        out_specs, out_shape, first, last = [], [], [], []
    grid_spec = pltpu.PrefetchScalarGridSpec(
        num_scalar_prefetch=1,
        grid=(chunks,),
        in_specs=[wide, pl.BlockSpec((1, CHUNK), lambda c, *_: (0, c)), *in_specs]
        + [anywhere()] * len(earlier),
        out_specs=[tile] * 8 + [state] * 2 + out_specs,
        scratch_shapes=first
        + [
            pltpu.VMEM((QUAD, QUAD), F32),
            pltpu.VMEM((QUAD, QUAD), F32),
            pltpu.VMEM((8, QUAD), F32),
        ]
        + last,
    )
    return pl.pallas_call(
        functools.partial(
            ordered,
            functools.partial(attention_forward, quad, shards),
            3 + len(operands),
            len(earlier),
        ),
        grid_spec=grid_spec,
        out_shape=[low] * 6 + [shaped((length, QUAD), F32), low, states, states]
        + out_shape,
        compiler_params=params(),
        cost_estimate=COST,
        name=f"attention_forward_{quad}",
    )(segments, x, segments, *operands, *earlier)


def call_feed_forward(shards, reps, tokens, *operands):
    length = operands[0].shape[0]
    r = 512 // shards
    payload = (reps, shards, branch_rows(shards, reps)[0], 256)
    vmem = pl.BlockSpec(memory_space=pltpu.VMEM)
    wide = (length, 512)
    return pl.pallas_call(
        functools.partial(feed_forward, shards, tokens),
        in_specs=[anywhere()] * 4 + [vmem] * 4 + [anywhere()] * 8,
        out_specs=[anywhere()] * 6,
        out_shape=[
            shaped(wide, BF16),
            shaped(wide, F32),
            shaped(wide, BF16),
            shaped(payload, BF16),
            *[shaped((reps // 2, *payload[1:]), BF16)] * 2,
        ],
        scratch_shapes=[
            pltpu.VMEM(wide, BF16),
            pltpu.VMEM(wide, BF16),
            pltpu.VMEM(wide, BF16),
            pltpu.VMEM((2 * shards, r // 2, 512), BF16),
            pltpu.VMEM((4, 512, 512), BF16),
            pltpu.VMEM((2048, 512), BF16),
            pltpu.VMEM((4, length, 512), BF16),
            pltpu.VMEM(wide, BF16),
            pltpu.VMEM(wide, F32),
            pltpu.VMEM(wide, BF16),
            pltpu.VMEM(payload, BF16),
            pltpu.VMEM(payload, BF16),
            pltpu.VMEM(wide, BF16),
            pltpu.VMEM(wide, BF16),
            pltpu.VMEM(wide, F32),
            pltpu.VMEM((512, 512), BF16),
            pltpu.VMEM((4, 512, 512), BF16),
            pltpu.VMEM((2048, 512), BF16),
            pltpu.VMEM((8, 512), F32),
            pltpu.VMEM((4, 8, 512), F32),
            pltpu.SemaphoreType.DMA((10 + 2 * reps,)),
        ],
        compiler_params=pltpu.CompilerParams(vmem_limit_bytes=VMEM_LIMIT),
        cost_estimate=COST,
        name="feed_forward",
    )(*operands)


def call_backward(shards, segments, x, sides, operands, earlier):
    length = x.shape[0]
    chunks = length // BACK
    r = 512 // shards
    back = lambda c: chunks - 1 - c
    wide = pl.BlockSpec((BACK, 512), lambda c, *_: (back(c), 0))
    own = pl.BlockSpec((BACK, QUAD), lambda c, *_: (back(c), 0))
    state = pl.BlockSpec((BACK // SUB, QUAD, QUAD), lambda c, *_: (back(c), 0, 0))
    payload = (2, 2, 2, shards // 2, 2 * r + 16, 128)
    grid_spec = pltpu.PrefetchScalarGridSpec(
        num_scalar_prefetch=1,
        grid=(chunks,),
        in_specs=[
            wide,
            pl.BlockSpec((1, BACK), lambda c, *_: (0, back(c))),
            *([own] * 7 + [state] * 2) * 2,
            wide,
            whole((4, 512, 512)),
            whole((8, 512)),
            wide,
            *[anywhere()] * len(earlier),
        ],
        out_specs=[wide, whole(payload), whole(payload)],
        scratch_shapes=[
            pltpu.VMEM((2, QUAD, QUAD), F32),
            pltpu.VMEM((2, QUAD, QUAD), F32),
            pltpu.VMEM((2, 8, QUAD), F32),
            pltpu.VMEM((512, 8 * QUAD), F32),
            pltpu.VMEM((8, 512), F32),
        ],
    )
    return pl.pallas_call(
        functools.partial(
            ordered, functools.partial(attention_backward, shards), 25, len(earlier)
        ),
        grid_spec=grid_spec,
        out_shape=[shaped((length, 512), F32), shaped(payload, BF16), shaped(payload, BF16)],
        compiler_params=params(),
        cost_estimate=COST,
        name="attention_backward",
    )(segments, x, segments, *sides[0], *sides[1], *operands, *earlier)


def swap(value, axis, bit):
    n = lax.axis_size(axis)
    return lax.ppermute(value, axis, [(i, i ^ bit) for i in range(n)])


def bit_groups(shards):
    bits = shards.bit_length() - 1
    return [(low, min(2, bits - low)) for low in range(1, bits, 2)]


def branch_rows(shards, reps):
    r = 512 // shards
    piece = -(-(9 * r + 16) // (8 * reps)) * 8
    names = [("contract", 4 * r)] + [(b, r) for b in range(4)] + [("output", r), ("vectors", 16)]
    rows, at = [], 0
    for name, height in names + [("none", piece * reps - 9 * r - 16)]:
        done = 0
        while done < height:
            part, offset = divmod(at, piece)
            size = min(height - done, piece - offset)
            rows.append((name, done, part, offset, size))
            done += size
            at += size
    return piece, rows


def add_arrived(shards, *refs):
    source, target = refs[0], refs[-1]
    for half in range(2):
        total = 0.0
        for rep in range(half, source.shape[0], 2):
            for s in range(shards):
                total = total + source[rep, s].astype(F32)
        target[half] = total.astype(BF16)


def call_add_arrived(shards, arrived, *others):
    reps, _, piece, width = arrived.shape
    return pl.pallas_call(
        functools.partial(add_arrived, shards),
        in_specs=[pl.BlockSpec(memory_space=pltpu.VMEM)] + [anywhere()] * len(others),
        out_specs=pl.BlockSpec(memory_space=pltpu.VMEM),
        out_shape=shaped((2, piece, width), BF16),
        compiler_params=pltpu.CompilerParams(vmem_limit_bytes=VMEM_LIMIT),
        cost_estimate=COST,
        name="add_arrived",
    )(arrived, *others)


def zero_of(arrays):
    return sum(array[(0,) * array.ndim] for array in arrays) * jnp.zeros((), BF16)


def after(value, *others):
    return lax.optimization_barrier((value, *others))[0]


def quarters(refs):
    _, core, cross = place()

    def quarter(rows, half, third):
        parts = [ref[rows, :] for ref in refs]
        near = jnp.where(core == half, parts[0], parts[1])
        far = jnp.where(core == half, parts[2], parts[3])
        return jnp.where(cross == third, near, far).astype(F32)

    def both(rows, third):
        return jnp.concatenate([quarter(rows, half, third) for half in range(2)], axis=1)

    return both


def assemble_branch(shards, count_ref, *refs):
    held = refs[-1]
    reps = held.shape[0]
    me = lax.axis_index("rep")
    for a in range(reps):
        held[me ^ a] = refs[a][...]
    contract_ref, expand_ref, output_ref, bias_1_ref, bias_2_ref, gain_ref, shift_ref, loss_ref = (
        refs[reps:-1]
    )
    r = 512 // shards
    _, rows = branch_rows(shards, reps)
    vectors = []
    for name, done, part, offset, size in rows:
        value = jnp.concatenate(
            [held[part, half, offset : offset + size, :] for half in range(2)], axis=1
        ).astype(F32)
        if name == "contract":
            contract_ref[done : done + size, :] = value
        elif name == "output":
            output_ref[done : done + size, :] = value
        elif name == "vectors":
            vectors.append(value[:, :256])
        elif name != "none":
            expand_ref[done : done + size, name * 512 : (name + 1) * 512] = value
    vectors = vectors[0] if len(vectors) == 1 else jnp.concatenate(vectors, axis=0)
    bias_1_ref[...] = vectors[8:9, : 4 * r]
    gain_ref[...] = vectors[0:1, :r]
    shift_ref[...] = vectors[1:2, :r]
    bias_2_ref[...] = vectors[2:3, :r]
    lane = lax.broadcasted_iota(jnp.int32, (1, 128), 1)
    power = jnp.zeros((1, 128), F32)
    for k in range(LOSS_DIGITS):
        power = jnp.where(lane == k, 8.0 ** (k - LOSS_ZERO), power)
    total = jnp.sum(vectors[0:1, 128:256] * power, axis=1, keepdims=True)
    count = 256.0 * count_ref[6:7, 0:1] + count_ref[6:7, 1:2]
    loss_ref[...] = total / (2.0 * count)


def assemble_mixer(shards, *refs):
    both = quarters(refs[:4])
    gain_ref, shift_ref = refs[8:]
    r = 512 // shards
    for m, ref in enumerate(refs[4:8]):
        for quad in range(2):
            at = quad * (2 * r + 16) + (m % 2) * r
            ref[:, quad * 256 : (quad + 1) * 256] = both(slice(at, at + r), m // 2)
    vectors = both(slice(4 * r + 16, 4 * r + 32), 0)
    gain_ref[...] = vectors[0:1, :r]
    shift_ref[...] = vectors[1:2, :r]


def assemble_all(shards, reps, count_ref, *refs):
    parts_q, parts_f, refs = refs[:4], refs[4 : 4 + reps], refs[4 + reps :]
    assemble_mixer(shards, *parts_q, *refs[:6])
    assemble_branch(shards, count_ref, *parts_f, *refs[6:])


def assemble(shards, count, parts_q, parts_f):
    reps = len(parts_f)
    r = 512 // shards
    shapes = [(r, 512)] * 4 + [(1, r)] * 2
    shapes += [(4 * r, 512), (r, 2048), (r, 512), (1, 4 * r), (1, r), (1, r), (1, r), (1, 1)]
    return pl.pallas_call(
        functools.partial(assemble_all, shards, reps),
        in_specs=[pl.BlockSpec(memory_space=pltpu.VMEM)] * (5 + reps),
        out_specs=[pl.BlockSpec(memory_space=pltpu.VMEM)] * len(shapes),
        out_shape=[shaped(shape, F32) for shape in shapes],
        scratch_shapes=[pltpu.VMEM((reps, *parts_f[0].shape), BF16)],
        cost_estimate=COST,
        name="assemble",
    )(count, *parts_q, *parts_f)


def add_low(*parts):
    return sum(part.astype(F32) for part in parts).astype(BF16)


def local(
    inputs,
    segments,
    valid_mask,
    teacher,
    query_weight,
    key_weight,
    value_weight,
    control_weight,
    output_weight,
    gain_first,
    shift_first,
    expand_weight,
    expand_bias,
    contract_weight,
    contract_bias,
    gain_second,
    shift_second,
):
    _, length, width = inputs.shape
    shards, reps = lax.axis_size("shard"), lax.axis_size("rep")
    r = width // shards
    core = lax.axis_index("rep") % 2
    cross = (lax.axis_index("rep") // 2) % 2
    groups = bit_groups(shards)

    matrices = (query_weight, key_weight, value_weight, control_weight, output_weight)
    matrices += (expand_weight, contract_weight)
    biases = (gain_first, shift_first, gain_second, shift_second, contract_bias, expand_bias)
    mixer, branch = call_pack(shards, matrices, biases, valid_mask)

    def along_z(payload):
        held = [payload[None]]
        for low, bits in groups:
            if len(held) > 1:
                held = [jnp.concatenate(held, axis=0)]
            held += [swap(held[0], "shard", a << low) for a in range(1, 1 << bits)]
        return held

    def halves(held):
        if len(held) == 4:
            return jnp.concatenate(held[:2], axis=0), jnp.concatenate(held[2:], axis=0)
        joined = jnp.concatenate(held, axis=0)
        half = joined.shape[0] // 2
        return joined[:half], joined[half:]

    def step_one(first, second):
        return swap(first, "shard", 1), swap(second, "rep", 2)

    def join(first, second, arrived):
        return jnp.concatenate([first, arrived[0]]), jnp.concatenate([second, arrived[1]])

    def step_two(first, second):
        return swap(first, "rep", 2), swap(second, "shard", 1)

    first, second = halves(along_z(mixer))
    held_b = along_z(branch + zero_of([second]))
    first, second = join(first, second, step_one(first, second))
    arrived = step_two(first, second)
    first_b, second_b = halves(held_b)
    pending = step_one(first_b, second_b)
    last = arrived[1] + zero_of(held_b[1:])
    mine_a = (first, arrived[0], second, last)
    theirs_a = tuple(swap(part, "rep", 1) for part in mine_a)

    x = inputs.reshape(length, width)
    forward_0 = call_forward(
        0, shards, segments, x, (*mine_a, *theirs_a), (first_b, second_b)
    )
    weights, vectors, bias, count = forward_0[10:]
    bit = 4
    while bit < reps:
        count = count + swap(count, "rep", bit)
        bit *= 2
    pending = after(pending, forward_0[7])
    first_b, second_b = join(first_b, second_b, pending)
    pending = step_two(first_b, second_b)
    near_b = swap(first_b, "rep", 1), swap(second_b, "rep", 1)
    forward_1 = call_forward(
        1, shards, segments, x, (weights, vectors), (first_b, second_b, *near_b)
    )
    pending = after(pending, forward_1[7])
    mine_b = (first_b, pending[0], second_b, pending[1])
    theirs_b = (near_b[0], swap(pending[0], "rep", 1), near_b[1], swap(pending[1], "rep", 1))
    mixed = (forward_0[7], forward_1[7])

    layer_out, grad_hidden, grad_mix, keep_f, send_low, send_high = call_feed_forward(
        shards,
        reps,
        float(length * shards * reps),
        x,
        *mixed,
        teacher.reshape(length, width),
        valid_mask,
        vectors,
        bias,
        count,
        *mine_b,
        *theirs_b,
    )

    def split(parts):
        return add_low(*(part[0] for part in parts)), add_low(*(part[1] for part in parts))

    def cross_first(parts):
        keep, send = split(parts)
        return keep, swap(send, "rep", 2)

    def row_first(parts):
        keep, send = split(parts)
        return keep, swap(send, "shard", 1)

    def z_stage(parts_list):
        current = parts_list
        for low, bits in reversed(groups):
            span = 1 << (low - 1)
            pieces = [
                jnp.concatenate(
                    [
                        add_low(*(part[a * span : (a + 1) * span] for part in parts))
                        for parts in current
                    ],
                    axis=1,
                )
                for a in range(1 << bits)
            ]
            arrived = [swap(pieces[a], "shard", a << low) for a in range(1, 1 << bits)]
            current = [(pieces[0], *arrived)]
        return current[0]

    def finish(parts):
        total = add_low(*(part[0] for part in parts))
        bit = 4
        while bit < reps:
            total = add_low(total, swap(total, "rep", bit))
            bit *= 2
        return [total] + [swap(total, "rep", a) for a in range(1, 4)]

    late_f = swap(send_low, "rep", 1), swap(send_high, "rep", 1)
    halves_f = keep_f[: reps // 2], keep_f[reps // 2 :]
    summed = jnp.concatenate([add_low(a, b) for a, b in zip(halves_f, late_f)], axis=0)
    every = summed.reshape(reps * shards, *summed.shape[2:])
    arrived_f = lax.all_to_all(every, ("rep", "shard"), 0, 0).reshape(summed.shape)
    sides = [(*saved[:7], *saved[8:10]) for saved in (forward_0, forward_1)]
    grad_inputs, keep_q, send_q = call_backward(
        shards, segments, x, sides, (grad_mix, weights, vectors, grad_hidden), (every,)
    )
    late_q = swap(send_q, "rep", 1)
    parts_0, parts_1 = row_first((keep_q[0], late_q[0])), cross_first((keep_q[1], late_q[1]))
    parts_0, parts_1 = cross_first(parts_0), row_first(parts_1)
    q_pieces = z_stage([parts_0, parts_1])
    total_f = call_add_arrived(shards, arrived_f, q_pieces[0])
    by_offset = {0: total_f}
    bit = 2
    while bit < reps:
        by_offset |= {a | bit: swap(part, "rep", bit) for a, part in list(by_offset.items())}
        bit *= 2
    by_offset |= {a | 1: swap(part, "rep", 1) for a, part in list(by_offset.items())}
    parts_f = [by_offset[a] for a in range(reps)]
    parts_q = finish(q_pieces)
    results = assemble(shards, count, parts_q, parts_f)
    mats, (gain_1, shift_1) = results[:4], results[4:6]
    grad_contract, grad_expand, grad_output, bias_1, bias_2, gain_2, shift_2, loss = results[6:]
    return (
        layer_out.reshape(inputs.shape),
        grad_inputs.reshape(inputs.shape),
        loss.reshape(()),
        *mats,
        grad_output,
        gain_1.reshape(r),
        shift_1.reshape(r),
        grad_expand,
        bias_1.reshape(4 * r),
        grad_contract,
        bias_2.reshape(r),
        gain_2.reshape(r),
        shift_2.reshape(r),
    )


def solution(mesh):
    every = P(("rep", "shard"), None, None)
    every_row = P(("rep", "shard"), None)
    matrix, vector = P("shard", None), P("shard")
    in_specs = (
        every,
        every_row,
        every_row,
        every,
        *[matrix] * 5,
        *[vector] * 2,
        matrix,
        vector,
        matrix,
        *[vector] * 3,
    )
    out_specs = (
        every,
        every,
        P(),
        *[matrix] * 5,
        *[vector] * 2,
        matrix,
        vector,
        matrix,
        *[vector] * 3,
    )
    return jax.shard_map(local, mesh=mesh, in_specs=in_specs, out_specs=out_specs, check_vma=False)
```

```python
import functools

import jax
import jax.numpy as jnp
from jax import lax
from jax.experimental import pallas as pl
from jax.experimental.pallas import tpu as pltpu
from jax.sharding import PartitionSpec as P

HEADS = 8
EPSILON = 1e-05
CHUNK = 512
SUB = 128
BACK = 512
QUAD = 256
F32 = jnp.float32
BF16 = jnp.bfloat16
VMEM_LIMIT = 60 << 20
LOSS_DIGITS = 30
LOSS_ZERO = 10
COST = pl.CostEstimate(flops=1000, bytes_accessed=1000, transcendentals=0)


def ordered(kernel, at, count, *refs):
    kernel(*refs[:at], *refs[at + count :])


def place():
    rep = lax.axis_index("rep")
    return lax.axis_index("shard"), rep % 2, (rep // 2) % 2


def slots_of(shards):
    ways = shards // 2
    low, high = range(ways // 2), range(ways // 2, ways)
    first = [(z, y, x) for x in (0, 1) for y in (0, 1) for z in low]
    second = [(z, y, x) for y in (0, 1) for x in (0, 1) for z in high]
    return first + second


def block_of(pieces, slot):
    each = pieces[0].shape[0]
    return pieces[slot // each].at[slot % each]


def nn(left, right):
    return jnp.dot(left, right, preferred_element_type=F32)


def nt(left, right):
    return lax.dot_general(left, right, (((1,), (1,)), ((), ())), preferred_element_type=F32)


def tn(left, right):
    return lax.dot_general(left, right, (((0,), (0,)), ((), ())), preferred_element_type=F32)


def head_lanes():
    lane = lax.broadcasted_iota(jnp.int32, (1, QUAD), 1) // 64
    return [jnp.where(lane == h, 1.0, 0.0).astype(BF16) for h in range(4)]


def block_diagonal():
    rows = lax.broadcasted_iota(jnp.int32, (QUAD, QUAD), 0) // 64
    columns = lax.broadcasted_iota(jnp.int32, (QUAD, QUAD), 1) // 64
    return jnp.where(rows == columns, 1.0, 0.0)


def as_column(row, width):
    tile = jnp.broadcast_to(row, (128, row.shape[1])).T
    return jnp.concatenate([tile] * (width // 128), axis=1)


def causal_mask(column, row):
    at = lax.broadcasted_iota(jnp.int32, (SUB, SUB), 0)
    source = lax.broadcasted_iota(jnp.int32, (SUB, SUB), 1)
    return jnp.where((column[:, :SUB] == row) & (source <= at), 1.0, 0.0).astype(BF16)


def causal_mask_transposed(column, row):
    source = lax.broadcasted_iota(jnp.int32, (SUB, SUB), 0)
    at = lax.broadcasted_iota(jnp.int32, (SUB, SUB), 1)
    return jnp.where((column[:, :SUB] == row) & (source <= at), 1.0, 0.0).astype(BF16)


def head_stack(values):
    return jnp.concatenate([values * lanes for lanes in head_lanes()], axis=0)


def four_times(mask):
    return jnp.concatenate([mask] * 4, axis=1)


def per_head(values, reduce, fill):
    lane = lax.broadcasted_iota(jnp.int32, (1, 128), 1)
    first = lane < 64
    tiles = []
    for tile in range(values.shape[1] // 128):
        part = values[:, tile * 128 : (tile + 1) * 128]
        one = reduce(jnp.where(first, part, fill), axis=-1, keepdims=True)
        two = reduce(jnp.where(first, fill, part), axis=-1, keepdims=True)
        tiles.append(jnp.where(first, one, two))
    return jnp.concatenate(tiles, axis=1)


def standardise(values):
    mean = jnp.mean(values, axis=-1, keepdims=True)
    centred = values - mean
    variance = jnp.mean(centred * centred, axis=-1, keepdims=True)
    scale = lax.rsqrt(variance + EPSILON)
    return centred * scale, scale


def norm_backward(gradient, gain, normal, scale):
    upstream = gradient * gain
    one = jnp.mean(upstream, axis=-1, keepdims=True)
    two = jnp.mean(upstream * normal, axis=-1, keepdims=True)
    return (upstream - one - normal * two) * scale


def spread(rows, shards):
    width = 512 // shards
    lane = lax.broadcasted_iota(jnp.int32, (8, 128), 1)
    tiles = [None] * 4
    for s in range(shards):
        tile, offset = divmod(s * width, 128)
        moved = pltpu.roll(rows[s], offset, 1) if offset else rows[s]
        inside = (lane >= offset) & (lane < offset + width)
        tiles[tile] = jnp.where(inside, moved, 0.0 if tiles[tile] is None else tiles[tile])
    return jnp.concatenate(tiles, axis=1)


def digits_of(value):
    lane = lax.broadcasted_iota(jnp.int32, (8, 128), 1)
    scale = jnp.zeros((8, 128), F32)
    for k in range(LOSS_DIGITS):
        scale = jnp.where(lane == k, 8.0 ** (LOSS_ZERO - k), scale)
    shifted = value * scale
    return jnp.floor(shifted) - 8.0 * jnp.floor(shifted * 0.125)


def piece_of(vectors, s, width):
    tile, offset = divmod(s * width, 128)
    part = vectors[:, tile * 128 : (tile + 1) * 128]
    return pltpu.roll(part, 128 - offset, 1) if offset else part


def pack(shards, *refs):
    query, key, value, control, output, expand, contract = refs[:7]
    gain_1, shift_1, gain_2, shift_2, bias_2, bias_1, valid = refs[7:14]
    mixer_ref, branch_ref = refs[14:]
    r = 512 // shards
    _, core, cross = place()

    def write(half, third):
        at = slice(half * 256, half * 256 + 256)
        for m, ref in enumerate(((query, key), (value, control))[third]):
            mixer_ref[m * r : (m + 1) * r] = ref[:, at]
        if third == 0:
            for b in range(4):
                part = expand[:, b * 512 + half * 256 : b * 512 + half * 256 + 256]
                branch_ref[b * r : (b + 1) * r] = part
        else:
            branch_ref[0 : 4 * r] = contract[:, at]
        branch_ref[4 * r : 4 * r + r // 2] = output[third * (r // 2) : (third + 1) * (r // 2), at]

    for half in range(2):
        for third in range(2):
            pl.when((core == half) & (cross == third))(functools.partial(write, half, third))

    row = lax.broadcasted_iota(jnp.int32, (16, 256), 0)
    lane = lax.broadcasted_iota(jnp.int32, (16, 256), 1)
    block = jnp.zeros((16, 256), F32)
    for k, ref in ((0, gain_1), (1, shift_1), (2, gain_2), (3, shift_2), (4, bias_2), (8, bias_1)):
        part = ref[...].astype(F32)
        part = jnp.concatenate([part[n : n + 1] for n in range(part.shape[0])], axis=1)
        width = part.shape[1]
        if width < 256:
            part = jnp.concatenate([part, jnp.zeros((1, 256 - width), F32)], axis=1)
        block = jnp.where(row == k, part, block)
    count = jnp.sum(valid[...].astype(F32))
    high = jnp.floor(count / 256.0)
    block = jnp.where((row == 6) & (lane == 0), high, block)
    block = jnp.where((row == 6) & (lane == 1), count - 256.0 * high, block)
    mixer_ref[2 * r : 2 * r + 16] = block.astype(BF16)


def attention_forward(quad, shards, seg_s, x_ref, seg_ref, *refs):
    step = pl.program_id(0)
    r = 512 // shards
    at = slice(quad * QUAD, (quad + 1) * QUAD)
    if quad == 0:
        pieces, refs = (refs[:4], refs[4:8]), refs[8:]
        q_ref, k_ref, v_ref, e_ref, p_ref, s_ref, rz_ref, mix_ref, one_ref, two_ref = refs[:10]
        w_ref, vec_ref, eb_ref, count_ref = refs[10:14]
        held, first_state, second_state, total_state, sems = refs[14:]
        weight = lambda m: w_ref[m, :, at]
    else:
        w_ref, vec_ref = refs[:2]
        q_ref, k_ref, v_ref, e_ref, p_ref, s_ref, rz_ref, mix_ref, one_ref, two_ref = refs[2:12]
        first_state, second_state, total_state = refs[12:]
        weight = lambda m: w_ref[m]

    @pl.when(step == 0)
    def _():
        first_state[...] = jnp.zeros_like(first_state)
        second_state[...] = jnp.zeros_like(second_state)
        total_state[...] = jnp.zeros_like(total_state)

    def assemble():
        me, core, cross = place()
        for half, source in enumerate(pieces):
            column = pl.multiple_of(((core + half) % 2) * 256, 256)
            for slot, (z, y, x) in enumerate(slots_of(shards)):
                owner = me ^ (2 * z + y)
                third = cross ^ x
                for m in range(2):
                    pltpu.make_async_copy(
                        block_of(source, slot).at[pl.ds(m * r, r)],
                        w_ref.at[
                            2 * third + m,
                            pl.ds(pl.multiple_of(owner * r, r), r),
                            pl.ds(column, 256),
                        ],
                        sems.at[0],
                    ).start()
                pltpu.make_async_copy(
                    block_of(source, slot).at[pl.ds(2 * r, 16)], held.at[2 * half + x, owner], sems.at[1]
                ).start()
        pltpu.make_async_copy(held, held, sems.at[1]).wait()
        own = [held[0, s].astype(F32) for s in range(shards)]
        count = sum(part[:8, :128] for part in own)
        for k in range(1, 4):
            count += jnp.sum(held[k, :, :8, :128].astype(F32), axis=0)
        count_ref[...] = count
        vec_ref[...] = spread([part[:8, :128] for part in own], shards)
        width = 2048 // shards
        lane = lax.broadcasted_iota(jnp.int32, (8, 128), 1)
        if width >= 128:
            for s in range(shards):
                eb_ref[:, s * width : (s + 1) * width] = own[s][8:16, :width]
        else:
            for tile in range(16):
                built = jnp.zeros((8, 128), F32)
                for k in range(128 // width):
                    part = own[tile * (128 // width) + k][8:16, :128]
                    moved = pltpu.roll(part, k * width, 1) if k else part
                    built = jnp.where((lane >= k * width) & (lane < (k + 1) * width), moved, built)
                eb_ref[:, tile * 128 : (tile + 1) * 128] = built
        pltpu.make_async_copy(w_ref, w_ref, sems.at[0]).wait()

    if quad == 0:
        pl.when(step == 0)(assemble)

    row_all = seg_ref[...].astype(F32)
    diagonal = block_diagonal()
    normal, _ = standardise(x_ref[...].astype(F32))
    normed = (normal * vec_ref[0:1, :] + vec_ref[1:2, :]).astype(BF16)
    q_ref[...] = nn(normed, weight(0)).astype(BF16)
    k_ref[...] = nn(normed, weight(1)).astype(BF16)
    v_ref[...] = nn(normed, weight(2)).astype(BF16)
    e_ref[...] = jnp.exp(nn(normed, weight(3))).astype(BF16)
    subs = range(CHUNK // SUB)
    spans = [slice(sub * SUB, (sub + 1) * SUB) for sub in subs]
    q, k, v, e = ([ref[rows] for rows in spans] for ref in (q_ref, k_ref, v_ref, e_ref))
    causal, causal_4, enters, one, two, totals = [], [], [], [], [], []
    first, second, running = first_state[...], second_state[...], total_state[0:1, :]
    for sub in subs:
        start = step * CHUNK + sub * SUB
        segment_last = seg_s[0, start + SUB - 1]
        segment_before = jnp.where(start == 0, -1, seg_s[0, jnp.maximum(start - 1, 0)])
        keep = jnp.where(segment_last == segment_before, 1.0, 0.0)
        row = row_all[:, spans[sub]]
        column = as_column(row, QUAD)
        causal.append(causal_mask(column, row))
        causal_4.append(four_times(causal[sub]))
        enters.append(jnp.where(column == segment_before.astype(F32), 1.0, 0.0))
        leaves = jnp.where(column == segment_last.astype(F32), 1.0, 0.0).astype(BF16)
        one.append(first.astype(BF16))
        two.append(second.astype(BF16))
        one_ref[sub] = one[sub]
        two_ref[sub] = two[sub]
        totals.append(nn(causal[sub], e[sub]) + enters[sub] * running)
        running = totals[sub][SUB - 1 : SUB, :]
        first = keep * first + diagonal * tn(k[sub] * leaves, e[sub])
        second = keep * second + diagonal * tn(e[sub] * leaves, v[sub])
    first_state[...] = first
    second_state[...] = second
    total_state[0:1, :] = running

    def each(function, *lists):
        return [function(*values) for values in zip(*lists)]

    def store(ref, values):
        for rows, value in zip(spans, values):
            ref[rows] = value

    inverse = each(lambda a: 1.0 / a, totals)
    store(rz_ref, inverse)
    e_stack = each(head_stack, e)
    scores = each(lambda a, b, c: nt(a, head_stack(b)).astype(BF16) * c, q, k, causal_4)
    gathered = each(
        lambda a, b, c, d, f: nn(a, b) + c * nn(d, f), scores, e_stack, enters, q, one
    )
    slot_scores = each(lambda a, b: a * (b * 0.125), gathered, inverse)
    raised = each(lambda a: jnp.exp(a - per_head(a, jnp.max, -jnp.inf)), slot_scores)
    shares = each(lambda a: a / per_head(a, jnp.sum, 0.0), raised)
    scaled = each(lambda a, b: (a * b).astype(BF16), shares, inverse)
    mixing = each(lambda a, b, c: nt(a, b).astype(BF16) * c, scaled, e_stack, causal_4)
    mixed = each(
        lambda a, b, c, d, f: nn(a, head_stack(b)) + c * nn(d, f), mixing, v, enters, scaled, two
    )
    store(s_ref, each(lambda a: a.astype(BF16), slot_scores))
    store(p_ref, each(lambda a: a.astype(BF16), shares))
    store(mix_ref, each(lambda a: a.astype(BF16), mixed))


def feed_forward(
    shards,
    tokens,
    x_ref,
    mix_0_ref,
    mix_1_ref,
    teacher_ref,
    valid_ref,
    vec_ref,
    eb_ref,
    count_ref,
    *refs,
):
    pieces, refs = (refs[:4], refs[4:8]), refs[8:]
    out_ref, hidden_ref, grad_mix_ref, keep_out_ref, *sends = refs[:6]
    x, mix, teacher, wo, we, wc, act, out, hidden_grad, grad_mix = refs[6:16]
    keep_ref, send_ref, normed, low, d_normed, d_wo, d_we, d_wc, d_vec, d_eb, sems = refs[16:]
    r = 512 // shards
    me, core, cross = place()
    copies = [
        pltpu.make_async_copy(mix_0_ref, mix.at[:, pl.ds(0, QUAD)], sems.at[0]),
        pltpu.make_async_copy(mix_1_ref, mix.at[:, pl.ds(QUAD, QUAD)], sems.at[1]),
        pltpu.make_async_copy(x_ref, x, sems.at[2]),
        pltpu.make_async_copy(teacher_ref, teacher, sems.at[3]),
    ]
    sources = list(enumerate(pieces))
    columns = [pl.multiple_of(((core + half) % 2) * 256, 256) for half, _ in sources]
    for copy in copies[:2]:
        copy.start()
    for half, source in sources:
        for slot, (z, y, cross_slot) in enumerate(slots_of(shards)):
            pltpu.make_async_copy(
                block_of(source, slot).at[pl.ds(4 * r, r // 2)],
                wo.at[2 * (me ^ (2 * z + y)) + (cross ^ cross_slot), :, pl.ds(columns[half], 256)],
                sems.at[4],
            ).start()
    copies[2].start()
    for half, source in sources:
        for slot, (z, y, cross_slot) in enumerate(slots_of(shards)):
            owner = me ^ (2 * z + y)

            def expansion():
                for b in range(4):
                    pltpu.make_async_copy(
                        block_of(source, slot).at[pl.ds(b * r, r)],
                        we.at[
                            b, pl.ds(pl.multiple_of(owner * r, r), r), pl.ds(columns[half], 256)
                        ],
                        sems.at[5],
                    ).start()

            def contraction():
                pltpu.make_async_copy(
                    block_of(source, slot).at[pl.ds(0, 4 * r)],
                    wc.at[
                        pl.ds(pl.multiple_of(owner * 4 * r, 4 * r), 4 * r),
                        pl.ds(columns[half], 256),
                    ],
                    sems.at[6],
                ).start()

            pl.when((cross ^ cross_slot) == 0)(expansion)
            pl.when((cross ^ cross_slot) == 1)(contraction)
    copies[3].start()

    gain, shift, bias = vec_ref[2:3, :], vec_ref[3:4, :], vec_ref[4:5, :]
    copies[0].wait()
    copies[1].wait()
    pltpu.make_async_copy(wo, wo, sems.at[4]).wait()
    copies[2].wait()
    weight_out = wo[...].reshape(512, 512)
    hidden = x[...].astype(F32) + nn(mix[...], weight_out)
    normal, scale = standardise(hidden)
    normed[...] = (normal * gain + shift).astype(BF16)
    pltpu.make_async_copy(we, we, sems.at[5]).wait()
    for b in range(4):
        before = nn(normed[...], we[b]) + eb_ref[0:1, b * 512 : (b + 1) * 512]
        act[b] = jnp.maximum(before, 0.0).astype(BF16)
    pltpu.make_async_copy(wc, wc, sems.at[6]).wait()
    active = jnp.concatenate([act[b] for b in range(4)], axis=1)
    result = hidden + (nn(active, wc[...]) + bias)
    out[...] = result.astype(BF16)
    out_copy = pltpu.make_async_copy(out, out_ref, sems.at[7])
    out_copy.start()
    copies[3].wait()
    valid = as_column(valid_ref[...].astype(F32), 512)
    error = result - teacher[...].astype(F32)
    masked = valid * error
    loss = jnp.sum(masked * error)
    count = 256.0 * count_ref[6:7, 0:1] + count_ref[6:7, 1:2]
    grad_result = masked * (tokens / count)
    hidden_grad[...] = grad_result
    low[...] = grad_result.astype(BF16)
    d_normed[...] = jnp.zeros_like(d_normed)

    @pl.loop(0, 4)
    def _(b):
        at = pl.ds(pl.multiple_of(b * 512, 512), 512)
        d_wc[at, :] = tn(act[b], low[...]).astype(BF16)
        grad = jnp.where(act[b] > 0, nt(low[...], wc[at, :]), 0.0).astype(BF16)
        d_we[b] = tn(normed[...], grad).astype(BF16)
        d_eb[b, 0:1, :] = jnp.sum(grad.astype(F32), axis=0, keepdims=True)
        d_normed[...] += nt(grad, we[b])

    incoming = d_normed[...]
    hidden = x[...].astype(F32) + nn(mix[...], weight_out)
    normal, scale = standardise(hidden)
    d_vec[0:1, :] = jnp.sum(incoming * normal, axis=0, keepdims=True)
    d_vec[1:2, :] = jnp.sum(incoming, axis=0, keepdims=True)
    d_vec[2:3, :] = jnp.sum(low[...].astype(F32), axis=0, keepdims=True)
    d_vec[3:8, :] = jnp.zeros((5, 512), F32)
    grad_hidden = hidden_grad[...] + norm_backward(incoming, gain, normal, scale)
    hidden_grad[...] = grad_hidden
    hidden_copy = pltpu.make_async_copy(hidden_grad, hidden_ref, sems.at[8])
    hidden_copy.start()
    grad_low = grad_hidden.astype(BF16)
    grad_mix[...] = nt(grad_low, weight_out).astype(BF16)
    mix_copy = pltpu.make_async_copy(grad_mix, grad_mix_ref, sems.at[9])
    mix_copy.start()
    d_wo[...] = tn(mix[...], grad_low).astype(BF16)

    width = 2048 // shards
    digits = digits_of(jnp.zeros((8, 128), F32) + loss)
    _, rows = branch_rows(shards, keep_ref.shape[0])
    d_eb_all = jnp.concatenate([d_eb[b] for b in range(4)], axis=1)
    extra = []
    for s in range(shards):
        top = jnp.concatenate([piece_of(d_vec[...], s, r), digits], axis=1)
        if width >= 128:
            low_rows = d_eb_all[:, s * width : (s + 1) * width]
        else:
            low_rows = piece_of(d_eb_all, s, width)
        if low_rows.shape[1] < 256:
            pad = jnp.zeros((8, 256 - low_rows.shape[1]), F32)
            low_rows = jnp.concatenate([low_rows, pad], axis=1)
        extra.append(jnp.concatenate([top, low_rows], axis=0).astype(BF16))

    def write(ref, at, wanted):
        for s in range(shards):
            for name, done, part, offset, size in rows:
                if part != wanted:
                    continue
                if name == "contract":
                    value = d_wc[s * 4 * r + done : s * 4 * r + done + size, at]
                elif name == "output":
                    value = d_wo[s * r + done : s * r + done + size, at]
                elif name == "vectors":
                    value = extra[s][done : done + size]
                elif name == "none":
                    value = jnp.zeros((size, 256), BF16)
                else:
                    value = d_we[name, s * r + done : s * r + done + size, at]
                ref[part, s, offset : offset + size, :] = value

    left, right = slice(0, 256), slice(256, 512)
    reps = keep_ref.shape[0]
    flights = []
    for part in range(reps):

        @pl.when(core == 0)
        def _():
            write(send_ref, right, part)
            write(keep_ref, left, part)

        @pl.when(core == 1)
        def _():
            write(send_ref, left, part)
            write(keep_ref, right, part)

        for n, (source, target) in enumerate(
            (
                (send_ref, sends[2 * part // reps].at[part % (reps // 2)]),
                (keep_ref, keep_out_ref.at[part]),
            )
        ):
            copy = pltpu.make_async_copy(source.at[part], target, sems.at[10 + 2 * part + n])
            copy.start()
            flights.append(copy)
    for copy in [out_copy, hidden_copy, mix_copy, *flights]:
        copy.wait()


def attention_backward(shards, seg_s, x_ref, seg_ref, *refs):
    sides, refs = (refs[:9], refs[9:18]), refs[18:]
    g_ref, w_ref, vec_ref, hidden_ref, out_ref, keep_ref, send_ref = refs[:7]
    first_state, second_state, total_state, d_w, d_vec = refs[7:]
    step = pl.program_id(0)
    chunks = pl.num_programs(0)
    chunk = chunks - 1 - step
    r = 512 // shards
    me, core, cross = place()

    @pl.when(step == 0)
    def _():
        for ref in (first_state, second_state, total_state, d_w, d_vec):
            ref[...] = jnp.zeros_like(ref)

    length = chunks * BACK
    row_all = seg_ref[...].astype(F32)
    diagonal = block_diagonal()
    found = [[], []]
    for sub in reversed(range(BACK // SUB)):
        rows = slice(sub * SUB, (sub + 1) * SUB)
        start = chunk * BACK + sub * SUB
        segment_first = seg_s[0, start]
        segment_before = jnp.where(start == 0, -1, seg_s[0, jnp.maximum(start - 1, 0)])
        after_at = jnp.minimum(start + SUB, length - 1)
        segment_after = jnp.where(start + SUB == length, -1, seg_s[0, after_at])
        keep = jnp.where(segment_first == segment_after, 1.0, 0.0)
        row = row_all[:, rows]
        column = as_column(row, QUAD)
        causal_4 = four_times(causal_mask(column, row))
        turned = causal_mask_transposed(column, row)
        turned_4 = four_times(turned)
        enters = jnp.where(column == segment_before.astype(F32), 1.0, 0.0)
        goes_on = jnp.where(column == segment_after.astype(F32), 1.0, 0.0)
        opens = jnp.where(column == segment_first.astype(F32), 1.0, 0.0).astype(BF16)

        def both(function, *lists):
            return [function(*values) for values in zip(*lists)]

        q, k, v, e = ([side[n][rows] for side in sides] for n in range(4))
        grad = [g_ref[rows, g * QUAD : (g + 1) * QUAD] for g in range(2)]
        shares = [side[4][rows].astype(F32) for side in sides]
        slot_scores = [side[5][rows].astype(F32) for side in sides]
        inverse = [side[6][rows] for side in sides]
        one = [side[7][sub] for side in sides]
        two = [side[8][sub] for side in sides]
        scaled = both(lambda a, b: a * b, shares, inverse)
        scaled_low = [a.astype(BF16) for a in scaled]
        one_back = [first_state[g].astype(BF16) for g in range(2)]
        two_back = [second_state[g].astype(BF16) for g in range(2)]
        e_stack = both(head_stack, e)

        d_mixing = both(lambda a, b: nt(a, head_stack(b)).astype(BF16) * causal_4, grad, v)
        d_scaled = both(
            lambda a, b, c, d: nn(a, b) + enters * nt(c, d), d_mixing, e_stack, grad, two
        )
        q_stack, grad_stack = both(head_stack, q), both(head_stack, grad)
        scaled_stack = both(head_stack, scaled_low)
        mixing_t = both(lambda a, b: nt(a, b).astype(BF16) * turned_4, e, scaled_stack)
        d_mixing_t = both(lambda a, b: nt(a, b).astype(BF16) * turned_4, v, grad_stack)
        scores_t = both(lambda a, b: nt(a, b).astype(BF16) * turned_4, k, q_stack)
        d_shares = both(lambda a, b: a * b, d_scaled, inverse)
        product = both(lambda a, b: a * b, shares, d_shares)
        d_scores = both(lambda a, b: a - b * per_head(a, jnp.sum, 0.0), product, shares)
        d_low = both(lambda a, b: (a * b * 0.125).astype(BF16), d_scores, inverse)
        d_totals = both(
            lambda a, b, c, d, i: -(a * b + c * d) * i,
            d_scaled,
            scaled,
            d_scores,
            slot_scores,
            inverse,
        )
        d_values = both(
            lambda a, b, c, d: nn(a, b) + goes_on * nn(c, d), mixing_t, grad_stack, e, two_back
        )
        d_slots = both(nn, d_mixing_t, scaled_stack)
        d_low_stack = both(head_stack, d_low)
        d_raw = both(lambda a, b: nt(a, b).astype(BF16) * causal_4, d_low, e_stack)
        d_raw_t = both(lambda a, b: nt(a, b).astype(BF16) * turned_4, e, d_low_stack)
        d_slots = both(lambda a, b, c: a + nn(b, c), d_slots, scores_t, d_low_stack)
        d_queries = both(
            lambda a, b, c, d: nn(a, head_stack(b)) + enters * nt(c, d), d_raw, k, d_low, one
        )
        d_keys = both(
            lambda a, b, c, d: nn(a, b) + goes_on * nt(c, d), d_raw_t, q_stack, e, one_back
        )
        totals_low = [a.astype(BF16) for a in d_totals]
        rest = both(lambda a, b: (a - b.astype(F32)).astype(BF16), d_totals, totals_low)
        sums = [
            nn(turned, totals_low[g]) + nn(turned, rest[g]) + goes_on * total_state[g, 0:1, :]
            for g in range(2)
        ]
        d_slots = both(
            lambda a, b, c, d, f, h: a + goes_on * (nn(b, c) + nt(d, f)) + h,
            d_slots,
            k,
            one_back,
            v,
            two_back,
            sums,
        )
        d_control = both(lambda a, b: a * b.astype(F32), d_slots, e)
        for g in range(2):
            total_state[g, 0:1, :] = sums[g][0:1, :]
            first_state[g] = keep * first_state[g] + diagonal * tn(q[g] * opens, d_low[g])
            second_state[g] = keep * second_state[g] + diagonal * tn(
                scaled_low[g] * opens, grad[g]
            )
            parts = (d_queries[g], d_keys[g], d_values[g], d_control[g])
            found[g].append([part.astype(BF16) for part in parts])
    grads = [
        jnp.concatenate([part[m] for part in reversed(found[g])], axis=0)
        for g in range(2)
        for m in range(4)
    ]

    normal, scale = standardise(x_ref[...].astype(F32))
    gain = vec_ref[0:1, :]
    normed = (normal * gain + vec_ref[1:2, :]).astype(BF16)
    d_w[...] += tn(normed, jnp.concatenate(grads, axis=1))
    d_normed = sum(
        nt(jnp.concatenate([grads[m], grads[4 + m]], axis=1), w_ref[m]) for m in range(4)
    )
    d_vec[0:1, :] += jnp.sum(d_normed * normal, axis=0, keepdims=True)
    d_vec[1:2, :] += jnp.sum(d_normed, axis=0, keepdims=True)
    out_ref[...] = hidden_ref[...] + norm_backward(d_normed, gain, normal, scale)

    @pl.when(step == chunks - 1)
    def _():
        def write(ref, half):
            for s in range(shards):
                y, z = (me ^ s) & 1, (me ^ s) >> 1
                top = piece_of(d_vec[...], s, r)
                both_rows = jnp.concatenate([top, jnp.zeros_like(top)], axis=0).astype(BF16)
                for g in range(2):
                    for m in range(4):
                        x = cross ^ (m // 2)
                        lead = (g, x, y, z) if g else (g, y, x, z)
                        at = (4 * g + m) * QUAD + half * 128
                        part = d_w[s * r : (s + 1) * r, at : at + 128].astype(BF16)
                        ref[(*lead, slice((m % 2) * r, (m % 2 + 1) * r), slice(None))] = part
                    for x in range(2):
                        lead = (g, x, y, z) if g else (g, y, x, z)
                        ref[(*lead, slice(2 * r, 2 * r + 16), slice(None))] = both_rows

        @pl.when(core == 0)
        def _():
            write(keep_ref, 0)
            write(send_ref, 1)

        @pl.when(core == 1)
        def _():
            write(keep_ref, 1)
            write(send_ref, 0)


def whole(shape):
    return pl.BlockSpec(shape, lambda *_: (0,) * len(shape))


def anywhere():
    return pl.BlockSpec(memory_space=pl.ANY)


def shaped(shape, dtype):
    return jax.ShapeDtypeStruct(shape, dtype)


def params():
    return pltpu.CompilerParams(
        dimension_semantics=("arbitrary",), vmem_limit_bytes=VMEM_LIMIT
    )


def call_pack(shards, matrices, vectors, valid):
    r = 512 // shards
    operands = [*matrices, *[v.reshape(-1, min(128, v.shape[0])) for v in vectors], valid]
    mixer, branch = (2 * r + 16, 256), (4 * r + r // 2, 256)
    return pl.pallas_call(
        functools.partial(pack, shards),
        grid=(1,),
        in_specs=[whole(v.shape) for v in operands],
        out_specs=[whole(mixer), whole(branch)],
        out_shape=[shaped(mixer, BF16), shaped(branch, BF16)],
        compiler_params=params(),
        cost_estimate=COST,
        name="pack",
    )(*operands)


def call_forward(quad, shards, segments, x, operands, earlier):
    length = x.shape[0]
    chunks = length // CHUNK
    wide = pl.BlockSpec((CHUNK, 512), lambda c, *_: (c, 0))
    tile = pl.BlockSpec((CHUNK, QUAD), lambda c, *_: (c, 0))
    state = pl.BlockSpec((CHUNK // SUB, QUAD, QUAD), lambda c, *_: (c, 0, 0))
    low = shaped((length, QUAD), BF16)
    states = shaped((length // SUB, QUAD, QUAD), BF16)
    if quad == 0:
        in_specs = [anywhere()] * 8
        out_specs = [whole((4, 512, 512)), whole((8, 512)), whole((8, 2048)), whole((8, 128))]
        out_shape = [shaped((4, 512, 512), BF16), shaped((8, 512), F32)]
        out_shape += [shaped((8, 2048), F32), shaped((8, 128), F32)]
        first = [pltpu.VMEM((4, shards, 16, 256), BF16)]
        last = [pltpu.SemaphoreType.DMA((2,))]
    else:
        in_specs = [pl.BlockSpec((4, 512, QUAD), lambda c, *_: (0, 0, 1)), whole((8, 512))]
        out_specs, out_shape, first, last = [], [], [], []
    grid_spec = pltpu.PrefetchScalarGridSpec(
        num_scalar_prefetch=1,
        grid=(chunks,),
        in_specs=[wide, pl.BlockSpec((1, CHUNK), lambda c, *_: (0, c)), *in_specs]
        + [anywhere()] * len(earlier),
        out_specs=[tile] * 8 + [state] * 2 + out_specs,
        scratch_shapes=first
        + [
            pltpu.VMEM((QUAD, QUAD), F32),
            pltpu.VMEM((QUAD, QUAD), F32),
            pltpu.VMEM((8, QUAD), F32),
        ]
        + last,
    )
    return pl.pallas_call(
        functools.partial(
            ordered,
            functools.partial(attention_forward, quad, shards),
            3 + len(operands),
            len(earlier),
        ),
        grid_spec=grid_spec,
        out_shape=[low] * 6 + [shaped((length, QUAD), F32), low, states, states]
        + out_shape,
        compiler_params=params(),
        cost_estimate=COST,
        name=f"attention_forward_{quad}",
    )(segments, x, segments, *operands, *earlier)


def call_feed_forward(shards, reps, tokens, *operands):
    length = operands[0].shape[0]
    r = 512 // shards
    payload = (reps, shards, branch_rows(shards, reps)[0], 256)
    vmem = pl.BlockSpec(memory_space=pltpu.VMEM)
    wide = (length, 512)
    return pl.pallas_call(
        functools.partial(feed_forward, shards, tokens),
        in_specs=[anywhere()] * 4 + [vmem] * 4 + [anywhere()] * 8,
        out_specs=[anywhere()] * 6,
        out_shape=[
            shaped(wide, BF16),
            shaped(wide, F32),
            shaped(wide, BF16),
            shaped(payload, BF16),
            *[shaped((reps // 2, *payload[1:]), BF16)] * 2,
        ],
        scratch_shapes=[
            pltpu.VMEM(wide, BF16),
            pltpu.VMEM(wide, BF16),
            pltpu.VMEM(wide, BF16),
            pltpu.VMEM((2 * shards, r // 2, 512), BF16),
            pltpu.VMEM((4, 512, 512), BF16),
            pltpu.VMEM((2048, 512), BF16),
            pltpu.VMEM((4, length, 512), BF16),
            pltpu.VMEM(wide, BF16),
            pltpu.VMEM(wide, F32),
            pltpu.VMEM(wide, BF16),
            pltpu.VMEM(payload, BF16),
            pltpu.VMEM(payload, BF16),
            pltpu.VMEM(wide, BF16),
            pltpu.VMEM(wide, BF16),
            pltpu.VMEM(wide, F32),
            pltpu.VMEM((512, 512), BF16),
            pltpu.VMEM((4, 512, 512), BF16),
            pltpu.VMEM((2048, 512), BF16),
            pltpu.VMEM((8, 512), F32),
            pltpu.VMEM((4, 8, 512), F32),
            pltpu.SemaphoreType.DMA((10 + 2 * reps,)),
        ],
        compiler_params=pltpu.CompilerParams(vmem_limit_bytes=VMEM_LIMIT),
        cost_estimate=COST,
        name="feed_forward",
    )(*operands)


def call_backward(shards, segments, x, sides, operands, earlier):
    length = x.shape[0]
    chunks = length // BACK
    r = 512 // shards
    back = lambda c: chunks - 1 - c
    wide = pl.BlockSpec((BACK, 512), lambda c, *_: (back(c), 0))
    own = pl.BlockSpec((BACK, QUAD), lambda c, *_: (back(c), 0))
    state = pl.BlockSpec((BACK // SUB, QUAD, QUAD), lambda c, *_: (back(c), 0, 0))
    payload = (2, 2, 2, shards // 2, 2 * r + 16, 128)
    grid_spec = pltpu.PrefetchScalarGridSpec(
        num_scalar_prefetch=1,
        grid=(chunks,),
        in_specs=[
            wide,
            pl.BlockSpec((1, BACK), lambda c, *_: (0, back(c))),
            *([own] * 7 + [state] * 2) * 2,
            wide,
            whole((4, 512, 512)),
            whole((8, 512)),
            wide,
            *[anywhere()] * len(earlier),
        ],
        out_specs=[wide, whole(payload), whole(payload)],
        scratch_shapes=[
            pltpu.VMEM((2, QUAD, QUAD), F32),
            pltpu.VMEM((2, QUAD, QUAD), F32),
            pltpu.VMEM((2, 8, QUAD), F32),
            pltpu.VMEM((512, 8 * QUAD), F32),
            pltpu.VMEM((8, 512), F32),
        ],
    )
    return pl.pallas_call(
        functools.partial(
            ordered, functools.partial(attention_backward, shards), 25, len(earlier)
        ),
        grid_spec=grid_spec,
        out_shape=[shaped((length, 512), F32), shaped(payload, BF16), shaped(payload, BF16)],
        compiler_params=params(),
        cost_estimate=COST,
        name="attention_backward",
    )(segments, x, segments, *sides[0], *sides[1], *operands, *earlier)


def swap(value, axis, bit):
    n = lax.axis_size(axis)
    return lax.ppermute(value, axis, [(i, i ^ bit) for i in range(n)])


def bit_groups(shards):
    bits = shards.bit_length() - 1
    return [(low, min(2, bits - low)) for low in range(1, bits, 2)]


def branch_rows(shards, reps):
    r = 512 // shards
    piece = -(-(9 * r + 16) // (8 * reps)) * 8
    names = [("contract", 4 * r)] + [(b, r) for b in range(4)] + [("output", r), ("vectors", 16)]
    rows, at = [], 0
    for name, height in names + [("none", piece * reps - 9 * r - 16)]:
        done = 0
        while done < height:
            part, offset = divmod(at, piece)
            size = min(height - done, piece - offset)
            rows.append((name, done, part, offset, size))
            done += size
            at += size
    return piece, rows


def add_arrived(shards, *refs):
    source, target = refs[0], refs[-1]
    for half in range(2):
        total = 0.0
        for rep in range(half, source.shape[0], 2):
            for s in range(shards):
                total = total + source[rep, s].astype(F32)
        target[half] = total.astype(BF16)


def call_add_arrived(shards, arrived, *others):
    reps, _, piece, width = arrived.shape
    return pl.pallas_call(
        functools.partial(add_arrived, shards),
        in_specs=[pl.BlockSpec(memory_space=pltpu.VMEM)] + [anywhere()] * len(others),
        out_specs=pl.BlockSpec(memory_space=pltpu.VMEM),
        out_shape=shaped((2, piece, width), BF16),
        compiler_params=pltpu.CompilerParams(vmem_limit_bytes=VMEM_LIMIT),
        cost_estimate=COST,
        name="add_arrived",
    )(arrived, *others)


def zero_of(arrays):
    return sum(array[(0,) * array.ndim] for array in arrays) * jnp.zeros((), BF16)


def after(value, *others):
    return lax.optimization_barrier((value, *others))[0]


def quarters(refs):
    _, core, cross = place()

    def quarter(rows, half, third):
        parts = [ref[rows, :] for ref in refs]
        near = jnp.where(core == half, parts[0], parts[1])
        far = jnp.where(core == half, parts[2], parts[3])
        return jnp.where(cross == third, near, far).astype(F32)

    def both(rows, third):
        return jnp.concatenate([quarter(rows, half, third) for half in range(2)], axis=1)

    return both


def assemble_branch(shards, count_ref, *refs):
    held = refs[-1]
    reps = held.shape[0]
    me = lax.axis_index("rep")
    for a in range(reps):
        held[me ^ a] = refs[a][...]
    contract_ref, expand_ref, output_ref, bias_1_ref, bias_2_ref, gain_ref, shift_ref, loss_ref = (
        refs[reps:-1]
    )
    r = 512 // shards
    _, rows = branch_rows(shards, reps)
    vectors = []
    for name, done, part, offset, size in rows:
        value = jnp.concatenate(
            [held[part, half, offset : offset + size, :] for half in range(2)], axis=1
        ).astype(F32)
        if name == "contract":
            contract_ref[done : done + size, :] = value
        elif name == "output":
            output_ref[done : done + size, :] = value
        elif name == "vectors":
            vectors.append(value[:, :256])
        elif name != "none":
            expand_ref[done : done + size, name * 512 : (name + 1) * 512] = value
    vectors = vectors[0] if len(vectors) == 1 else jnp.concatenate(vectors, axis=0)
    bias_1_ref[...] = vectors[8:9, : 4 * r]
    gain_ref[...] = vectors[0:1, :r]
    shift_ref[...] = vectors[1:2, :r]
    bias_2_ref[...] = vectors[2:3, :r]
    lane = lax.broadcasted_iota(jnp.int32, (1, 128), 1)
    power = jnp.zeros((1, 128), F32)
    for k in range(LOSS_DIGITS):
        power = jnp.where(lane == k, 8.0 ** (k - LOSS_ZERO), power)
    total = jnp.sum(vectors[0:1, 128:256] * power, axis=1, keepdims=True)
    count = 256.0 * count_ref[6:7, 0:1] + count_ref[6:7, 1:2]
    loss_ref[...] = total / (2.0 * count)


def assemble_mixer(shards, *refs):
    both = quarters(refs[:4])
    gain_ref, shift_ref = refs[8:]
    r = 512 // shards
    for m, ref in enumerate(refs[4:8]):
        for quad in range(2):
            at = quad * (2 * r + 16) + (m % 2) * r
            ref[:, quad * 256 : (quad + 1) * 256] = both(slice(at, at + r), m // 2)
    vectors = both(slice(4 * r + 16, 4 * r + 32), 0)
    gain_ref[...] = vectors[0:1, :r]
    shift_ref[...] = vectors[1:2, :r]


def assemble_all(shards, reps, count_ref, *refs):
    parts_q, parts_f, refs = refs[:4], refs[4 : 4 + reps], refs[4 + reps :]
    assemble_mixer(shards, *parts_q, *refs[:6])
    assemble_branch(shards, count_ref, *parts_f, *refs[6:])


def assemble(shards, count, parts_q, parts_f):
    reps = len(parts_f)
    r = 512 // shards
    shapes = [(r, 512)] * 4 + [(1, r)] * 2
    shapes += [(4 * r, 512), (r, 2048), (r, 512), (1, 4 * r), (1, r), (1, r), (1, r), (1, 1)]
    return pl.pallas_call(
        functools.partial(assemble_all, shards, reps),
        in_specs=[pl.BlockSpec(memory_space=pltpu.VMEM)] * (5 + reps),
        out_specs=[pl.BlockSpec(memory_space=pltpu.VMEM)] * len(shapes),
        out_shape=[shaped(shape, F32) for shape in shapes],
        scratch_shapes=[pltpu.VMEM((reps, *parts_f[0].shape), BF16)],
        cost_estimate=COST,
        name="assemble",
    )(count, *parts_q, *parts_f)


def add_low(*parts):
    return sum(part.astype(F32) for part in parts).astype(BF16)


def local(
    inputs,
    segments,
    valid_mask,
    teacher,
    query_weight,
    key_weight,
    value_weight,
    control_weight,
    output_weight,
    gain_first,
    shift_first,
    expand_weight,
    expand_bias,
    contract_weight,
    contract_bias,
    gain_second,
    shift_second,
):
    _, length, width = inputs.shape
    shards, reps = lax.axis_size("shard"), lax.axis_size("rep")
    r = width // shards
    core = lax.axis_index("rep") % 2
    cross = (lax.axis_index("rep") // 2) % 2
    groups = bit_groups(shards)

    matrices = (query_weight, key_weight, value_weight, control_weight, output_weight)
    matrices += (expand_weight, contract_weight)
    biases = (gain_first, shift_first, gain_second, shift_second, contract_bias, expand_bias)
    mixer, branch = call_pack(shards, matrices, biases, valid_mask)

    def along_z(payload):
        held = [payload[None]]
        for low, bits in groups:
            if len(held) > 1:
                held = [jnp.concatenate(held, axis=0)]
            held += [swap(held[0], "shard", a << low) for a in range(1, 1 << bits)]
        return held

    def halves(held):
        if len(held) == 4:
            return jnp.concatenate(held[:2], axis=0), jnp.concatenate(held[2:], axis=0)
        joined = jnp.concatenate(held, axis=0)
        half = joined.shape[0] // 2
        return joined[:half], joined[half:]

    def step_one(first, second):
        return swap(first, "shard", 1), swap(second, "rep", 2)

    def join(first, second, arrived):
        return jnp.concatenate([first, arrived[0]]), jnp.concatenate([second, arrived[1]])

    def step_two(first, second):
        return swap(first, "rep", 2), swap(second, "shard", 1)

    first, second = halves(along_z(mixer))
    held_b = along_z(branch + zero_of([second]))
    first, second = join(first, second, step_one(first, second))
    arrived = step_two(first, second)
    first_b, second_b = halves(held_b)
    pending = step_one(first_b, second_b)
    last = arrived[1] + zero_of(held_b[1:])
    mine_a = (first, arrived[0], second, last)
    theirs_a = tuple(swap(part, "rep", 1) for part in mine_a)

    x = inputs.reshape(length, width)
    forward_0 = call_forward(
        0, shards, segments, x, (*mine_a, *theirs_a), (first_b, second_b)
    )
    weights, vectors, bias, count = forward_0[10:]
    bit = 4
    while bit < reps:
        count = count + swap(count, "rep", bit)
        bit *= 2
    pending = after(pending, forward_0[7])
    first_b, second_b = join(first_b, second_b, pending)
    pending = step_two(first_b, second_b)
    near_b = swap(first_b, "rep", 1), swap(second_b, "rep", 1)
    forward_1 = call_forward(
        1, shards, segments, x, (weights, vectors), (first_b, second_b, *near_b)
    )
    pending = after(pending, forward_1[7])
    mine_b = (first_b, pending[0], second_b, pending[1])
    theirs_b = (near_b[0], swap(pending[0], "rep", 1), near_b[1], swap(pending[1], "rep", 1))
    mixed = (forward_0[7], forward_1[7])

    layer_out, grad_hidden, grad_mix, keep_f, send_low, send_high = call_feed_forward(
        shards,
        reps,
        float(length * shards * reps),
        x,
        *mixed,
        teacher.reshape(length, width),
        valid_mask,
        vectors,
        bias,
        count,
        *mine_b,
        *theirs_b,
    )

    def split(parts):
        return add_low(*(part[0] for part in parts)), add_low(*(part[1] for part in parts))

    def cross_first(parts):
        keep, send = split(parts)
        return keep, swap(send, "rep", 2)

    def row_first(parts):
        keep, send = split(parts)
        return keep, swap(send, "shard", 1)

    def z_stage(parts_list):
        current = parts_list
        for low, bits in reversed(groups):
            span = 1 << (low - 1)
            pieces = [
                jnp.concatenate(
                    [
                        add_low(*(part[a * span : (a + 1) * span] for part in parts))
                        for parts in current
                    ],
                    axis=1,
                )
                for a in range(1 << bits)
            ]
            arrived = [swap(pieces[a], "shard", a << low) for a in range(1, 1 << bits)]
            current = [(pieces[0], *arrived)]
        return current[0]

    def finish(parts):
        total = add_low(*(part[0] for part in parts))
        bit = 4
        while bit < reps:
            total = add_low(total, swap(total, "rep", bit))
            bit *= 2
        return [total] + [swap(total, "rep", a) for a in range(1, 4)]

    late_f = swap(send_low, "rep", 1), swap(send_high, "rep", 1)
    halves_f = keep_f[: reps // 2], keep_f[reps // 2 :]
    summed = jnp.concatenate([add_low(a, b) for a, b in zip(halves_f, late_f)], axis=0)
    every = summed.reshape(reps * shards, *summed.shape[2:])
    arrived_f = lax.all_to_all(every, ("rep", "shard"), 0, 0).reshape(summed.shape)
    sides = [(*saved[:7], *saved[8:10]) for saved in (forward_0, forward_1)]
    grad_inputs, keep_q, send_q = call_backward(
        shards, segments, x, sides, (grad_mix, weights, vectors, grad_hidden), (every,)
    )
    late_q = swap(send_q, "rep", 1)
    parts_0, parts_1 = row_first((keep_q[0], late_q[0])), cross_first((keep_q[1], late_q[1]))
    parts_0, parts_1 = cross_first(parts_0), row_first(parts_1)
    q_pieces = z_stage([parts_0, parts_1])
    total_f = call_add_arrived(shards, arrived_f, q_pieces[0])
    by_offset = {0: total_f}
    bit = 2
    while bit < reps:
        by_offset |= {a | bit: swap(part, "rep", bit) for a, part in list(by_offset.items())}
        bit *= 2
    by_offset |= {a | 1: swap(part, "rep", 1) for a, part in list(by_offset.items())}
    parts_f = [by_offset[a] for a in range(reps)]
    parts_q = finish(q_pieces)
    results = assemble(shards, count, parts_q, parts_f)
    mats, (gain_1, shift_1) = results[:4], results[4:6]
    grad_contract, grad_expand, grad_output, bias_1, bias_2, gain_2, shift_2, loss = results[6:]
    return (
        layer_out.reshape(inputs.shape),
        grad_inputs.reshape(inputs.shape),
        loss.reshape(()),
        *mats,
        grad_output,
        gain_1.reshape(r),
        shift_1.reshape(r),
        grad_expand,
        bias_1.reshape(4 * r),
        grad_contract,
        bias_2.reshape(r),
        gain_2.reshape(r),
        shift_2.reshape(r),
    )


def solution(mesh):
    every = P(("rep", "shard"), None, None)
    every_row = P(("rep", "shard"), None)
    matrix, vector = P("shard", None), P("shard")
    in_specs = (
        every,
        every_row,
        every_row,
        every,
        *[matrix] * 5,
        *[vector] * 2,
        matrix,
        vector,
        matrix,
        *[vector] * 3,
    )
    out_specs = (
        every,
        every,
        P(),
        *[matrix] * 5,
        *[vector] * 2,
        matrix,
        vector,
        matrix,
        *[vector] * 3,
    )
    return jax.shard_map(local, mesh=mesh, in_specs=in_specs, out_specs=out_specs, check_vma=False)
```
